256 devices in a mesh: sec: 2 (over y_lo), gx: 8 (over y_hi, x), gy: 16 (over z, core).
Axes of the slice: x: 4, y: 4 (y_hi: 2, y_lo: 2; y = y_hi * 2 + y_lo), z: 8, core: 2. Of those that a mesh axis runs over, the one named last changes fastest.
Arguments:
- state: float32 [2, 3, 8, 16, 102400], P('sec', None, 'gx', 'gy'), may hold values from -6 to 6
- previous: float32 [2, 3, 8, 16, 102400], P('sec', None, 'gx', 'gy'), may hold values from -6 to 6
- coeff: float32 [2, 2, 8, 16, 102400], P('sec', None, 'gx', 'gy'), may hold values from 0.04 to 0.16
- wet_mask: int32 [8, 16, 102400], P('gx', 'gy'), may hold values 0 or 1
- link_dest: int32 [2, 8, 16, 256, 1], P('sec', 'gx', 'gy'), may hold values from 0 to 127; in each aligned block of 256 rows (0 to 255, 256 to 511, ..., all dimensions but the last counted through in order) at most 4 rows name the same one
- link_rows: int32 [2, 8, 16, 256, 2], P('sec', 'gx', 'gy'), may hold values from 0 to 79, as said below
- link_weight: float32 [2, 8, 16, 256], P('sec', 'gx', 'gy'), may hold values from 0.5 to 2
Outputs:
- final_state: float32 [2, 3, 8, 16, 102400], P('sec', None, 'gx', 'gy')
The draws below stay inside these ranges and needn't reach their ends.
Inputs may be any that keep to these rules, and one draw needn't show every extreme that they name: `link_rows`: in section 0, [..., 0] lies below 8 and [..., 1] below 80; in section 1, [..., 0] lies below 80 and [..., 1] below 8. `link_dest`: among the 256 links of one device at most 4 name the same owner.
All inputs are finite; a program needn't handle non-finite values. No bound on the sum of `wet_mask` on one device may be relied on, other than what follows from the above.
Results may differ from the reference program's by a relative error of at most 0.0001.
Values sent between devices are 32-bit elements; how exact they have to be, the bound alone decides.
A program may use at most 128 MiB of HBM per device.

```python
import math
import jax
import jax.numpy as jnp
import numpy as np
from jax import lax

CX = 8
CY = 128
REFINE = 10
NL = 100
STEPS = 4
CAP = 4
LINKS = 256
NXG = 64
NYG = 2048
N_GX = 8
N_GY = 16


def draw_link_rows(key, part):
    shape = (2, N_GX, N_GY, LINKS)
    first_key, second_key = jax.random.split(key)
    source_bound = jnp.array([CX, REFINE * CX], dtype=jnp.int32)[:, None, None, None]
    landing_bound = jnp.array([REFINE * CX, CX], dtype=jnp.int32)[:, None, None, None]
    source_rows = jax.random.randint(first_key, shape, 0, 1 << 30, dtype=jnp.int32) % source_bound
    landing = jax.random.randint(second_key, shape, 0, 1 << 30, dtype=jnp.int32) % landing_bound
    source_rows = source_rows.at[1, 0, 0, 0].set(REFINE * CX - 1)
    landing = landing.at[0, 0, 0, 0].set(REFINE * CX - 1)
    return jnp.stack([source_rows, landing], axis=-1)


def plant(drawn, rng, smallest, high):
    index_at = [jax.random.randint(jax.random.fold_in(rng, axis), (), 0, length) for axis, length in enumerate(drawn.shape)]
    widest = drawn.shape.index(max(drawn.shape))
    beside = index_at[:widest] + [(index_at[widest] + 1) % drawn.shape[widest]] + index_at[widest + 1:]
    return drawn.at[tuple(index_at)].set(smallest).at[tuple(beside)].set(high)


def block_levels(own_key, shape, shards, smallest, top_value):
    level, own = 1.0, jax.random.fold_in(own_key, 6)
    for dim, blocks in shards:
        steps = jnp.exp(jax.random.uniform(jax.random.fold_in(own, dim), (blocks,), jnp.float32, smallest / len(shards), top_value / len(shards)))
        level = level * jnp.repeat(steps, shape[dim] // blocks).reshape([-1 if axis == dim else 1 for axis in range(len(shape))])
    return level


def deal_out(own_key, own, number, rows, number_of, top, most, lean):
    sequence = jax.random.permutation(own_key, number_of)
    heavy_load, usual = portions_of(number_of, rows * top, most, lean, True), portions_of(number_of, rows * top, most, lean, False)
    places = jnp.arange(number_of)

    def named(lengths, rotation):
        used = int((lengths > 0).sum())
        fixed = max(1, used // 4)
        shifted = fixed + (places - fixed + rotation * (used - fixed)) % max(1, number_of - fixed)
        return jnp.zeros((number_of,), jnp.int32).at[sequence[jnp.where(places < fixed, places, shifted)]].set(jnp.asarray(lengths, jnp.int32))

    lengths = jnp.where(number % 4 == 0, named(heavy_load, number // 4), named(usual, number - number // 4 - 1))
    mixed = jax.random.permutation(jax.random.fold_in(own, 3), number_of)
    giver, taker = mixed[0:number_of // 2 * 2:2], mixed[1:number_of // 2 * 2:2]
    slack = jnp.minimum(lengths[giver] - 1, most - lengths[taker]) // 2
    slack = jnp.where((giver == sequence[0]) | (taker == sequence[0]) | (lengths[taker] == 0), 0, jnp.maximum(slack, 0))
    shifted = jax.random.randint(jax.random.fold_in(own, 4), (number_of // 2,), 0, 1 << 20) % (slack + 1)
    lengths = lengths.at[giver].add(-shifted).at[taker].add(shifted)
    items = jnp.searchsorted(jnp.cumsum(lengths), jnp.arange(rows * top), side="right").astype(jnp.int32)
    listing = items.reshape(top, rows).T
    listing = listing[jax.random.permutation(jax.random.fold_in(own, 1), rows)]
    rotation = jax.random.randint(jax.random.fold_in(own, 2), (rows, 1), 0, top)
    return jnp.take_along_axis(listing, (jnp.arange(top)[None, :] + rotation) % top, axis=1)


def portions_of(number_of, total, limit, skew, full):
    loads = [(1 << 20) // math.isqrt(rank ** skew) + 1 for rank in range(1, number_of + 1)]
    largest = limit if full else min(limit, max(-(-total // number_of), total * loads[0] // sum(loads)))
    least = 1 if total - largest >= number_of - 1 else 0
    holding, rest = [largest] + [least] * (number_of - 1), total - largest - least * (number_of - 1)
    while rest > 0:
        candidates = [i for i in range(1, number_of) if holding[i] < largest] or [i for i in range(1, number_of) if holding[i] < limit]
        mass, budget = sum([loads[i] for i in candidates]), rest
        for i in candidates:
            more = min(limit - holding[i], max(1, budget * loads[i] // mass), rest)
            holding[i] = holding[i] + more
            rest = rest - more
    return np.array(holding)


def centred(own_key, shape, deviation, limit, shards=(), kind=jnp.bfloat16):
    level = block_levels(own_key, shape, shards, -0.22, 0.18) if shards else 1.0
    drawn = jax.random.normal(own_key, shape, jnp.float32) * deviation * level
    return jnp.minimum(jnp.maximum(drawn, -limit), limit).astype(kind)


def setup_inputs(seed: int = 0) -> dict:
    splits = jax.random.split(jax.random.key(seed), 8)
    state = centred(splits[0], (2, 3, N_GX, N_GY, CX * NL * CY), 1.0, 6.0, ((0, 2), (2, 8), (3, 16)), jnp.float32)
    previous = centred(splits[1], (2, 3, N_GX, N_GY, CX * NL * CY), 1.0, 6.0, ((0, 2), (2, 8), (3, 16)), jnp.float32)
    coeff = jnp.clip(0.04 + 0.12 * jax.random.uniform(splits[2], (2, 2, N_GX, N_GY, CX * NL * CY), jnp.float32) ** block_levels(splits[2], (2, 2, N_GX, N_GY, CX * NL * CY), ((0, 2), (2, 8), (3, 16)), -0.2, 0.2), 0.04, 0.16)
    wet_mask = plant((jax.random.randint(splits[3], (N_GX, N_GY, REFINE * CX * REFINE * CY), 0, 4) < 3).astype(jnp.int32), jax.random.fold_in(splits[3], 1), 0, 1)
    link_dest_keys = jax.random.split(jax.random.fold_in(splits[4], 1), 2 * N_GX * N_GY * LINKS // LINKS)
    link_dest_turns = jax.random.permutation(jax.random.fold_in(splits[4], 3), 2 * N_GX * N_GY * LINKS // LINKS)
    link_dest = jax.vmap(lambda own, number: deal_out(jax.random.fold_in(splits[4], 2), own, number, LINKS, N_GX * N_GY, 1, CAP, 2))(link_dest_keys, link_dest_turns).reshape((2, N_GX, N_GY, LINKS, 1))
    link_rows = draw_link_rows(jax.random.fold_in(splits[7], 71), 0)
    link_weight = jnp.clip(jnp.exp(math.log(2.0) - 1.3862944 * jax.random.uniform(splits[6], (2, N_GX, N_GY, LINKS), jnp.float32) ** block_levels(splits[6], (2, N_GX, N_GY, LINKS), ((0, 2), (1, 8), (2, 16)), -0.2, 0.2)), 0.5, 2.0)
    return dict(state=state, previous=previous, coeff=coeff, wet_mask=wet_mask, link_dest=link_dest, link_rows=link_rows, link_weight=link_weight)


def second_along(values, axis_index):
    widths = [(1, 1) if dim_index == axis_index else (0, 0) for dim_index in range(values.ndim)]
    padded = jnp.pad(values, widths)
    extent = values.shape[axis_index]
    forward_part = lax.slice_in_dim(padded, 2, extent + 2, axis=axis_index)
    backward_part = lax.slice_in_dim(padded, 0, extent, axis=axis_index)
    return forward_part - 2.0 * values + backward_part


def difference_along(values, axis_index):
    widths = [(1, 1) if dim_index == axis_index else (0, 0) for dim_index in range(values.ndim)]
    padded = jnp.pad(values, widths)
    extent = values.shape[axis_index]
    forward_part = lax.slice_in_dim(padded, 2, extent + 2, axis=axis_index)
    backward_part = lax.slice_in_dim(padded, 0, extent, axis=axis_index)
    return forward_part - backward_part


def to_elastic(blocks, count):
    return blocks.reshape(count, N_GX, N_GY, CX, NL, CY).transpose(0, 1, 3, 4, 2, 5).reshape(count, NXG, NL, NYG)


def from_elastic(field, count):
    return field.reshape(count, N_GX, CX, NL, N_GY, CY).transpose(0, 1, 4, 2, 3, 5).reshape(count, N_GX, N_GY, CX * NL * CY)


def to_sheet(blocks, count):
    return blocks.reshape(count, N_GX, N_GY, REFINE * CX, REFINE * CY).transpose(0, 1, 3, 2, 4).reshape(count, NXG * REFINE, NYG * REFINE)


def from_sheet(sheet, count):
    return sheet.reshape(count, N_GX, REFINE * CX, N_GY, REFINE * CY).transpose(0, 1, 3, 2, 4).reshape(count, N_GX, N_GY, CX * NL * CY)


def couple(elastic_field, sheet, link_dest, link_rows, link_weight):
    fine_rows = REFINE * CX
    uplift = elastic_field[2, :, 0, :].reshape(N_GX, CX, N_GY, CY).transpose(0, 2, 1, 3)
    surface = sheet[0].reshape(N_GX, fine_rows, N_GY, REFINE * CY).transpose(0, 2, 1, 3)
    from_elastic_tiles = jnp.take_along_axis(uplift, link_rows[0, :, :, :, 0:1], axis=2) * link_weight[0][..., None]
    picked = jnp.take_along_axis(surface, link_rows[1, :, :, :, 0:1], axis=2)
    averaged = jnp.sum(picked.reshape(N_GX, N_GY, LINKS, CY, REFINE), axis=-1) / REFINE
    from_shallow_tiles = averaged * link_weight[1][..., None]
    target_shallow = (link_dest[0, :, :, :, 0] * fine_rows + link_rows[0, :, :, :, 1]).reshape(-1)
    target_elastic = (link_dest[1, :, :, :, 0] * CX + link_rows[1, :, :, :, 1]).reshape(-1)
    into_shallow = jnp.zeros((N_GX * N_GY * fine_rows, CY), jnp.float32).at[target_shallow].add(from_elastic_tiles.reshape(-1, CY))
    into_elastic = jnp.zeros((N_GX * N_GY * CX, CY), jnp.float32).at[target_elastic].add(from_shallow_tiles.reshape(-1, CY))
    into_shallow = into_shallow.reshape(N_GX, N_GY, fine_rows, CY).transpose(0, 2, 1, 3).reshape(NXG * REFINE, NYG)
    into_shallow = jnp.repeat(into_shallow, REFINE, axis=1)
    into_elastic = into_elastic.reshape(N_GX, N_GY, CX, CY).transpose(0, 2, 1, 3).reshape(NXG, NYG)
    return into_elastic, into_shallow


def elastic_step(current_field, previous_field, shear_modulus, lame_first, surface_force):
    own_axis = (0, 2, 1)
    stiffness = lame_first + 2.0 * shear_modulus
    updated_list = []
    for component in range(3):
        displaced = current_field[component]
        factors = [stiffness if own_axis[component] == axis_index else shear_modulus for axis_index in range(3)]
        acceleration = factors[0] * second_along(displaced, 0) + factors[1] * second_along(displaced, 1) + factors[2] * second_along(displaced, 2)
        updated = 2.0 * displaced - previous_field[component] + acceleration
        if component == 2:
            updated = updated.at[:, 0, :].add(surface_force)
        updated_list.append(updated)
    return jnp.stack(updated_list)


def shallow_step(current_sheet, previous_sheet, wave_factor, area_factor, wetness, source):
    flux_first = wetness * (previous_sheet[1] - wave_factor * difference_along(current_sheet[0], 0))
    flux_second = wetness * (previous_sheet[2] - wave_factor * difference_along(current_sheet[0], 1))
    divergence = difference_along(current_sheet[1], 0) + difference_along(current_sheet[2], 1)
    height = wetness * (previous_sheet[0] - area_factor * divergence + source)
    return jnp.stack([height, flux_first, flux_second])


def reference(state, previous, coeff, wet_mask, link_dest, link_rows, link_weight):
    elastic_now = to_elastic(state[0], 3)
    elastic_before = to_elastic(previous[0], 3)
    sheet_now = to_sheet(state[1], 3)
    sheet_before = to_sheet(previous[1], 3)
    moduli = to_elastic(coeff[0], 2)
    factors = to_sheet(coeff[1], 2)
    wetness = to_sheet(wet_mask[None], 1)[0].astype(jnp.float32)
    for step_index in range(STEPS):
        into_elastic, into_shallow = couple(elastic_now, sheet_now, link_dest, link_rows, link_weight)
        elastic_new = elastic_step(elastic_now, elastic_before, moduli[0], moduli[1], into_elastic)
        sheet_new = shallow_step(sheet_now, sheet_before, factors[0], factors[1], wetness, into_shallow)
        elastic_before, elastic_now = elastic_now, elastic_new
        sheet_before, sheet_now = sheet_now, sheet_new
    return jnp.stack([from_elastic(elastic_now, 3), from_sheet(sheet_now, 3)])
```

```python
import jax
import jax.numpy as jnp
from jax import lax
from jax.experimental import pallas as pl
from jax.experimental.pallas import tpu as pltpu
from jax.sharding import PartitionSpec as P

CX = 8
CY = 128
REFINE = 10
NL = 100
STEPS = 4
CAP = 4

ROWS = CX * NL
BASE = 104
PAD_ROWS = BASE + ROWS + NL + 8
CHUNK = 40


def from_partner(value, axis, stride):
    return lax.ppermute(value, axis, [(i, i ^ 1 << stride) for i in range(lax.axis_size(axis))])


def shift_pairs(axis):
    count = lax.axis_size(axis)
    forward = [(i, i + 1) for i in range(count - 1)]
    backward = [(target, source) for source, target in forward]
    return forward, backward


def exchange_halos(current):
    forward_x, backward_x = shift_pairs("gx")
    forward_y, backward_y = shift_pairs("gy")
    low_x = lax.ppermute(current[:, ROWS - NL :], "gx", forward_x)
    high_x = lax.ppermute(current[:, :NL], "gx", backward_x)
    low_y = lax.ppermute(current[:, :, CY - 1 :], "gy", forward_y)
    high_y = lax.ppermute(current[:, :, :1], "gy", backward_y)
    return low_x, high_x, low_y, high_y


def fill_scratch(scratch, cur_ref, low_ref, high_ref, fields):
    for f in range(fields):
        scratch[f, pl.ds(BASE - NL, NL), :] = low_ref[f]
        scratch[f, pl.ds(BASE, ROWS), :] = cur_ref[f]
        scratch[f, pl.ds(BASE + ROWS, NL), :] = high_ref[f]


def lane_index(rows):
    return lax.broadcasted_iota(jnp.int32, (rows, CY), 1)


def row_mask(r0, rows, period, phase):
    local = lax.broadcasted_iota(jnp.int32, (rows, CY), 0)
    mask = jnp.zeros((rows, CY), jnp.bool_)
    for r in range(rows):
        if (r0 + r) % period == phase:
            mask = mask | (local == r)
    return mask


def elastic_kernel(cur_ref, prev_ref, coef_ref, low_ref, high_ref, left_ref, right_ref, force_ref, out_ref, scratch):
    fill_scratch(scratch, cur_ref, low_ref, high_ref, 3)
    lanes = lane_index(CHUNK)
    first_lane = lanes == 0
    last_lane = lanes == CY - 1
    own_axis = (0, 2, 1)
    for r0 in range(0, ROWS, CHUNK):
        top_layer = row_mask(r0, CHUNK, NL, 0)
        bottom_layer = row_mask(r0, CHUNK, NL, NL - 1)
        shear = coef_ref[0, pl.ds(r0, CHUNK), :]
        lame = coef_ref[1, pl.ds(r0, CHUNK), :]
        stiffness = lame + 2.0 * shear
        for c in range(3):
            at = BASE + r0
            v = scratch[c, pl.ds(at, CHUNK), :]
            along_first = scratch[c, pl.ds(at + NL, CHUNK), :] - 2.0 * v + scratch[c, pl.ds(at - NL, CHUNK), :]
            deeper = jnp.where(bottom_layer, 0.0, scratch[c, pl.ds(at + 1, CHUNK), :])
            shallower = jnp.where(top_layer, 0.0, scratch[c, pl.ds(at - 1, CHUNK), :])
            along_depth = deeper - 2.0 * v + shallower
            after = jnp.where(last_lane, right_ref[c, pl.ds(r0, CHUNK), :], pltpu.roll(v, CY - 1, 1))
            before = jnp.where(first_lane, left_ref[c, pl.ds(r0, CHUNK), :], pltpu.roll(v, 1, 1))
            along_second = after - 2.0 * v + before
            factors = [stiffness if own_axis[c] == axis_index else shear for axis_index in range(3)]
            acceleration = factors[0] * along_first + factors[1] * along_depth + factors[2] * along_second
            out_ref[c, pl.ds(r0, CHUNK), :] = 2.0 * v - prev_ref[c, pl.ds(r0, CHUNK), :] + acceleration
    for x in range(CX):
        out_ref[2, pl.ds(x * NL, 1), :] = out_ref[2, pl.ds(x * NL, 1), :] + force_ref[pl.ds(x, 1), :]


def shallow_kernel(cur_ref, prev_ref, coef_ref, wet_ref, low_ref, high_ref, left_ref, right_ref, source_ref, out_ref, scratch):
    fill_scratch(scratch, cur_ref, low_ref, high_ref, 3)
    lanes = lane_index(CHUNK)
    first_lane = lanes == 0
    last_lane = lanes == CY - 1
    first_block = row_mask(0, CHUNK, REFINE, 0)
    last_block = row_mask(0, CHUNK, REFINE, REFINE - 1)
    for r0 in range(0, ROWS, CHUNK):
        at = BASE + r0

        def rows_diff(f):
            return scratch[f, pl.ds(at + REFINE, CHUNK), :] - scratch[f, pl.ds(at - REFINE, CHUNK), :]

        def columns_diff(f):
            v = scratch[f, pl.ds(at, CHUNK), :]
            wrap_after = jnp.where(last_block, right_ref[f, pl.ds(r0, CHUNK), :],
                                   pltpu.roll(scratch[f, pl.ds(at + 1, CHUNK), :], CY - 1, 1))
            wrap_before = jnp.where(first_block, left_ref[f, pl.ds(r0, CHUNK), :],
                                    pltpu.roll(scratch[f, pl.ds(at - 1, CHUNK), :], 1, 1))
            after = jnp.where(last_lane, wrap_after, pltpu.roll(v, CY - 1, 1))
            before = jnp.where(first_lane, wrap_before, pltpu.roll(v, 1, 1))
            return after - before

        wave = coef_ref[0, pl.ds(r0, CHUNK), :]
        area = coef_ref[1, pl.ds(r0, CHUNK), :]
        wet = wet_ref[pl.ds(r0, CHUNK), :].astype(jnp.float32)
        eta_r = rows_diff(0)
        eta_c = columns_diff(0)
        out_ref[1, pl.ds(r0, CHUNK), :] = wet * (prev_ref[1, pl.ds(r0, CHUNK), :] - wave * eta_r)
        out_ref[2, pl.ds(r0, CHUNK), :] = wet * (prev_ref[2, pl.ds(r0, CHUNK), :] - wave * eta_c)
        divergence = rows_diff(1) + columns_diff(2)
        out_ref[0, pl.ds(r0, CHUNK), :] = wet * (
            prev_ref[0, pl.ds(r0, CHUNK), :] - area * divergence + source_ref[pl.ds(r0, CHUNK), :]
        )


def vmem_specs(count):
    return [pl.BlockSpec(memory_space=pltpu.VMEM)] * count


def run_elastic(*operands):
    return pl.pallas_call(
        elastic_kernel,
        out_shape=jax.ShapeDtypeStruct((3, ROWS, CY), jnp.float32),
        in_specs=vmem_specs(len(operands)),
        out_specs=pl.BlockSpec(memory_space=pltpu.VMEM),
        scratch_shapes=[pltpu.VMEM((3, PAD_ROWS, CY), jnp.float32)],
    )(*operands)


def run_shallow(*operands):
    return pl.pallas_call(
        shallow_kernel,
        out_shape=jax.ShapeDtypeStruct((3, ROWS, CY), jnp.float32),
        in_specs=vmem_specs(len(operands)),
        out_specs=pl.BlockSpec(memory_space=pltpu.VMEM),
        scratch_shapes=[pltpu.VMEM((3, PAD_ROWS, CY), jnp.float32)],
    )(*operands)


def route(payload):
    tile_data, tile_rows = payload
    width = tile_data.shape[-1]
    received_data, received_rows = (
        lax.all_to_all(tile_data, ("gx", "gy"), split_axis=0, concat_axis=0, tiled=True),
        lax.all_to_all(tile_rows, ("gx", "gy"), split_axis=0, concat_axis=0, tiled=True),
    )
    return (received_data.reshape(-1, width), received_rows.reshape(-1))


def deliver(outgoing, send_rows):
    routed = route((outgoing, send_rows))
    return from_partner((routed[0], routed[1]), "sec", 0)


def on_device(state, previous, coeff, wet_mask, link_dest, link_rows, link_weight):
    section = lax.axis_index("sec")
    owners = lax.axis_size("gx") * lax.axis_size("gy")
    fine_rows = REFINE * CX
    fine_cols = REFINE * CY
    current = state[0, :, 0, 0].reshape(3, ROWS, CY)
    earlier = previous[0, :, 0, 0].reshape(3, ROWS, CY)
    factors = coeff[0, :, 0, 0].reshape(2, ROWS, CY)
    wet = wet_mask[0, 0].reshape(ROWS, CY)
    targets = link_dest.reshape(-1)
    pairs = link_rows.reshape(-1, 2)
    source_rows = pairs[:, 0]
    landing = pairs[:, 1]
    weights = link_weight.reshape(-1)
    one_hot = (targets[:, None] == jnp.arange(owners, dtype=jnp.int32)[None, :]).astype(jnp.int32)
    before = jnp.cumsum(one_hot, axis=0) - one_hot
    slot_index = jnp.sum(before * one_hot, axis=1)
    position = targets * CAP + slot_index
    send_rows = jnp.zeros((owners * CAP,), jnp.int32).at[position].set(landing).reshape(owners, CAP)
    for step_index in range(STEPS):
        low_x, high_x, low_y, high_y = exchange_halos(current)

        def elastic_rows():
            return current[2].reshape(CX, NL, CY)[:, 0, :][source_rows]

        def shallow_rows():
            picked_fine = current[0].reshape(fine_rows, fine_cols)[source_rows]
            return jnp.sum(picked_fine.reshape(-1, CY, REFINE), axis=-1) / REFINE

        picked = lax.cond(section == 0, elastic_rows, shallow_rows)
        outgoing = (
            jnp.zeros((owners * CAP, CY), jnp.float32).at[position].set(picked * weights[:, None])
        )
        outgoing = outgoing.reshape(owners, CAP, CY)
        arrived, arrived_rows = deliver(outgoing, send_rows)

        def elastic_branch():
            surface_force = jnp.zeros((CX, CY), jnp.float32).at[arrived_rows].add(arrived)
            return run_elastic(current, earlier, factors, low_x, high_x, low_y, high_y, surface_force)

        def shallow_branch():
            coarse_source = jnp.zeros((fine_rows, CY), jnp.float32).at[arrived_rows].add(arrived)
            source = jnp.repeat(coarse_source, REFINE, axis=1).reshape(ROWS, CY)
            blocks = (3, fine_rows, REFINE, 1)
            left = jnp.broadcast_to(low_y.reshape(blocks)[:, :, REFINE - 1 :], blocks).reshape(3, ROWS, 1)
            right = jnp.broadcast_to(high_y.reshape(blocks)[:, :, :1], blocks).reshape(3, ROWS, 1)
            return run_shallow(current, earlier, factors, wet, low_x, high_x, left, right, source)

        updated = lax.cond(section == 0, elastic_branch, shallow_branch)
        earlier, current = (current, updated)
    return current.reshape(1, 3, 1, 1, -1)


def solution(mesh):
    placed = (
        P("sec", None, "gx", "gy", None),
        P("sec", None, "gx", "gy", None),
        P("sec", None, "gx", "gy", None),
        P("gx", "gy", None),
        P("sec", "gx", "gy", None, None),
        P("sec", "gx", "gy", None, None),
        P("sec", "gx", "gy", None),
    )
    return jax.shard_map(
        on_device,
        mesh=mesh,
        in_specs=placed,
        out_specs=P("sec", None, "gx", "gy", None),
        check_vma=False,
    )
```

```python
import jax
import jax.numpy as jnp
from jax import lax
from jax.experimental import pallas as pl
from jax.experimental.pallas import tpu as pltpu
from jax.sharding import PartitionSpec as P

CX = 8
CY = 128
REFINE = 10
NL = 100
STEPS = 4
CAP = 4

ROWS = CX * NL
BASE = 104
PAD_ROWS = BASE + ROWS + NL + 8
CHUNK = 40


def from_partner(value, axis, stride):
    return lax.ppermute(value, axis, [(i, i ^ 1 << stride) for i in range(lax.axis_size(axis))])


def shift_pairs(axis):
    count = lax.axis_size(axis)
    forward = [(i, i + 1) for i in range(count - 1)]
    backward = [(target, source) for source, target in forward]
    return forward, backward


def exchange_halos(current):
    forward_x, backward_x = shift_pairs("gx")
    forward_y, backward_y = shift_pairs("gy")
    low_x = lax.ppermute(current[:, ROWS - NL :], "gx", forward_x)
    high_x = lax.ppermute(current[:, :NL], "gx", backward_x)
    low_y = lax.ppermute(current[:, :, CY - 1 :], "gy", forward_y)
    high_y = lax.ppermute(current[:, :, :1], "gy", backward_y)
    return low_x, high_x, low_y, high_y


def fill_scratch(scratch, cur_ref, low_ref, high_ref, fields):
    for f in range(fields):
        scratch[f, pl.ds(BASE - NL, NL), :] = low_ref[f]
        scratch[f, pl.ds(BASE, ROWS), :] = cur_ref[f]
        scratch[f, pl.ds(BASE + ROWS, NL), :] = high_ref[f]


def lane_index(rows):
    return lax.broadcasted_iota(jnp.int32, (rows, CY), 1)


def row_mask(r0, rows, period, phase):
    local = lax.broadcasted_iota(jnp.int32, (rows, CY), 0)
    mask = jnp.zeros((rows, CY), jnp.bool_)
    for r in range(rows):
        if (r0 + r) % period == phase:
            mask = mask | (local == r)
    return mask


def exact_dot(a, b):
    return jnp.dot(a, b, precision=lax.Precision.HIGHEST, preferred_element_type=jnp.float32)


def landing_sum(rows_ref, arrived_ref, count):
    slots = rows_ref.shape[1]
    one_hot = (lax.broadcasted_iota(jnp.int32, (count, slots), 0) == rows_ref[...]).astype(jnp.float32)
    return exact_dot(one_hot, arrived_ref[...])


def spread(cb):
    coarse = lax.broadcasted_iota(jnp.int32, (CY, CY), 0)
    fine = lax.broadcasted_iota(jnp.int32, (CY, CY), 1) + cb * CY
    return ((fine >= coarse * REFINE) & (fine < coarse * REFINE + REFINE)).astype(jnp.float32)


def elastic_kernel(cur_ref, prev_ref, coef_ref, low_ref, high_ref, left_ref, right_ref, rows_ref, arrived_ref,
                   pick_ref, out_ref, tiles_ref, scratch):
    fill_scratch(scratch, cur_ref, low_ref, high_ref, 3)
    force = landing_sum(rows_ref, arrived_ref, CX)
    lanes = lane_index(CHUNK)
    first_lane = lanes == 0
    last_lane = lanes == CY - 1
    own_axis = (0, 2, 1)
    for r0 in range(0, ROWS, CHUNK):
        top_layer = row_mask(r0, CHUNK, NL, 0)
        bottom_layer = row_mask(r0, CHUNK, NL, NL - 1)
        shear = coef_ref[0, pl.ds(r0, CHUNK), :]
        lame = coef_ref[1, pl.ds(r0, CHUNK), :]
        stiffness = lame + 2.0 * shear
        for c in range(3):
            at = BASE + r0
            v = scratch[c, pl.ds(at, CHUNK), :]
            along_first = scratch[c, pl.ds(at + NL, CHUNK), :] - 2.0 * v + scratch[c, pl.ds(at - NL, CHUNK), :]
            deeper = jnp.where(bottom_layer, 0.0, scratch[c, pl.ds(at + 1, CHUNK), :])
            shallower = jnp.where(top_layer, 0.0, scratch[c, pl.ds(at - 1, CHUNK), :])
            along_depth = deeper - 2.0 * v + shallower
            after = jnp.where(last_lane, right_ref[c, pl.ds(r0, CHUNK), :], pltpu.roll(v, CY - 1, 1))
            before = jnp.where(first_lane, left_ref[c, pl.ds(r0, CHUNK), :], pltpu.roll(v, 1, 1))
            along_second = after - 2.0 * v + before
            factors = [stiffness if own_axis[c] == axis_index else shear for axis_index in range(3)]
            acceleration = factors[0] * along_first + factors[1] * along_depth + factors[2] * along_second
            out_ref[c, pl.ds(r0, CHUNK), :] = 2.0 * v - prev_ref[c, pl.ds(r0, CHUNK), :] + acceleration
    for x in range(CX):
        out_ref[2, pl.ds(x * NL, 1), :] = out_ref[2, pl.ds(x * NL, 1), :] + force[x : x + 1]
    uplift = out_ref[2, pl.ds(0, CX, stride=NL), :]
    tiles_ref[...] = exact_dot(pick_ref[:, :CX], uplift)


def shallow_kernel(cur_ref, prev_ref, coef_ref, wet_ref, low_ref, high_ref, left_ref, right_ref, rows_ref, arrived_ref,
                   pick_ref, out_ref, tiles_ref, scratch, source_ref):
    fill_scratch(scratch, cur_ref, low_ref, high_ref, 3)
    coarse_source = landing_sum(rows_ref, arrived_ref, REFINE * CX)
    for cb in range(REFINE):
        source_ref[pl.ds(cb, REFINE * CX, stride=REFINE), :] = exact_dot(coarse_source, spread(cb))
    lanes = lane_index(CHUNK)
    first_lane = lanes == 0
    last_lane = lanes == CY - 1
    first_block = row_mask(0, CHUNK, REFINE, 0)
    last_block = row_mask(0, CHUNK, REFINE, REFINE - 1)
    for r0 in range(0, ROWS, CHUNK):
        at = BASE + r0

        def rows_diff(f):
            return scratch[f, pl.ds(at + REFINE, CHUNK), :] - scratch[f, pl.ds(at - REFINE, CHUNK), :]

        def columns_diff(f):
            v = scratch[f, pl.ds(at, CHUNK), :]
            wrap_after = jnp.where(last_block, right_ref[f, pl.ds(r0, CHUNK), :],
                                   pltpu.roll(scratch[f, pl.ds(at + 1, CHUNK), :], CY - 1, 1))
            wrap_before = jnp.where(first_block, left_ref[f, pl.ds(r0, CHUNK), :],
                                    pltpu.roll(scratch[f, pl.ds(at - 1, CHUNK), :], 1, 1))
            after = jnp.where(last_lane, wrap_after, pltpu.roll(v, CY - 1, 1))
            before = jnp.where(first_lane, wrap_before, pltpu.roll(v, 1, 1))
            return after - before

        wave = coef_ref[0, pl.ds(r0, CHUNK), :]
        area = coef_ref[1, pl.ds(r0, CHUNK), :]
        wet = wet_ref[pl.ds(r0, CHUNK), :].astype(jnp.float32)
        eta_r = rows_diff(0)
        eta_c = columns_diff(0)
        out_ref[1, pl.ds(r0, CHUNK), :] = wet * (prev_ref[1, pl.ds(r0, CHUNK), :] - wave * eta_r)
        out_ref[2, pl.ds(r0, CHUNK), :] = wet * (prev_ref[2, pl.ds(r0, CHUNK), :] - wave * eta_c)
        divergence = rows_diff(1) + columns_diff(2)
        out_ref[0, pl.ds(r0, CHUNK), :] = wet * (
            prev_ref[0, pl.ds(r0, CHUNK), :] - area * divergence + source_ref[pl.ds(r0, CHUNK), :]
        )
    total = jnp.zeros((REFINE * CX, CY), jnp.float32)
    for cb in range(REFINE):
        total = total + exact_dot(out_ref[0, pl.ds(cb, REFINE * CX, stride=REFINE), :], spread(cb).T)
    tiles_ref[...] = exact_dot(pick_ref[...], total / REFINE)


def vmem_specs(count):
    return [pl.BlockSpec(memory_space=pltpu.VMEM)] * count


def run_step(kernel, scratch_shapes, *operands):
    slots = operands[-1].shape[0]
    return pl.pallas_call(
        kernel,
        out_shape=(
            jax.ShapeDtypeStruct((3, ROWS, CY), jnp.float32),
            jax.ShapeDtypeStruct((slots, CY), jnp.float32),
        ),
        in_specs=vmem_specs(len(operands)),
        out_specs=tuple(vmem_specs(2)),
        scratch_shapes=scratch_shapes,
    )(*operands)


def route(payload):
    tile_data, tile_rows = payload
    width = tile_data.shape[-1]
    received_data, received_rows = (
        lax.all_to_all(tile_data, ("gx", "gy"), split_axis=0, concat_axis=0, tiled=True),
        lax.all_to_all(tile_rows, ("gx", "gy"), split_axis=0, concat_axis=0, tiled=True),
    )
    return (received_data.reshape(-1, width), received_rows.reshape(-1))


def deliver(outgoing, send_rows):
    routed = route((outgoing, send_rows))
    return from_partner((routed[0], routed[1]), "sec", 0)


def on_device(state, previous, coeff, wet_mask, link_dest, link_rows, link_weight):
    section = lax.axis_index("sec")
    owners = lax.axis_size("gx") * lax.axis_size("gy")
    fine_rows = REFINE * CX
    fine_cols = REFINE * CY
    current = state[0, :, 0, 0].reshape(3, ROWS, CY)
    earlier = previous[0, :, 0, 0].reshape(3, ROWS, CY)
    factors = coeff[0, :, 0, 0].reshape(2, ROWS, CY)
    wet = wet_mask[0, 0].reshape(ROWS, CY)
    targets = link_dest.reshape(-1)
    pairs = link_rows.reshape(-1, 2)
    source_rows = pairs[:, 0]
    landing = pairs[:, 1]
    weights = link_weight.reshape(-1)
    one_hot = (targets[:, None] == jnp.arange(owners, dtype=jnp.int32)[None, :]).astype(jnp.int32)
    before = jnp.cumsum(one_hot, axis=0) - one_hot
    slot_index = jnp.sum(before * one_hot, axis=1)
    position = targets * CAP + slot_index
    send_rows = jnp.zeros((owners * CAP,), jnp.int32).at[position].set(landing).reshape(owners, CAP)
    pick = jnp.zeros((owners * CAP, fine_rows), jnp.float32).at[position, source_rows].add(weights)

    def elastic_rows():
        return current[2].reshape(CX, NL, CY)[:, 0, :][source_rows]

    def shallow_rows():
        picked_fine = current[0].reshape(fine_rows, fine_cols)[source_rows]
        return jnp.sum(picked_fine.reshape(-1, CY, REFINE), axis=-1) / REFINE

    picked = lax.cond(section == 0, elastic_rows, shallow_rows)
    outgoing = jnp.zeros((owners * CAP, CY), jnp.float32).at[position].set(picked * weights[:, None])
    for step_index in range(STEPS):
        low_x, high_x, low_y, high_y = exchange_halos(current)
        arrived, arrived_rows = deliver(outgoing.reshape(owners, CAP, CY), send_rows)
        arrived_rows = arrived_rows.reshape(1, -1)

        def elastic_branch():
            scratch = [pltpu.VMEM((3, PAD_ROWS, CY), jnp.float32)]
            return run_step(elastic_kernel, scratch, current, earlier, factors, low_x, high_x, low_y, high_y,
                            arrived_rows, arrived, pick)

        def shallow_branch():
            blocks = (3, fine_rows, REFINE, 1)
            left = jnp.broadcast_to(low_y.reshape(blocks)[:, :, REFINE - 1 :], blocks).reshape(3, ROWS, 1)
            right = jnp.broadcast_to(high_y.reshape(blocks)[:, :, :1], blocks).reshape(3, ROWS, 1)
            scratch = [pltpu.VMEM((3, PAD_ROWS, CY), jnp.float32), pltpu.VMEM((ROWS, CY), jnp.float32)]
            return run_step(shallow_kernel, scratch, current, earlier, factors, wet, low_x, high_x, left, right,
                            arrived_rows, arrived, pick)

        updated, outgoing = lax.cond(section == 0, elastic_branch, shallow_branch)
        earlier, current = (current, updated)
    return current.reshape(1, 3, 1, 1, -1)


def solution(mesh):
    placed = (
        P("sec", None, "gx", "gy", None),
        P("sec", None, "gx", "gy", None),
        P("sec", None, "gx", "gy", None),
        P("gx", "gy", None),
        P("sec", "gx", "gy", None, None),
        P("sec", "gx", "gy", None, None),
        P("sec", "gx", "gy", None),
    )
    return jax.shard_map(
        on_device,
        mesh=mesh,
        in_specs=placed,
        out_specs=P("sec", None, "gx", "gy", None),
        check_vma=False,
    )
```

```python
import jax
import jax.numpy as jnp
from jax import lax
from jax.experimental import pallas as pl
from jax.experimental.pallas import tpu as pltpu
from jax.sharding import PartitionSpec as P

CX = 8
CY = 128
REFINE = 10
NL = 100
STEPS = 4
CAP = 4

ROWS = CX * NL
BASE = 104
PAD_ROWS = BASE + ROWS + NL + 8
CHUNK = 40
EDGE = 16


def from_partner(value, axis, stride):
    return lax.ppermute(value, axis, [(i, i ^ 1 << stride) for i in range(lax.axis_size(axis))])


def shift_pairs(axis):
    count = lax.axis_size(axis)
    forward = [(i, i + 1) for i in range(count - 1)]
    backward = [(target, source) for source, target in forward]
    return forward, backward


def exchange_halos(current):
    forward_x, backward_x = shift_pairs("gx")
    forward_y, backward_y = shift_pairs("gy")
    low_x = lax.ppermute(current[:, ROWS - NL :], "gx", forward_x)
    high_x = lax.ppermute(current[:, :NL], "gx", backward_x)
    low_y = lax.ppermute(current[:, :, CY - 1 :], "gy", forward_y)
    high_y = lax.ppermute(current[:, :, :1], "gy", backward_y)
    return low_x, high_x, low_y, high_y


def fill_scratch(scratch, cur_ref, low_ref, high_ref, fields):
    for f in range(fields):
        scratch[f, pl.ds(BASE - NL, NL), :] = low_ref[f]
        scratch[f, pl.ds(BASE, ROWS), :] = cur_ref[f]
        scratch[f, pl.ds(BASE + ROWS, NL), :] = high_ref[f]


def lane_index(rows):
    return lax.broadcasted_iota(jnp.int32, (rows, CY), 1)


def row_mask(r0, rows, period, phase):
    local = lax.broadcasted_iota(jnp.int32, (rows, CY), 0)
    mask = jnp.zeros((rows, CY), jnp.bool_)
    for r in range(rows):
        if (r0 + r) % period == phase:
            mask = mask | (local == r)
    return mask


def exact_dot(a, b):
    return jnp.dot(a, b, precision=lax.Precision.HIGHEST, preferred_element_type=jnp.float32)


def landing_sum(rows_ref, arrived_ref, count):
    slots = rows_ref.shape[1]
    one_hot = (lax.broadcasted_iota(jnp.int32, (count, slots), 0) == rows_ref[...]).astype(jnp.float32)
    return exact_dot(one_hot, arrived_ref[...])


def spread(cb):
    coarse = lax.broadcasted_iota(jnp.int32, (CY, CY), 0)
    fine = lax.broadcasted_iota(jnp.int32, (CY, CY), 1) + cb * CY
    return ((fine >= coarse * REFINE) & (fine < coarse * REFINE + REFINE)).astype(jnp.float32)


def elastic_kernel(cur_ref, prev_ref, coef_ref, low_ref, high_ref, left_ref, right_ref, rows_ref, arrived_ref,
                   pick_ref, out_ref, tiles_ref, scratch):
    fill_scratch(scratch, cur_ref, low_ref, high_ref, 3)
    force = landing_sum(rows_ref, arrived_ref, CX)
    lanes = lane_index(CHUNK)
    first_lane = lanes == 0
    last_lane = lanes == CY - 1
    own_axis = (0, 2, 1)
    for r0 in range(0, ROWS, CHUNK):
        top_layer = row_mask(r0, CHUNK, NL, 0)
        bottom_layer = row_mask(r0, CHUNK, NL, NL - 1)
        shear = coef_ref[0, pl.ds(r0, CHUNK), :]
        lame = coef_ref[1, pl.ds(r0, CHUNK), :]
        stiffness = lame + 2.0 * shear
        for c in range(3):
            at = BASE + r0
            v = scratch[c, pl.ds(at, CHUNK), :]
            along_first = scratch[c, pl.ds(at + NL, CHUNK), :] - 2.0 * v + scratch[c, pl.ds(at - NL, CHUNK), :]
            deeper = jnp.where(bottom_layer, 0.0, scratch[c, pl.ds(at + 1, CHUNK), :])
            shallower = jnp.where(top_layer, 0.0, scratch[c, pl.ds(at - 1, CHUNK), :])
            along_depth = deeper - 2.0 * v + shallower
            after = jnp.where(last_lane, right_ref[c, pl.ds(r0, CHUNK), :], pltpu.roll(v, CY - 1, 1))
            before = jnp.where(first_lane, left_ref[c, pl.ds(r0, CHUNK), :], pltpu.roll(v, 1, 1))
            along_second = after - 2.0 * v + before
            factors = [stiffness if own_axis[c] == axis_index else shear for axis_index in range(3)]
            acceleration = factors[0] * along_first + factors[1] * along_depth + factors[2] * along_second
            out_ref[c, pl.ds(r0, CHUNK), :] = 2.0 * v - prev_ref[c, pl.ds(r0, CHUNK), :] + acceleration
    for x in range(CX):
        out_ref[2, pl.ds(x * NL, 1), :] = out_ref[2, pl.ds(x * NL, 1), :] + force[x : x + 1]
    uplift = out_ref[2, pl.ds(0, CX, stride=NL), :]
    tiles_ref[...] = exact_dot(pick_ref[:, :CX], uplift)


def shallow_kernel(cur_ref, prev_ref, coef_ref, wet_ref, low_ref, high_ref, left_ref, right_ref, rows_ref, arrived_ref,
                   pick_ref, out_ref, tiles_ref, scratch, source_ref, left_pad, right_pad):
    fill_scratch(scratch, cur_ref, low_ref, high_ref, 3)
    for f in range(3):
        left_pad[f, pl.ds(EDGE, ROWS), :] = left_ref[f]
        right_pad[f, pl.ds(EDGE, ROWS), :] = right_ref[f]
    coarse_source = landing_sum(rows_ref, arrived_ref, REFINE * CX)
    for cb in range(REFINE):
        source_ref[pl.ds(cb, REFINE * CX, stride=REFINE), :] = exact_dot(coarse_source, spread(cb))
    lanes = lane_index(CHUNK)
    first_lane = lanes == 0
    last_lane = lanes == CY - 1
    first_block = row_mask(0, CHUNK, REFINE, 0)
    last_block = row_mask(0, CHUNK, REFINE, REFINE - 1)
    for r0 in range(0, ROWS, CHUNK):
        at = BASE + r0

        def rows_diff(f):
            return scratch[f, pl.ds(at + REFINE, CHUNK), :] - scratch[f, pl.ds(at - REFINE, CHUNK), :]

        def columns_diff(f):
            v = scratch[f, pl.ds(at, CHUNK), :]
            wrap_after = jnp.where(last_block, right_pad[f, pl.ds(EDGE + r0 - (REFINE - 1), CHUNK), :],
                                   pltpu.roll(scratch[f, pl.ds(at + 1, CHUNK), :], CY - 1, 1))
            wrap_before = jnp.where(first_block, left_pad[f, pl.ds(EDGE + r0 + REFINE - 1, CHUNK), :],
                                    pltpu.roll(scratch[f, pl.ds(at - 1, CHUNK), :], 1, 1))
            after = jnp.where(last_lane, wrap_after, pltpu.roll(v, CY - 1, 1))
            before = jnp.where(first_lane, wrap_before, pltpu.roll(v, 1, 1))
            return after - before

        wave = coef_ref[0, pl.ds(r0, CHUNK), :]
        area = coef_ref[1, pl.ds(r0, CHUNK), :]
        wet = wet_ref[pl.ds(r0, CHUNK), :].astype(jnp.float32)
        eta_r = rows_diff(0)
        eta_c = columns_diff(0)
        out_ref[1, pl.ds(r0, CHUNK), :] = wet * (prev_ref[1, pl.ds(r0, CHUNK), :] - wave * eta_r)
        out_ref[2, pl.ds(r0, CHUNK), :] = wet * (prev_ref[2, pl.ds(r0, CHUNK), :] - wave * eta_c)
        divergence = rows_diff(1) + columns_diff(2)
        out_ref[0, pl.ds(r0, CHUNK), :] = wet * (
            prev_ref[0, pl.ds(r0, CHUNK), :] - area * divergence + source_ref[pl.ds(r0, CHUNK), :]
        )
    total = jnp.zeros((REFINE * CX, CY), jnp.float32)
    for cb in range(REFINE):
        total = total + exact_dot(out_ref[0, pl.ds(cb, REFINE * CX, stride=REFINE), :], spread(cb).T)
    tiles_ref[...] = exact_dot(pick_ref[...], total / REFINE)


def vmem_specs(count):
    return [pl.BlockSpec(memory_space=pltpu.VMEM)] * count


def run_step(kernel, scratch_shapes, *operands):
    slots = operands[-1].shape[0]
    return pl.pallas_call(
        kernel,
        out_shape=(
            jax.ShapeDtypeStruct((3, ROWS, CY), jnp.float32),
            jax.ShapeDtypeStruct((slots, CY), jnp.float32),
        ),
        in_specs=vmem_specs(len(operands)),
        out_specs=tuple(vmem_specs(2)),
        scratch_shapes=scratch_shapes,
    )(*operands)


def route(payload):
    tile_data, tile_rows = payload
    width = tile_data.shape[-1]
    received_data, received_rows = (
        lax.all_to_all(tile_data, ("gx", "gy"), split_axis=0, concat_axis=0, tiled=True),
        lax.all_to_all(tile_rows, ("gx", "gy"), split_axis=0, concat_axis=0, tiled=True),
    )
    return (received_data.reshape(-1, width), received_rows.reshape(-1))


def deliver(outgoing, send_rows):
    routed = route((outgoing, send_rows))
    return from_partner((routed[0], routed[1]), "sec", 0)


def on_device(state, previous, coeff, wet_mask, link_dest, link_rows, link_weight):
    section = lax.axis_index("sec")
    owners = lax.axis_size("gx") * lax.axis_size("gy")
    fine_rows = REFINE * CX
    fine_cols = REFINE * CY
    current = state[0, :, 0, 0].reshape(3, ROWS, CY)
    earlier = previous[0, :, 0, 0].reshape(3, ROWS, CY)
    factors = coeff[0, :, 0, 0].reshape(2, ROWS, CY)
    wet = wet_mask[0, 0].reshape(ROWS, CY)
    targets = link_dest.reshape(-1)
    pairs = link_rows.reshape(-1, 2)
    source_rows = pairs[:, 0]
    landing = pairs[:, 1]
    weights = link_weight.reshape(-1)
    one_hot = (targets[:, None] == jnp.arange(owners, dtype=jnp.int32)[None, :]).astype(jnp.int32)
    before = jnp.cumsum(one_hot, axis=0) - one_hot
    slot_index = jnp.sum(before * one_hot, axis=1)
    position = targets * CAP + slot_index
    send_rows = jnp.zeros((owners * CAP,), jnp.int32).at[position].set(landing).reshape(owners, CAP)
    slot_rows = jnp.full((owners * CAP,), -1, jnp.int32).at[position].set(source_rows)
    slot_weights = jnp.zeros((owners * CAP,), jnp.float32).at[position].set(weights)
    pick = jnp.where(slot_rows[:, None] == jnp.arange(fine_rows, dtype=jnp.int32)[None, :], slot_weights[:, None], 0.0)

    def elastic_rows():
        return current[2].reshape(CX, NL, CY)[:, 0, :][source_rows]

    def shallow_rows():
        picked_fine = current[0].reshape(fine_rows, fine_cols)[source_rows]
        return jnp.sum(picked_fine.reshape(-1, CY, REFINE), axis=-1) / REFINE

    picked = lax.cond(section == 0, elastic_rows, shallow_rows)
    outgoing = jnp.zeros((owners * CAP, CY), jnp.float32).at[position].set(picked * weights[:, None])
    for step_index in range(STEPS):
        low_x, high_x, low_y, high_y = exchange_halos(current)
        arrived, arrived_rows = deliver(outgoing.reshape(owners, CAP, CY), send_rows)
        arrived_rows = arrived_rows.reshape(1, -1)

        def elastic_branch():
            scratch = [pltpu.VMEM((3, PAD_ROWS, CY), jnp.float32)]
            return run_step(elastic_kernel, scratch, current, earlier, factors, low_x, high_x, low_y, high_y,
                            arrived_rows, arrived, pick)

        def shallow_branch():
            scratch = [
                pltpu.VMEM((3, PAD_ROWS, CY), jnp.float32),
                pltpu.VMEM((ROWS, CY), jnp.float32),
                pltpu.VMEM((3, ROWS + 2 * EDGE, 1), jnp.float32),
                pltpu.VMEM((3, ROWS + 2 * EDGE, 1), jnp.float32),
            ]
            return run_step(shallow_kernel, scratch, current, earlier, factors, wet, low_x, high_x, low_y, high_y,
                            arrived_rows, arrived, pick)

        updated, outgoing = lax.cond(section == 0, elastic_branch, shallow_branch)
        earlier, current = (current, updated)
    return current.reshape(1, 3, 1, 1, -1)


def solution(mesh):
    placed = (
        P("sec", None, "gx", "gy", None),
        P("sec", None, "gx", "gy", None),
        P("sec", None, "gx", "gy", None),
        P("gx", "gy", None),
        P("sec", "gx", "gy", None, None),
        P("sec", "gx", "gy", None, None),
        P("sec", "gx", "gy", None),
    )
    return jax.shard_map(
        on_device,
        mesh=mesh,
        in_specs=placed,
        out_specs=P("sec", None, "gx", "gy", None),
        check_vma=False,
    )
```

```python
import functools

import jax
import jax.numpy as jnp
from jax import lax
from jax.experimental import pallas as pl
from jax.experimental.pallas import tpu as pltpu
from jax.sharding import PartitionSpec as P

CX = 8
CY = 128
REFINE = 10
NL = 100
STEPS = 4
CAP = 4

ROWS = CX * NL
BASE = 104
PAD_ROWS = BASE + ROWS + NL + 8
CHUNK = 40
EDGE = 16


def from_partner(value, axis, stride):
    return lax.ppermute(value, axis, [(i, i ^ 1 << stride) for i in range(lax.axis_size(axis))])


def shift_pairs(axis):
    count = lax.axis_size(axis)
    forward = [(i, i + 1) for i in range(count - 1)]
    backward = [(target, source) for source, target in forward]
    return forward, backward


def exchange_halos(current):
    forward_x, backward_x = shift_pairs("gx")
    forward_y, backward_y = shift_pairs("gy")
    low_x = lax.ppermute(current[:, ROWS - NL :], "gx", forward_x)
    high_x = lax.ppermute(current[:, :NL], "gx", backward_x)
    low_y = lax.ppermute(current[:, :, CY - 1 :], "gy", forward_y)
    high_y = lax.ppermute(current[:, :, :1], "gy", backward_y)
    return low_x, high_x, low_y, high_y


def fill_scratch(scratch, cur_ref, low_ref, high_ref, fields):
    for f in range(fields):
        scratch[f, pl.ds(BASE - NL, NL), :] = low_ref[f]
        scratch[f, pl.ds(BASE, ROWS), :] = cur_ref[f]
        scratch[f, pl.ds(BASE + ROWS, NL), :] = high_ref[f]


def lane_index(rows):
    return lax.broadcasted_iota(jnp.int32, (rows, CY), 1)


def row_mask(r0, rows, period, phase):
    local = lax.broadcasted_iota(jnp.int32, (rows, CY), 0)
    mask = jnp.zeros((rows, CY), jnp.bool_)
    for r in range(rows):
        if (r0 + r) % period == phase:
            mask = mask | (local == r)
    return mask


def exact_dot(a, b):
    return jnp.dot(a, b, precision=lax.Precision.HIGHEST, preferred_element_type=jnp.float32)


def landing_sum(rows_ref, arrived_ref, count):
    slots = rows_ref.shape[1]
    one_hot = (lax.broadcasted_iota(jnp.int32, (count, slots), 0) == rows_ref[...]).astype(jnp.float32)
    return exact_dot(one_hot, arrived_ref[...])


def spread(cb):
    coarse = lax.broadcasted_iota(jnp.int32, (CY, CY), 0)
    fine = lax.broadcasted_iota(jnp.int32, (CY, CY), 1) + cb * CY
    return ((fine >= coarse * REFINE) & (fine < coarse * REFINE + REFINE)).astype(jnp.float32)


def elastic_kernel(cur_ref, prev_ref, coef_ref, low_ref, high_ref, left_ref, right_ref, rows_ref, arrived_ref,
                   pick_ref, out_ref, tiles_ref, scratch):
    fill_scratch(scratch, cur_ref, low_ref, high_ref, 3)
    force = landing_sum(rows_ref, arrived_ref, CX)
    lanes = lane_index(CHUNK)
    first_lane = lanes == 0
    last_lane = lanes == CY - 1
    own_axis = (0, 2, 1)
    for r0 in range(0, ROWS, CHUNK):
        top_layer = row_mask(r0, CHUNK, NL, 0)
        bottom_layer = row_mask(r0, CHUNK, NL, NL - 1)
        shear = coef_ref[0, pl.ds(r0, CHUNK), :]
        lame = coef_ref[1, pl.ds(r0, CHUNK), :]
        stiffness = lame + 2.0 * shear
        for c in range(3):
            at = BASE + r0
            v = scratch[c, pl.ds(at, CHUNK), :]
            along_first = scratch[c, pl.ds(at + NL, CHUNK), :] - 2.0 * v + scratch[c, pl.ds(at - NL, CHUNK), :]
            deeper = jnp.where(bottom_layer, 0.0, scratch[c, pl.ds(at + 1, CHUNK), :])
            shallower = jnp.where(top_layer, 0.0, scratch[c, pl.ds(at - 1, CHUNK), :])
            along_depth = deeper - 2.0 * v + shallower
            after = jnp.where(last_lane, right_ref[c, pl.ds(r0, CHUNK), :], pltpu.roll(v, CY - 1, 1))
            before = jnp.where(first_lane, left_ref[c, pl.ds(r0, CHUNK), :], pltpu.roll(v, 1, 1))
            along_second = after - 2.0 * v + before
            factors = [stiffness if own_axis[c] == axis_index else shear for axis_index in range(3)]
            acceleration = factors[0] * along_first + factors[1] * along_depth + factors[2] * along_second
            out_ref[c, pl.ds(r0, CHUNK), :] = 2.0 * v - prev_ref[c, pl.ds(r0, CHUNK), :] + acceleration
    for x in range(CX):
        out_ref[2, pl.ds(x * NL, 1), :] = out_ref[2, pl.ds(x * NL, 1), :] + force[x : x + 1]
    uplift = out_ref[2, pl.ds(0, CX, stride=NL), :]
    tiles_ref[...] = exact_dot(pick_ref[:, :CX], uplift)


def shallow_kernel(cur_ref, prev_ref, coef_ref, wet_ref, low_ref, high_ref, left_ref, right_ref, rows_ref, arrived_ref,
                   pick_ref, out_ref, tiles_ref, scratch, source_ref, left_pad, right_pad):
    fill_scratch(scratch, cur_ref, low_ref, high_ref, 3)
    for f in range(3):
        left_pad[f, pl.ds(EDGE, ROWS), :] = left_ref[f]
        right_pad[f, pl.ds(EDGE, ROWS), :] = right_ref[f]
    coarse_source = landing_sum(rows_ref, arrived_ref, REFINE * CX)
    for cb in range(REFINE):
        source_ref[pl.ds(cb, REFINE * CX, stride=REFINE), :] = exact_dot(coarse_source, spread(cb))
    lanes = lane_index(CHUNK)
    first_lane = lanes == 0
    last_lane = lanes == CY - 1
    first_block = row_mask(0, CHUNK, REFINE, 0)
    last_block = row_mask(0, CHUNK, REFINE, REFINE - 1)
    for r0 in range(0, ROWS, CHUNK):
        at = BASE + r0

        def rows_diff(f):
            return scratch[f, pl.ds(at + REFINE, CHUNK), :] - scratch[f, pl.ds(at - REFINE, CHUNK), :]

        def columns_diff(f):
            v = scratch[f, pl.ds(at, CHUNK), :]
            wrap_after = jnp.where(last_block, right_pad[f, pl.ds(EDGE + r0 - (REFINE - 1), CHUNK), :],
                                   pltpu.roll(scratch[f, pl.ds(at + 1, CHUNK), :], CY - 1, 1))
            wrap_before = jnp.where(first_block, left_pad[f, pl.ds(EDGE + r0 + REFINE - 1, CHUNK), :],
                                    pltpu.roll(scratch[f, pl.ds(at - 1, CHUNK), :], 1, 1))
            after = jnp.where(last_lane, wrap_after, pltpu.roll(v, CY - 1, 1))
            before = jnp.where(first_lane, wrap_before, pltpu.roll(v, 1, 1))
            return after - before

        wave = coef_ref[0, pl.ds(r0, CHUNK), :]
        area = coef_ref[1, pl.ds(r0, CHUNK), :]
        wet = wet_ref[pl.ds(r0, CHUNK), :].astype(jnp.float32)
        eta_r = rows_diff(0)
        eta_c = columns_diff(0)
        out_ref[1, pl.ds(r0, CHUNK), :] = wet * (prev_ref[1, pl.ds(r0, CHUNK), :] - wave * eta_r)
        out_ref[2, pl.ds(r0, CHUNK), :] = wet * (prev_ref[2, pl.ds(r0, CHUNK), :] - wave * eta_c)
        divergence = rows_diff(1) + columns_diff(2)
        out_ref[0, pl.ds(r0, CHUNK), :] = wet * (
            prev_ref[0, pl.ds(r0, CHUNK), :] - area * divergence + source_ref[pl.ds(r0, CHUNK), :]
        )
    total = jnp.zeros((REFINE * CX, CY), jnp.float32)
    for cb in range(REFINE):
        total = total + exact_dot(out_ref[0, pl.ds(cb, REFINE * CX, stride=REFINE), :], spread(cb).T)
    tiles_ref[...] = exact_dot(pick_ref[...], total / REFINE)


def vmem_specs(count):
    return [pl.BlockSpec(memory_space=pltpu.VMEM)] * count


def run_step(kernel, scratch_shapes, *operands):
    slots = operands[-1].shape[0]
    return pl.pallas_call(
        kernel,
        out_shape=(
            jax.ShapeDtypeStruct((3, ROWS, CY), jnp.float32),
            jax.ShapeDtypeStruct((slots, CY), jnp.float32),
        ),
        in_specs=vmem_specs(len(operands)),
        out_specs=tuple(vmem_specs(2)),
        scratch_shapes=scratch_shapes,
    )(*operands)


def exchange_kernel(sizes, out_ref, in_ref, land, send_sem, recv_sem):
    owners, columns = sizes
    other = 1 - lax.axis_index("sec")
    me = lax.axis_index("gx") * columns + lax.axis_index("gy")
    barrier = pltpu.get_barrier_semaphore()

    def greet(d, carry):
        pl.semaphore_signal(barrier, inc=1, device_id=(other, d // columns, d % columns),
                            device_id_type=pl.DeviceIdType.MESH)
        return carry

    lax.fori_loop(0, owners, greet, 0)
    pl.semaphore_wait(barrier, owners)

    def send(d, carry):
        pltpu.make_async_remote_copy(
            src_ref=out_ref.at[pl.ds(d * CAP, CAP)],
            dst_ref=land.at[pl.ds(me * CAP, CAP)],
            send_sem=send_sem,
            recv_sem=recv_sem,
            device_id=(other, d // columns, d % columns),
            device_id_type=pl.DeviceIdType.MESH,
        ).start()
        return carry

    lax.fori_loop(0, owners, send, 0)
    whole = pltpu.make_async_remote_copy(
        src_ref=out_ref,
        dst_ref=land,
        send_sem=send_sem,
        recv_sem=recv_sem,
        device_id=(other, lax.axis_index("gx"), lax.axis_index("gy")),
        device_id_type=pl.DeviceIdType.MESH,
    )
    whole.wait_send()
    whole.wait_recv()
    in_ref[...] = land[...]


def exchange_tiles(outgoing, owners, columns):
    return pl.pallas_call(
        functools.partial(exchange_kernel, (owners, columns)),
        out_shape=jax.ShapeDtypeStruct(outgoing.shape, jnp.float32),
        in_specs=vmem_specs(1),
        out_specs=pl.BlockSpec(memory_space=pltpu.VMEM),
        scratch_shapes=[
            pltpu.VMEM(outgoing.shape, jnp.float32),
            pltpu.SemaphoreType.DMA(()),
            pltpu.SemaphoreType.DMA(()),
        ],
        compiler_params=pltpu.CompilerParams(collective_id=0, has_side_effects=True),
    )(outgoing)


def route(payload):
    tile_data, tile_rows = payload
    width = tile_data.shape[-1]
    received_data, received_rows = (
        lax.all_to_all(tile_data, ("gx", "gy"), split_axis=0, concat_axis=0, tiled=True),
        lax.all_to_all(tile_rows, ("gx", "gy"), split_axis=0, concat_axis=0, tiled=True),
    )
    return (received_data.reshape(-1, width), received_rows.reshape(-1))


def deliver(outgoing, send_rows):
    routed = route((outgoing, send_rows))
    return from_partner((routed[0], routed[1]), "sec", 0)


def on_device(state, previous, coeff, wet_mask, link_dest, link_rows, link_weight):
    section = lax.axis_index("sec")
    owners = lax.axis_size("gx") * lax.axis_size("gy")
    fine_rows = REFINE * CX
    fine_cols = REFINE * CY
    current = state[0, :, 0, 0].reshape(3, ROWS, CY)
    earlier = previous[0, :, 0, 0].reshape(3, ROWS, CY)
    factors = coeff[0, :, 0, 0].reshape(2, ROWS, CY)
    wet = wet_mask[0, 0].reshape(ROWS, CY)
    targets = link_dest.reshape(-1)
    pairs = link_rows.reshape(-1, 2)
    source_rows = pairs[:, 0]
    landing = pairs[:, 1]
    weights = link_weight.reshape(-1)
    one_hot = (targets[:, None] == jnp.arange(owners, dtype=jnp.int32)[None, :]).astype(jnp.int32)
    before = jnp.cumsum(one_hot, axis=0) - one_hot
    slot_index = jnp.sum(before * one_hot, axis=1)
    position = targets * CAP + slot_index
    send_rows = jnp.zeros((owners * CAP,), jnp.int32).at[position].set(landing).reshape(owners, CAP)
    slot_rows = jnp.full((owners * CAP,), -1, jnp.int32).at[position].set(source_rows)
    slot_weights = jnp.zeros((owners * CAP,), jnp.float32).at[position].set(weights)
    pick = jnp.where(slot_rows[:, None] == jnp.arange(fine_rows, dtype=jnp.int32)[None, :], slot_weights[:, None], 0.0)

    def elastic_rows():
        return current[2].reshape(CX, NL, CY)[:, 0, :][source_rows]

    def shallow_rows():
        picked_fine = current[0].reshape(fine_rows, fine_cols)[source_rows]
        return jnp.sum(picked_fine.reshape(-1, CY, REFINE), axis=-1) / REFINE

    picked = lax.cond(section == 0, elastic_rows, shallow_rows)
    outgoing = jnp.zeros((owners * CAP, CY), jnp.float32).at[position].set(picked * weights[:, None])
    arrived_rows = deliver(jnp.zeros((owners, CAP, CY), jnp.float32), send_rows)[1].reshape(1, -1)
    for step_index in range(STEPS):
        low_x, high_x, low_y, high_y = exchange_halos(current)
        arrived = exchange_tiles(outgoing, owners, lax.axis_size("gy"))

        def elastic_branch():
            scratch = [pltpu.VMEM((3, PAD_ROWS, CY), jnp.float32)]
            return run_step(elastic_kernel, scratch, current, earlier, factors, low_x, high_x, low_y, high_y,
                            arrived_rows, arrived, pick)

        def shallow_branch():
            scratch = [
                pltpu.VMEM((3, PAD_ROWS, CY), jnp.float32),
                pltpu.VMEM((ROWS, CY), jnp.float32),
                pltpu.VMEM((3, ROWS + 2 * EDGE, 1), jnp.float32),
                pltpu.VMEM((3, ROWS + 2 * EDGE, 1), jnp.float32),
            ]
            return run_step(shallow_kernel, scratch, current, earlier, factors, wet, low_x, high_x, low_y, high_y,
                            arrived_rows, arrived, pick)

        updated, outgoing = lax.cond(section == 0, elastic_branch, shallow_branch)
        earlier, current = (current, updated)
    return current.reshape(1, 3, 1, 1, -1)


def solution(mesh):
    placed = (
        P("sec", None, "gx", "gy", None),
        P("sec", None, "gx", "gy", None),
        P("sec", None, "gx", "gy", None),
        P("gx", "gy", None),
        P("sec", "gx", "gy", None, None),
        P("sec", "gx", "gy", None, None),
        P("sec", "gx", "gy", None),
    )
    return jax.shard_map(
        on_device,
        mesh=mesh,
        in_specs=placed,
        out_specs=P("sec", None, "gx", "gy", None),
        check_vma=False,
    )
```

```python
import functools

import jax
import jax.numpy as jnp
from jax import lax
from jax.experimental import pallas as pl
from jax.experimental.pallas import tpu as pltpu
from jax.sharding import PartitionSpec as P

CX = 8
CY = 128
REFINE = 10
NL = 100
STEPS = 4
CAP = 4

ROWS = CX * NL
BASE = 104
PAD_ROWS = BASE + ROWS + BASE
CHUNK = 40
EDGE = 16
HALO_ROWS = NL + 4


def from_partner(value, axis, stride):
    return lax.ppermute(value, axis, [(i, i ^ 1 << stride) for i in range(lax.axis_size(axis))])


def shift_pairs(axis):
    count = lax.axis_size(axis)
    forward = [(i, i + 1) for i in range(count - 1)]
    backward = [(target, source) for source, target in forward]
    return forward, backward


def exchange_halos(current):
    forward_y, backward_y = shift_pairs("gy")
    low_y = lax.ppermute(current[:, :, CY - 1 :], "gy", forward_y)
    high_y = lax.ppermute(current[:, :, :1], "gy", backward_y)
    return low_y, high_y


def fill_scratch(scratch, cur_ref, low_ref, high_ref, fields):
    for f in range(fields):
        scratch[f, pl.ds(BASE - HALO_ROWS, HALO_ROWS), :] = low_ref[f]
        scratch[f, pl.ds(BASE, ROWS), :] = cur_ref[f]
        scratch[f, pl.ds(BASE + ROWS, HALO_ROWS), :] = high_ref[f]


def lane_index(rows):
    return lax.broadcasted_iota(jnp.int32, (rows, CY), 1)


def row_mask(r0, rows, period, phase):
    local = lax.broadcasted_iota(jnp.int32, (rows, CY), 0)
    mask = jnp.zeros((rows, CY), jnp.bool_)
    for r in range(rows):
        if (r0 + r) % period == phase:
            mask = mask | (local == r)
    return mask


def exact_dot(a, b):
    return jnp.dot(a, b, precision=lax.Precision.HIGHEST, preferred_element_type=jnp.float32)


def landing_sum(rows_ref, arrived_ref, count):
    slots = rows_ref.shape[1]
    one_hot = (lax.broadcasted_iota(jnp.int32, (count, slots), 0) == rows_ref[...]).astype(jnp.float32)
    return exact_dot(one_hot, arrived_ref[...])


def spread(cb):
    coarse = lax.broadcasted_iota(jnp.int32, (CY, CY), 0)
    fine = lax.broadcasted_iota(jnp.int32, (CY, CY), 1) + cb * CY
    return ((fine >= coarse * REFINE) & (fine < coarse * REFINE + REFINE)).astype(jnp.float32)


def elastic_kernel(cur_ref, prev_ref, coef_ref, low_ref, high_ref, left_ref, right_ref, rows_ref, arrived_ref,
                   pick_ref, out_ref, tiles_ref, scratch):
    fill_scratch(scratch, cur_ref, low_ref, high_ref, 3)
    force = landing_sum(rows_ref, arrived_ref, CX)
    lanes = lane_index(CHUNK)
    first_lane = lanes == 0
    last_lane = lanes == CY - 1
    own_axis = (0, 2, 1)
    for r0 in range(0, ROWS, CHUNK):
        top_layer = row_mask(r0, CHUNK, NL, 0)
        bottom_layer = row_mask(r0, CHUNK, NL, NL - 1)
        shear = coef_ref[0, pl.ds(r0, CHUNK), :]
        lame = coef_ref[1, pl.ds(r0, CHUNK), :]
        stiffness = lame + 2.0 * shear
        for c in range(3):
            at = BASE + r0
            v = scratch[c, pl.ds(at, CHUNK), :]
            along_first = scratch[c, pl.ds(at + NL, CHUNK), :] - 2.0 * v + scratch[c, pl.ds(at - NL, CHUNK), :]
            deeper = jnp.where(bottom_layer, 0.0, scratch[c, pl.ds(at + 1, CHUNK), :])
            shallower = jnp.where(top_layer, 0.0, scratch[c, pl.ds(at - 1, CHUNK), :])
            along_depth = deeper - 2.0 * v + shallower
            after = jnp.where(last_lane, right_ref[c, pl.ds(r0, CHUNK), :], pltpu.roll(v, CY - 1, 1))
            before = jnp.where(first_lane, left_ref[c, pl.ds(r0, CHUNK), :], pltpu.roll(v, 1, 1))
            along_second = after - 2.0 * v + before
            factors = [stiffness if own_axis[c] == axis_index else shear for axis_index in range(3)]
            acceleration = factors[0] * along_first + factors[1] * along_depth + factors[2] * along_second
            out_ref[c, pl.ds(r0, CHUNK), :] = 2.0 * v - prev_ref[c, pl.ds(r0, CHUNK), :] + acceleration
    for x in range(CX):
        out_ref[2, pl.ds(x * NL, 1), :] = out_ref[2, pl.ds(x * NL, 1), :] + force[x : x + 1]
    uplift = out_ref[2, pl.ds(0, CX, stride=NL), :]
    tiles_ref[...] = exact_dot(pick_ref[:, :CX], uplift)


def shallow_kernel(cur_ref, prev_ref, coef_ref, wet_ref, low_ref, high_ref, left_ref, right_ref, rows_ref, arrived_ref,
                   pick_ref, out_ref, tiles_ref, scratch, source_ref, left_pad, right_pad):
    fill_scratch(scratch, cur_ref, low_ref, high_ref, 3)
    for f in range(3):
        left_pad[f, pl.ds(EDGE, ROWS), :] = left_ref[f]
        right_pad[f, pl.ds(EDGE, ROWS), :] = right_ref[f]
    coarse_source = landing_sum(rows_ref, arrived_ref, REFINE * CX)
    for cb in range(REFINE):
        source_ref[pl.ds(cb, REFINE * CX, stride=REFINE), :] = exact_dot(coarse_source, spread(cb))
    lanes = lane_index(CHUNK)
    first_lane = lanes == 0
    last_lane = lanes == CY - 1
    first_block = row_mask(0, CHUNK, REFINE, 0)
    last_block = row_mask(0, CHUNK, REFINE, REFINE - 1)
    for r0 in range(0, ROWS, CHUNK):
        at = BASE + r0

        def rows_diff(f):
            return scratch[f, pl.ds(at + REFINE, CHUNK), :] - scratch[f, pl.ds(at - REFINE, CHUNK), :]

        def columns_diff(f):
            v = scratch[f, pl.ds(at, CHUNK), :]
            wrap_after = jnp.where(last_block, right_pad[f, pl.ds(EDGE + r0 - (REFINE - 1), CHUNK), :],
                                   pltpu.roll(scratch[f, pl.ds(at + 1, CHUNK), :], CY - 1, 1))
            wrap_before = jnp.where(first_block, left_pad[f, pl.ds(EDGE + r0 + REFINE - 1, CHUNK), :],
                                    pltpu.roll(scratch[f, pl.ds(at - 1, CHUNK), :], 1, 1))
            after = jnp.where(last_lane, wrap_after, pltpu.roll(v, CY - 1, 1))
            before = jnp.where(first_lane, wrap_before, pltpu.roll(v, 1, 1))
            return after - before

        wave = coef_ref[0, pl.ds(r0, CHUNK), :]
        area = coef_ref[1, pl.ds(r0, CHUNK), :]
        wet = wet_ref[pl.ds(r0, CHUNK), :].astype(jnp.float32)
        eta_r = rows_diff(0)
        eta_c = columns_diff(0)
        out_ref[1, pl.ds(r0, CHUNK), :] = wet * (prev_ref[1, pl.ds(r0, CHUNK), :] - wave * eta_r)
        out_ref[2, pl.ds(r0, CHUNK), :] = wet * (prev_ref[2, pl.ds(r0, CHUNK), :] - wave * eta_c)
        divergence = rows_diff(1) + columns_diff(2)
        out_ref[0, pl.ds(r0, CHUNK), :] = wet * (
            prev_ref[0, pl.ds(r0, CHUNK), :] - area * divergence + source_ref[pl.ds(r0, CHUNK), :]
        )
    total = jnp.zeros((REFINE * CX, CY), jnp.float32)
    for cb in range(REFINE):
        total = total + exact_dot(out_ref[0, pl.ds(cb, REFINE * CX, stride=REFINE), :], spread(cb).T)
    tiles_ref[...] = exact_dot(pick_ref[...], total / REFINE)


def vmem_specs(count):
    return [pl.BlockSpec(memory_space=pltpu.VMEM)] * count


def run_step(kernel, scratch_shapes, *operands):
    slots = operands[-1].shape[0]
    return pl.pallas_call(
        kernel,
        out_shape=(
            jax.ShapeDtypeStruct((3, ROWS, CY), jnp.float32),
            jax.ShapeDtypeStruct((slots, CY), jnp.float32),
        ),
        in_specs=vmem_specs(len(operands)),
        out_specs=tuple(vmem_specs(2)),
        scratch_shapes=scratch_shapes,
    )(*operands)


def exchange_kernel(sizes, cur_ref, out_ref, in_ref, low_ref, high_ref, land, halo, send_sem, recv_sem,
                    halo_send, halo_recv):
    owners, rows_of, columns = sizes
    other = 1 - lax.axis_index("sec")
    section = lax.axis_index("sec")
    gx = lax.axis_index("gx")
    gy = lax.axis_index("gy")
    me = gx * columns + gy
    has_low = gx > 0
    has_high = gx < rows_of - 1
    halo[...] = jnp.zeros_like(halo)
    barrier = pltpu.get_barrier_semaphore()
    def greet(d, carry):
        pl.semaphore_signal(barrier, inc=1, device_id=(other, d // columns, d % columns),
                            device_id_type=pl.DeviceIdType.MESH)
        return carry

    lax.fori_loop(0, owners, greet, 0, unroll=8)

    @pl.when(has_low)
    def _():
        pl.semaphore_signal(barrier, inc=1, device_id=(section, gx - 1, gy), device_id_type=pl.DeviceIdType.MESH)

    @pl.when(has_high)
    def _():
        pl.semaphore_signal(barrier, inc=1, device_id=(section, gx + 1, gy), device_id_type=pl.DeviceIdType.MESH)

    pl.semaphore_wait(barrier, owners + has_low.astype(jnp.int32) + has_high.astype(jnp.int32))

    def slab_copy(start, slot, target):
        return pltpu.make_async_remote_copy(
            src_ref=cur_ref.at[:, pl.ds(start, HALO_ROWS), :],
            dst_ref=halo.at[slot],
            send_sem=halo_send.at[slot],
            recv_sem=halo_recv.at[slot],
            device_id=(section, target, gy),
            device_id_type=pl.DeviceIdType.MESH,
        )

    @pl.when(has_high)
    def _():
        slab_copy(ROWS - HALO_ROWS, 0, gx + 1).start()

    @pl.when(has_low)
    def _():
        slab_copy(0, 1, gx - 1).start()

    def send(d, carry):
        pltpu.make_async_remote_copy(
            src_ref=out_ref.at[pl.ds(d * CAP, CAP)],
            dst_ref=land.at[pl.ds(me * CAP, CAP)],
            send_sem=send_sem,
            recv_sem=recv_sem,
            device_id=(other, d // columns, d % columns),
            device_id_type=pl.DeviceIdType.MESH,
        ).start()
        return carry

    lax.fori_loop(0, owners, send, 0, unroll=8)
    whole = pltpu.make_async_remote_copy(
        src_ref=out_ref,
        dst_ref=land,
        send_sem=send_sem,
        recv_sem=recv_sem,
        device_id=(other, gx, gy),
        device_id_type=pl.DeviceIdType.MESH,
    )

    @pl.when(has_high)
    def _():
        slab_copy(ROWS - HALO_ROWS, 0, gx + 1).wait_send()
        slab_copy(0, 1, gx + 1).wait_recv()

    @pl.when(has_low)
    def _():
        slab_copy(0, 1, gx - 1).wait_send()
        slab_copy(ROWS - HALO_ROWS, 0, gx - 1).wait_recv()

    whole.wait_send()
    whole.wait_recv()
    in_ref[...] = land[...]
    low_ref[...] = halo[0]
    high_ref[...] = halo[1]


def exchange(current, outgoing, owners, rows_of, columns):
    halo_shape = jax.ShapeDtypeStruct((3, HALO_ROWS, CY), jnp.float32)
    return pl.pallas_call(
        functools.partial(exchange_kernel, (owners, rows_of, columns)),
        out_shape=(jax.ShapeDtypeStruct(outgoing.shape, jnp.float32), halo_shape, halo_shape),
        in_specs=[pl.BlockSpec(memory_space=pl.ANY), pl.BlockSpec(memory_space=pltpu.VMEM)],
        out_specs=tuple(vmem_specs(3)),
        scratch_shapes=[
            pltpu.VMEM(outgoing.shape, jnp.float32),
            pltpu.VMEM((2, 3, HALO_ROWS, CY), jnp.float32),
            pltpu.SemaphoreType.DMA(()),
            pltpu.SemaphoreType.DMA(()),
            pltpu.SemaphoreType.DMA((2,)),
            pltpu.SemaphoreType.DMA((2,)),
        ],
        compiler_params=pltpu.CompilerParams(collective_id=0, has_side_effects=True),
    )(current, outgoing)


def route(payload):
    tile_data, tile_rows = payload
    width = tile_data.shape[-1]
    received_data, received_rows = (
        lax.all_to_all(tile_data, ("gx", "gy"), split_axis=0, concat_axis=0, tiled=True),
        lax.all_to_all(tile_rows, ("gx", "gy"), split_axis=0, concat_axis=0, tiled=True),
    )
    return (received_data.reshape(-1, width), received_rows.reshape(-1))


def deliver(outgoing, send_rows):
    routed = route((outgoing, send_rows))
    return from_partner((routed[0], routed[1]), "sec", 0)


def on_device(state, previous, coeff, wet_mask, link_dest, link_rows, link_weight):
    section = lax.axis_index("sec")
    owners = lax.axis_size("gx") * lax.axis_size("gy")
    fine_rows = REFINE * CX
    fine_cols = REFINE * CY
    current = state[0, :, 0, 0].reshape(3, ROWS, CY)
    earlier = previous[0, :, 0, 0].reshape(3, ROWS, CY)
    factors = coeff[0, :, 0, 0].reshape(2, ROWS, CY)
    wet = wet_mask[0, 0].reshape(ROWS, CY)
    targets = link_dest.reshape(-1)
    pairs = link_rows.reshape(-1, 2)
    source_rows = pairs[:, 0]
    landing = pairs[:, 1]
    weights = link_weight.reshape(-1)
    one_hot = (targets[:, None] == jnp.arange(owners, dtype=jnp.int32)[None, :]).astype(jnp.int32)
    before = jnp.cumsum(one_hot, axis=0) - one_hot
    slot_index = jnp.sum(before * one_hot, axis=1)
    position = targets * CAP + slot_index
    send_rows = jnp.zeros((owners * CAP,), jnp.int32).at[position].set(landing).reshape(owners, CAP)
    slot_rows = jnp.full((owners * CAP,), -1, jnp.int32).at[position].set(source_rows)
    slot_weights = jnp.zeros((owners * CAP,), jnp.float32).at[position].set(weights)
    pick = jnp.where(slot_rows[:, None] == jnp.arange(fine_rows, dtype=jnp.int32)[None, :], slot_weights[:, None], 0.0)

    def elastic_rows():
        return current[2].reshape(CX, NL, CY)[:, 0, :][source_rows]

    def shallow_rows():
        picked_fine = current[0].reshape(fine_rows, fine_cols)[source_rows]
        return jnp.sum(picked_fine.reshape(-1, CY, REFINE), axis=-1) / REFINE

    picked = lax.cond(section == 0, elastic_rows, shallow_rows)
    outgoing = jnp.zeros((owners * CAP, CY), jnp.float32).at[position].set(picked * weights[:, None])
    arrived_rows = deliver(jnp.zeros((owners, CAP, CY), jnp.float32), send_rows)[1].reshape(1, -1)
    for step_index in range(STEPS):
        low_y, high_y = exchange_halos(current)
        arrived, low_x, high_x = exchange(current, outgoing, owners, lax.axis_size("gx"), lax.axis_size("gy"))

        def elastic_branch():
            scratch = [pltpu.VMEM((3, PAD_ROWS, CY), jnp.float32)]
            return run_step(elastic_kernel, scratch, current, earlier, factors, low_x, high_x, low_y, high_y,
                            arrived_rows, arrived, pick)

        def shallow_branch():
            scratch = [
                pltpu.VMEM((3, PAD_ROWS, CY), jnp.float32),
                pltpu.VMEM((ROWS, CY), jnp.float32),
                pltpu.VMEM((3, ROWS + 2 * EDGE, 1), jnp.float32),
                pltpu.VMEM((3, ROWS + 2 * EDGE, 1), jnp.float32),
            ]
            return run_step(shallow_kernel, scratch, current, earlier, factors, wet, low_x, high_x, low_y, high_y,
                            arrived_rows, arrived, pick)

        updated, outgoing = lax.cond(section == 0, elastic_branch, shallow_branch)
        earlier, current = (current, updated)
    return current.reshape(1, 3, 1, 1, -1)


def solution(mesh):
    placed = (
        P("sec", None, "gx", "gy", None),
        P("sec", None, "gx", "gy", None),
        P("sec", None, "gx", "gy", None),
        P("gx", "gy", None),
        P("sec", "gx", "gy", None, None),
        P("sec", "gx", "gy", None, None),
        P("sec", "gx", "gy", None),
    )
    return jax.shard_map(
        on_device,
        mesh=mesh,
        in_specs=placed,
        out_specs=P("sec", None, "gx", "gy", None),
        check_vma=False,
    )
```

```python
import functools

import jax
import jax.numpy as jnp
from jax import lax
from jax.experimental import pallas as pl
from jax.experimental.pallas import tpu as pltpu
from jax.sharding import PartitionSpec as P

CX = 8
CY = 128
REFINE = 10
NL = 100
STEPS = 4
CAP = 4

ROWS = CX * NL
BASE = 104
PAD_ROWS = BASE + ROWS + BASE
CHUNK = 40
EDGE = 16
HALO_ROWS = NL + 4
EDGE_LANES = 896


def from_partner(value, axis, stride):
    return lax.ppermute(value, axis, [(i, i ^ 1 << stride) for i in range(lax.axis_size(axis))])


def shift_pairs(axis):
    count = lax.axis_size(axis)
    forward = [(i, i + 1) for i in range(count - 1)]
    backward = [(target, source) for source, target in forward]
    return forward, backward


def fill_scratch(scratch, cur_ref, low_ref, high_ref, fields):
    for f in range(fields):
        scratch[f, pl.ds(BASE - HALO_ROWS, HALO_ROWS), :] = low_ref[f]
        scratch[f, pl.ds(BASE, ROWS), :] = cur_ref[f]
        scratch[f, pl.ds(BASE + ROWS, HALO_ROWS), :] = high_ref[f]


def lane_index(rows):
    return lax.broadcasted_iota(jnp.int32, (rows, CY), 1)


def row_mask(r0, rows, period, phase):
    local = lax.broadcasted_iota(jnp.int32, (rows, CY), 0)
    mask = jnp.zeros((rows, CY), jnp.bool_)
    for r in range(rows):
        if (r0 + r) % period == phase:
            mask = mask | (local == r)
    return mask


def exact_dot(a, b):
    return jnp.dot(a, b, precision=lax.Precision.HIGHEST, preferred_element_type=jnp.float32)


def landing_sum(rows_ref, arrived_ref, count):
    slots = rows_ref.shape[1]
    one_hot = (lax.broadcasted_iota(jnp.int32, (count, slots), 0) == rows_ref[...]).astype(jnp.float32)
    return exact_dot(one_hot, arrived_ref[...])


def edge_rows(out_ref, edges_ref):
    rows = lax.broadcasted_iota(jnp.int32, (8, CY), 0)
    lanes = lax.broadcasted_iota(jnp.int32, (8, CY), 1)
    select = (((rows == 0) & (lanes == CY - 1)) | ((rows == 1) & (lanes == 0))).astype(jnp.float32)
    for f in range(3):
        picked = lax.dot_general(select, out_ref[f], (((1,), (1,)), ((), ())), precision=lax.Precision.HIGHEST,
                                 preferred_element_type=jnp.float32)
        edges_ref[f] = jnp.zeros(edges_ref.shape[1:], jnp.float32)
        edges_ref[f, :, pl.ds(0, ROWS)] = picked


def fill_sides(low_rows_ref, high_rows_ref, left_pad, right_pad):
    for f in range(3):
        left_pad[f, pl.ds(EDGE, ROWS), :] = jnp.transpose(low_rows_ref[f])[:ROWS, 0:1]
        right_pad[f, pl.ds(EDGE, ROWS), :] = jnp.transpose(high_rows_ref[f])[:ROWS, 1:2]


def spread(cb):
    coarse = lax.broadcasted_iota(jnp.int32, (CY, CY), 0)
    fine = lax.broadcasted_iota(jnp.int32, (CY, CY), 1) + cb * CY
    return ((fine >= coarse * REFINE) & (fine < coarse * REFINE + REFINE)).astype(jnp.float32)


def elastic_kernel(cur_ref, prev_ref, coef_ref, low_ref, high_ref, low_rows_ref, high_rows_ref, rows_ref, arrived_ref,
                   pick_ref, out_ref, tiles_ref, edges_ref, scratch, left_pad, right_pad):
    fill_scratch(scratch, cur_ref, low_ref, high_ref, 3)
    fill_sides(low_rows_ref, high_rows_ref, left_pad, right_pad)
    force = landing_sum(rows_ref, arrived_ref, CX)
    lanes = lane_index(CHUNK)
    first_lane = lanes == 0
    last_lane = lanes == CY - 1
    own_axis = (0, 2, 1)
    for r0 in range(0, ROWS, CHUNK):
        top_layer = row_mask(r0, CHUNK, NL, 0)
        bottom_layer = row_mask(r0, CHUNK, NL, NL - 1)
        shear = coef_ref[0, pl.ds(r0, CHUNK), :]
        lame = coef_ref[1, pl.ds(r0, CHUNK), :]
        stiffness = lame + 2.0 * shear
        for c in range(3):
            at = BASE + r0
            v = scratch[c, pl.ds(at, CHUNK), :]
            along_first = scratch[c, pl.ds(at + NL, CHUNK), :] - 2.0 * v + scratch[c, pl.ds(at - NL, CHUNK), :]
            deeper = jnp.where(bottom_layer, 0.0, scratch[c, pl.ds(at + 1, CHUNK), :])
            shallower = jnp.where(top_layer, 0.0, scratch[c, pl.ds(at - 1, CHUNK), :])
            along_depth = deeper - 2.0 * v + shallower
            after = jnp.where(last_lane, right_pad[c, pl.ds(EDGE + r0, CHUNK), :], pltpu.roll(v, CY - 1, 1))
            before = jnp.where(first_lane, left_pad[c, pl.ds(EDGE + r0, CHUNK), :], pltpu.roll(v, 1, 1))
            along_second = after - 2.0 * v + before
            factors = [stiffness if own_axis[c] == axis_index else shear for axis_index in range(3)]
            acceleration = factors[0] * along_first + factors[1] * along_depth + factors[2] * along_second
            out_ref[c, pl.ds(r0, CHUNK), :] = 2.0 * v - prev_ref[c, pl.ds(r0, CHUNK), :] + acceleration
    for x in range(CX):
        out_ref[2, pl.ds(x * NL, 1), :] = out_ref[2, pl.ds(x * NL, 1), :] + force[x : x + 1]
    uplift = out_ref[2, pl.ds(0, CX, stride=NL), :]
    tiles_ref[...] = exact_dot(pick_ref[:, :CX], uplift)
    edge_rows(out_ref, edges_ref)


def shallow_kernel(cur_ref, prev_ref, coef_ref, wet_ref, low_ref, high_ref, low_rows_ref, high_rows_ref, rows_ref,
                   arrived_ref, pick_ref, out_ref, tiles_ref, edges_ref, scratch, source_ref, left_pad, right_pad):
    fill_scratch(scratch, cur_ref, low_ref, high_ref, 3)
    fill_sides(low_rows_ref, high_rows_ref, left_pad, right_pad)
    coarse_source = landing_sum(rows_ref, arrived_ref, REFINE * CX)
    for cb in range(REFINE):
        source_ref[pl.ds(cb, REFINE * CX, stride=REFINE), :] = exact_dot(coarse_source, spread(cb))
    lanes = lane_index(CHUNK)
    first_lane = lanes == 0
    last_lane = lanes == CY - 1
    first_block = row_mask(0, CHUNK, REFINE, 0)
    last_block = row_mask(0, CHUNK, REFINE, REFINE - 1)
    for r0 in range(0, ROWS, CHUNK):
        at = BASE + r0

        def rows_diff(f):
            return scratch[f, pl.ds(at + REFINE, CHUNK), :] - scratch[f, pl.ds(at - REFINE, CHUNK), :]

        def columns_diff(f):
            v = scratch[f, pl.ds(at, CHUNK), :]
            wrap_after = jnp.where(last_block, right_pad[f, pl.ds(EDGE + r0 - (REFINE - 1), CHUNK), :],
                                   pltpu.roll(scratch[f, pl.ds(at + 1, CHUNK), :], CY - 1, 1))
            wrap_before = jnp.where(first_block, left_pad[f, pl.ds(EDGE + r0 + REFINE - 1, CHUNK), :],
                                    pltpu.roll(scratch[f, pl.ds(at - 1, CHUNK), :], 1, 1))
            after = jnp.where(last_lane, wrap_after, pltpu.roll(v, CY - 1, 1))
            before = jnp.where(first_lane, wrap_before, pltpu.roll(v, 1, 1))
            return after - before

        wave = coef_ref[0, pl.ds(r0, CHUNK), :]
        area = coef_ref[1, pl.ds(r0, CHUNK), :]
        wet = wet_ref[pl.ds(r0, CHUNK), :].astype(jnp.float32)
        eta_r = rows_diff(0)
        eta_c = columns_diff(0)
        out_ref[1, pl.ds(r0, CHUNK), :] = wet * (prev_ref[1, pl.ds(r0, CHUNK), :] - wave * eta_r)
        out_ref[2, pl.ds(r0, CHUNK), :] = wet * (prev_ref[2, pl.ds(r0, CHUNK), :] - wave * eta_c)
        divergence = rows_diff(1) + columns_diff(2)
        out_ref[0, pl.ds(r0, CHUNK), :] = wet * (
            prev_ref[0, pl.ds(r0, CHUNK), :] - area * divergence + source_ref[pl.ds(r0, CHUNK), :]
        )
    total = jnp.zeros((REFINE * CX, CY), jnp.float32)
    for cb in range(REFINE):
        total = total + exact_dot(out_ref[0, pl.ds(cb, REFINE * CX, stride=REFINE), :], spread(cb).T)
    tiles_ref[...] = exact_dot(pick_ref[...], total / REFINE)
    edge_rows(out_ref, edges_ref)


def vmem_specs(count):
    return [pl.BlockSpec(memory_space=pltpu.VMEM)] * count


def run_step(kernel, scratch_shapes, *operands):
    slots = operands[-1].shape[0]
    return pl.pallas_call(
        kernel,
        out_shape=(
            jax.ShapeDtypeStruct((3, ROWS, CY), jnp.float32),
            jax.ShapeDtypeStruct((slots, CY), jnp.float32),
            jax.ShapeDtypeStruct((3, 8, EDGE_LANES), jnp.float32),
        ),
        in_specs=vmem_specs(len(operands)),
        out_specs=tuple(vmem_specs(3)),
        scratch_shapes=scratch_shapes,
    )(*operands)


def exchange_kernel(sizes, cur_ref, edges_ref, out_ref, in_ref, low_ref, high_ref, low_rows_ref, high_rows_ref,
                    land, halo, sides, send_sem, recv_sem, halo_send, halo_recv, side_send, side_recv):
    owners, rows_of, columns = sizes
    other = 1 - lax.axis_index("sec")
    section = lax.axis_index("sec")
    gx = lax.axis_index("gx")
    gy = lax.axis_index("gy")
    me = gx * columns + gy
    has_low = gx > 0
    has_high = gx < rows_of - 1
    has_left = gy > 0
    has_right = gy < columns - 1
    halo[...] = jnp.zeros_like(halo)
    sides[...] = jnp.zeros_like(sides)
    barrier = pltpu.get_barrier_semaphore()
    def greet(d, carry):
        pl.semaphore_signal(barrier, inc=1, device_id=(other, d // columns, d % columns),
                            device_id_type=pl.DeviceIdType.MESH)
        return carry

    lax.fori_loop(0, owners, greet, 0, unroll=8)

    @pl.when(has_low)
    def _():
        pl.semaphore_signal(barrier, inc=1, device_id=(section, gx - 1, gy), device_id_type=pl.DeviceIdType.MESH)

    @pl.when(has_high)
    def _():
        pl.semaphore_signal(barrier, inc=1, device_id=(section, gx + 1, gy), device_id_type=pl.DeviceIdType.MESH)

    @pl.when(has_left)
    def _():
        pl.semaphore_signal(barrier, inc=1, device_id=(section, gx, gy - 1), device_id_type=pl.DeviceIdType.MESH)

    @pl.when(has_right)
    def _():
        pl.semaphore_signal(barrier, inc=1, device_id=(section, gx, gy + 1), device_id_type=pl.DeviceIdType.MESH)

    neighbours = [has_low, has_high, has_left, has_right]
    pl.semaphore_wait(barrier, owners + sum(n.astype(jnp.int32) for n in neighbours))

    def side_copy(slot, target):
        return pltpu.make_async_remote_copy(
            src_ref=edges_ref,
            dst_ref=sides.at[slot],
            send_sem=side_send.at[slot],
            recv_sem=side_recv.at[slot],
            device_id=(section, gx, target),
            device_id_type=pl.DeviceIdType.MESH,
        )

    @pl.when(has_right)
    def _():
        side_copy(0, gy + 1).start()

    @pl.when(has_left)
    def _():
        side_copy(1, gy - 1).start()

    def slab_copy(start, slot, target):
        return pltpu.make_async_remote_copy(
            src_ref=cur_ref.at[:, pl.ds(start, HALO_ROWS), :],
            dst_ref=halo.at[slot],
            send_sem=halo_send.at[slot],
            recv_sem=halo_recv.at[slot],
            device_id=(section, target, gy),
            device_id_type=pl.DeviceIdType.MESH,
        )

    @pl.when(has_high)
    def _():
        slab_copy(ROWS - HALO_ROWS, 0, gx + 1).start()

    @pl.when(has_low)
    def _():
        slab_copy(0, 1, gx - 1).start()

    def send(d, carry):
        pltpu.make_async_remote_copy(
            src_ref=out_ref.at[pl.ds(d * CAP, CAP)],
            dst_ref=land.at[pl.ds(me * CAP, CAP)],
            send_sem=send_sem,
            recv_sem=recv_sem,
            device_id=(other, d // columns, d % columns),
            device_id_type=pl.DeviceIdType.MESH,
        ).start()
        return carry

    lax.fori_loop(0, owners, send, 0, unroll=8)
    whole = pltpu.make_async_remote_copy(
        src_ref=out_ref,
        dst_ref=land,
        send_sem=send_sem,
        recv_sem=recv_sem,
        device_id=(other, gx, gy),
        device_id_type=pl.DeviceIdType.MESH,
    )

    @pl.when(has_high)
    def _():
        slab_copy(ROWS - HALO_ROWS, 0, gx + 1).wait_send()
        slab_copy(0, 1, gx + 1).wait_recv()

    @pl.when(has_low)
    def _():
        slab_copy(0, 1, gx - 1).wait_send()
        slab_copy(ROWS - HALO_ROWS, 0, gx - 1).wait_recv()

    @pl.when(has_right)
    def _():
        side_copy(0, gy + 1).wait_send()
        side_copy(1, gy + 1).wait_recv()

    @pl.when(has_left)
    def _():
        side_copy(1, gy - 1).wait_send()
        side_copy(0, gy - 1).wait_recv()

    whole.wait_send()
    whole.wait_recv()
    in_ref[...] = land[...]
    low_ref[...] = halo[0]
    high_ref[...] = halo[1]
    low_rows_ref[...] = sides[0]
    high_rows_ref[...] = sides[1]


def exchange(current, edges, outgoing, owners, rows_of, columns):
    halo_shape = jax.ShapeDtypeStruct((3, HALO_ROWS, CY), jnp.float32)
    side_shape = jax.ShapeDtypeStruct(edges.shape, jnp.float32)
    return pl.pallas_call(
        functools.partial(exchange_kernel, (owners, rows_of, columns)),
        out_shape=(jax.ShapeDtypeStruct(outgoing.shape, jnp.float32), halo_shape, halo_shape, side_shape, side_shape),
        in_specs=[pl.BlockSpec(memory_space=pl.ANY)] * 2 + [pl.BlockSpec(memory_space=pltpu.VMEM)],
        out_specs=tuple(vmem_specs(5)),
        scratch_shapes=[
            pltpu.VMEM(outgoing.shape, jnp.float32),
            pltpu.VMEM((2, 3, HALO_ROWS, CY), jnp.float32),
            pltpu.VMEM((2,) + edges.shape, jnp.float32),
            pltpu.SemaphoreType.DMA(()),
            pltpu.SemaphoreType.DMA(()),
            pltpu.SemaphoreType.DMA((2,)),
            pltpu.SemaphoreType.DMA((2,)),
            pltpu.SemaphoreType.DMA((2,)),
            pltpu.SemaphoreType.DMA((2,)),
        ],
        compiler_params=pltpu.CompilerParams(collective_id=0, has_side_effects=True),
    )(current, edges, outgoing)


def route(payload):
    tile_data, tile_rows = payload
    width = tile_data.shape[-1]
    received_data, received_rows = (
        lax.all_to_all(tile_data, ("gx", "gy"), split_axis=0, concat_axis=0, tiled=True),
        lax.all_to_all(tile_rows, ("gx", "gy"), split_axis=0, concat_axis=0, tiled=True),
    )
    return (received_data.reshape(-1, width), received_rows.reshape(-1))


def deliver(outgoing, send_rows):
    routed = route((outgoing, send_rows))
    return from_partner((routed[0], routed[1]), "sec", 0)


def on_device(state, previous, coeff, wet_mask, link_dest, link_rows, link_weight):
    section = lax.axis_index("sec")
    owners = lax.axis_size("gx") * lax.axis_size("gy")
    fine_rows = REFINE * CX
    fine_cols = REFINE * CY
    current = state[0, :, 0, 0].reshape(3, ROWS, CY)
    earlier = previous[0, :, 0, 0].reshape(3, ROWS, CY)
    factors = coeff[0, :, 0, 0].reshape(2, ROWS, CY)
    wet = wet_mask[0, 0].reshape(ROWS, CY)
    targets = link_dest.reshape(-1)
    pairs = link_rows.reshape(-1, 2)
    source_rows = pairs[:, 0]
    landing = pairs[:, 1]
    weights = link_weight.reshape(-1)
    one_hot = (targets[:, None] == jnp.arange(owners, dtype=jnp.int32)[None, :]).astype(jnp.int32)
    before = jnp.cumsum(one_hot, axis=0) - one_hot
    slot_index = jnp.sum(before * one_hot, axis=1)
    position = targets * CAP + slot_index
    send_rows = jnp.zeros((owners * CAP,), jnp.int32).at[position].set(landing).reshape(owners, CAP)
    slot_rows = jnp.full((owners * CAP,), -1, jnp.int32).at[position].set(source_rows)
    slot_weights = jnp.zeros((owners * CAP,), jnp.float32).at[position].set(weights)
    pick = jnp.where(slot_rows[:, None] == jnp.arange(fine_rows, dtype=jnp.int32)[None, :], slot_weights[:, None], 0.0)

    def elastic_rows():
        return current[2].reshape(CX, NL, CY)[:, 0, :][source_rows]

    def shallow_rows():
        picked_fine = current[0].reshape(fine_rows, fine_cols)[source_rows]
        return jnp.sum(picked_fine.reshape(-1, CY, REFINE), axis=-1) / REFINE

    picked = lax.cond(section == 0, elastic_rows, shallow_rows)
    outgoing = jnp.zeros((owners * CAP, CY), jnp.float32).at[position].set(picked * weights[:, None])
    arrived_rows = deliver(jnp.zeros((owners, CAP, CY), jnp.float32), send_rows)[1].reshape(1, -1)
    edges = jnp.stack([current[:, :, CY - 1], current[:, :, 0]], axis=1)
    edges = jnp.pad(edges, ((0, 0), (0, 8 - 2), (0, EDGE_LANES - ROWS)))
    for step_index in range(STEPS):
        arrived, low_x, high_x, low_y, high_y = exchange(
            current, edges, outgoing, owners, lax.axis_size("gx"), lax.axis_size("gy")
        )

        def elastic_branch():
            scratch = [
                pltpu.VMEM((3, PAD_ROWS, CY), jnp.float32),
                pltpu.VMEM((3, ROWS + 2 * EDGE, 1), jnp.float32),
                pltpu.VMEM((3, ROWS + 2 * EDGE, 1), jnp.float32),
            ]
            return run_step(elastic_kernel, scratch, current, earlier, factors, low_x, high_x, low_y, high_y,
                            arrived_rows, arrived, pick)

        def shallow_branch():
            scratch = [
                pltpu.VMEM((3, PAD_ROWS, CY), jnp.float32),
                pltpu.VMEM((ROWS, CY), jnp.float32),
                pltpu.VMEM((3, ROWS + 2 * EDGE, 1), jnp.float32),
                pltpu.VMEM((3, ROWS + 2 * EDGE, 1), jnp.float32),
            ]
            return run_step(shallow_kernel, scratch, current, earlier, factors, wet, low_x, high_x, low_y, high_y,
                            arrived_rows, arrived, pick)

        updated, outgoing, edges = lax.cond(section == 0, elastic_branch, shallow_branch)
        earlier, current = (current, updated)
    return current.reshape(1, 3, 1, 1, -1)


def solution(mesh):
    placed = (
        P("sec", None, "gx", "gy", None),
        P("sec", None, "gx", "gy", None),
        P("sec", None, "gx", "gy", None),
        P("gx", "gy", None),
        P("sec", "gx", "gy", None, None),
        P("sec", "gx", "gy", None, None),
        P("sec", "gx", "gy", None),
    )
    return jax.shard_map(
        on_device,
        mesh=mesh,
        in_specs=placed,
        out_specs=P("sec", None, "gx", "gy", None),
        check_vma=False,
    )
```

```python
import functools

import jax
import jax.numpy as jnp
from jax import lax
from jax.experimental import pallas as pl
from jax.experimental.pallas import tpu as pltpu
from jax.sharding import PartitionSpec as P

CX = 8
CY = 128
REFINE = 10
NL = 100
STEPS = 4
CAP = 4

ROWS = CX * NL
BASE = 104
PAD_ROWS = BASE + ROWS + BASE
CHUNK = 40
EDGE = 16
HALO_ROWS = NL + 4
EDGE_LANES = 896


def from_partner(value, axis, stride):
    return lax.ppermute(value, axis, [(i, i ^ 1 << stride) for i in range(lax.axis_size(axis))])


def shift_pairs(axis):
    count = lax.axis_size(axis)
    forward = [(i, i + 1) for i in range(count - 1)]
    backward = [(target, source) for source, target in forward]
    return forward, backward


def fill_scratch(scratch, cur_ref, low_ref, high_ref, fields):
    for f in range(fields):
        scratch[f, pl.ds(BASE - HALO_ROWS, HALO_ROWS), :] = low_ref[f]
        scratch[f, pl.ds(BASE, ROWS), :] = cur_ref[f]
        scratch[f, pl.ds(BASE + ROWS, HALO_ROWS), :] = high_ref[f]


def lane_index(rows):
    return lax.broadcasted_iota(jnp.int32, (rows, CY), 1)


def row_mask(r0, rows, period, phase):
    local = lax.broadcasted_iota(jnp.int32, (rows, CY), 0)
    mask = jnp.zeros((rows, CY), jnp.bool_)
    for r in range(rows):
        if (r0 + r) % period == phase:
            mask = mask | (local == r)
    return mask


def exact_dot(a, b):
    return jnp.dot(a, b, precision=lax.Precision.HIGHEST, preferred_element_type=jnp.float32)


def landing_sum(rows_ref, arrived_ref, count):
    slots = rows_ref.shape[1]
    one_hot = (lax.broadcasted_iota(jnp.int32, (count, slots), 0) == rows_ref[...]).astype(jnp.float32)
    return exact_dot(one_hot, arrived_ref[...])


def edge_rows(out_ref, edges_ref):
    rows = lax.broadcasted_iota(jnp.int32, (8, CY), 0)
    lanes = lax.broadcasted_iota(jnp.int32, (8, CY), 1)
    select = (((rows == 0) & (lanes == CY - 1)) | ((rows == 1) & (lanes == 0))).astype(jnp.float32)
    for f in range(3):
        picked = lax.dot_general(select, out_ref[f], (((1,), (1,)), ((), ())), precision=lax.Precision.HIGHEST,
                                 preferred_element_type=jnp.float32)
        edges_ref[f] = jnp.zeros(edges_ref.shape[1:], jnp.float32)
        edges_ref[f, :, pl.ds(0, ROWS)] = picked


def fill_sides(low_rows_ref, high_rows_ref, left_pad, right_pad):
    for f in range(3):
        left_pad[f, pl.ds(EDGE, ROWS), :] = jnp.transpose(low_rows_ref[f])[:ROWS, 0:1]
        right_pad[f, pl.ds(EDGE, ROWS), :] = jnp.transpose(high_rows_ref[f])[:ROWS, 1:2]


def spread(cb):
    coarse = lax.broadcasted_iota(jnp.int32, (CY, CY), 0)
    fine = lax.broadcasted_iota(jnp.int32, (CY, CY), 1) + cb * CY
    return ((fine >= coarse * REFINE) & (fine < coarse * REFINE + REFINE)).astype(jnp.float32)


def elastic_kernel(cur_ref, prev_ref, coef_ref, low_ref, high_ref, low_rows_ref, high_rows_ref, rows_ref, arrived_ref,
                   pick_ref, out_ref, tiles_ref, edges_ref, scratch, left_pad, right_pad):
    fill_scratch(scratch, cur_ref, low_ref, high_ref, 3)
    fill_sides(low_rows_ref, high_rows_ref, left_pad, right_pad)
    force = landing_sum(rows_ref, arrived_ref, CX)
    lanes = lane_index(CHUNK)
    first_lane = lanes == 0
    last_lane = lanes == CY - 1
    own_axis = (0, 2, 1)
    for r0 in range(0, ROWS, CHUNK):
        top_layer = row_mask(r0, CHUNK, NL, 0)
        bottom_layer = row_mask(r0, CHUNK, NL, NL - 1)
        shear = coef_ref[0, pl.ds(r0, CHUNK), :]
        lame = coef_ref[1, pl.ds(r0, CHUNK), :]
        stiffness = lame + 2.0 * shear
        for c in range(3):
            at = BASE + r0
            v = scratch[c, pl.ds(at, CHUNK), :]
            along_first = scratch[c, pl.ds(at + NL, CHUNK), :] - 2.0 * v + scratch[c, pl.ds(at - NL, CHUNK), :]
            deeper = jnp.where(bottom_layer, 0.0, scratch[c, pl.ds(at + 1, CHUNK), :])
            shallower = jnp.where(top_layer, 0.0, scratch[c, pl.ds(at - 1, CHUNK), :])
            along_depth = deeper - 2.0 * v + shallower
            after = jnp.where(last_lane, right_pad[c, pl.ds(EDGE + r0, CHUNK), :], pltpu.roll(v, CY - 1, 1))
            before = jnp.where(first_lane, left_pad[c, pl.ds(EDGE + r0, CHUNK), :], pltpu.roll(v, 1, 1))
            along_second = after - 2.0 * v + before
            factors = [stiffness if own_axis[c] == axis_index else shear for axis_index in range(3)]
            acceleration = factors[0] * along_first + factors[1] * along_depth + factors[2] * along_second
            out_ref[c, pl.ds(r0, CHUNK), :] = 2.0 * v - prev_ref[c, pl.ds(r0, CHUNK), :] + acceleration
    for x in range(CX):
        out_ref[2, pl.ds(x * NL, 1), :] = out_ref[2, pl.ds(x * NL, 1), :] + force[x : x + 1]
    elastic_tiles(out_ref, pick_ref, tiles_ref)
    edge_rows(out_ref, edges_ref)


def shallow_kernel(cur_ref, prev_ref, coef_ref, wet_ref, low_ref, high_ref, low_rows_ref, high_rows_ref, rows_ref,
                   arrived_ref, pick_ref, out_ref, tiles_ref, edges_ref, scratch, source_ref, left_pad, right_pad):
    fill_scratch(scratch, cur_ref, low_ref, high_ref, 3)
    fill_sides(low_rows_ref, high_rows_ref, left_pad, right_pad)
    coarse_source = landing_sum(rows_ref, arrived_ref, REFINE * CX)
    for cb in range(REFINE):
        source_ref[pl.ds(cb, REFINE * CX, stride=REFINE), :] = exact_dot(coarse_source, spread(cb))
    lanes = lane_index(CHUNK)
    first_lane = lanes == 0
    last_lane = lanes == CY - 1
    first_block = row_mask(0, CHUNK, REFINE, 0)
    last_block = row_mask(0, CHUNK, REFINE, REFINE - 1)
    for r0 in range(0, ROWS, CHUNK):
        at = BASE + r0

        def rows_diff(f):
            return scratch[f, pl.ds(at + REFINE, CHUNK), :] - scratch[f, pl.ds(at - REFINE, CHUNK), :]

        def columns_diff(f):
            v = scratch[f, pl.ds(at, CHUNK), :]
            wrap_after = jnp.where(last_block, right_pad[f, pl.ds(EDGE + r0 - (REFINE - 1), CHUNK), :],
                                   pltpu.roll(scratch[f, pl.ds(at + 1, CHUNK), :], CY - 1, 1))
            wrap_before = jnp.where(first_block, left_pad[f, pl.ds(EDGE + r0 + REFINE - 1, CHUNK), :],
                                    pltpu.roll(scratch[f, pl.ds(at - 1, CHUNK), :], 1, 1))
            after = jnp.where(last_lane, wrap_after, pltpu.roll(v, CY - 1, 1))
            before = jnp.where(first_lane, wrap_before, pltpu.roll(v, 1, 1))
            return after - before

        wave = coef_ref[0, pl.ds(r0, CHUNK), :]
        area = coef_ref[1, pl.ds(r0, CHUNK), :]
        wet = wet_ref[pl.ds(r0, CHUNK), :].astype(jnp.float32)
        eta_r = rows_diff(0)
        eta_c = columns_diff(0)
        out_ref[1, pl.ds(r0, CHUNK), :] = wet * (prev_ref[1, pl.ds(r0, CHUNK), :] - wave * eta_r)
        out_ref[2, pl.ds(r0, CHUNK), :] = wet * (prev_ref[2, pl.ds(r0, CHUNK), :] - wave * eta_c)
        divergence = rows_diff(1) + columns_diff(2)
        out_ref[0, pl.ds(r0, CHUNK), :] = wet * (
            prev_ref[0, pl.ds(r0, CHUNK), :] - area * divergence + source_ref[pl.ds(r0, CHUNK), :]
        )
    shallow_tiles(out_ref, pick_ref, tiles_ref)
    edge_rows(out_ref, edges_ref)


def shallow_tiles(field_ref, pick_ref, tiles_ref):
    total = jnp.zeros((REFINE * CX, CY), jnp.float32)
    for cb in range(REFINE):
        total = total + exact_dot(field_ref[0, pl.ds(cb, REFINE * CX, stride=REFINE), :], spread(cb).T)
    tiles_ref[...] = exact_dot(pick_ref[...], total / REFINE)


def elastic_tiles(field_ref, pick_ref, tiles_ref):
    uplift = field_ref[2, pl.ds(0, CX, stride=NL), :]
    tiles_ref[...] = exact_dot(pick_ref[:, :CX], uplift)


def prepare_kernel(tiles_of, cur_ref, pick_ref, tiles_ref, edges_ref):
    tiles_of(cur_ref, pick_ref, tiles_ref)
    edge_rows(cur_ref, edges_ref)


def prepare(tiles_of, current, pick):
    return pl.pallas_call(
        functools.partial(prepare_kernel, tiles_of),
        out_shape=(
            jax.ShapeDtypeStruct((pick.shape[0], CY), jnp.float32),
            jax.ShapeDtypeStruct((3, 8, EDGE_LANES), jnp.float32),
        ),
        in_specs=vmem_specs(2),
        out_specs=tuple(vmem_specs(2)),
    )(current, pick)


def vmem_specs(count):
    return [pl.BlockSpec(memory_space=pltpu.VMEM)] * count


def run_step(kernel, scratch_shapes, *operands):
    slots = operands[-1].shape[0]
    return pl.pallas_call(
        kernel,
        out_shape=(
            jax.ShapeDtypeStruct((3, ROWS, CY), jnp.float32),
            jax.ShapeDtypeStruct((slots, CY), jnp.float32),
            jax.ShapeDtypeStruct((3, 8, EDGE_LANES), jnp.float32),
        ),
        in_specs=vmem_specs(len(operands)),
        out_specs=tuple(vmem_specs(3)),
        scratch_shapes=scratch_shapes,
    )(*operands)


def exchange_kernel(sizes, cur_ref, edges_ref, out_ref, in_ref, low_ref, high_ref, low_rows_ref, high_rows_ref,
                    land, halo, sides, send_sem, recv_sem, halo_send, halo_recv, side_send, side_recv):
    owners, rows_of, columns = sizes
    other = 1 - lax.axis_index("sec")
    section = lax.axis_index("sec")
    gx = lax.axis_index("gx")
    gy = lax.axis_index("gy")
    me = gx * columns + gy
    has_low = gx > 0
    has_high = gx < rows_of - 1
    has_left = gy > 0
    has_right = gy < columns - 1
    halo[...] = jnp.zeros_like(halo)
    sides[...] = jnp.zeros_like(sides)
    barrier = pltpu.get_barrier_semaphore()
    def greet(d, carry):
        pl.semaphore_signal(barrier, inc=1, device_id=(other, d // columns, d % columns),
                            device_id_type=pl.DeviceIdType.MESH)
        return carry

    lax.fori_loop(0, owners, greet, 0, unroll=8)

    @pl.when(has_low)
    def _():
        pl.semaphore_signal(barrier, inc=1, device_id=(section, gx - 1, gy), device_id_type=pl.DeviceIdType.MESH)

    @pl.when(has_high)
    def _():
        pl.semaphore_signal(barrier, inc=1, device_id=(section, gx + 1, gy), device_id_type=pl.DeviceIdType.MESH)

    @pl.when(has_left)
    def _():
        pl.semaphore_signal(barrier, inc=1, device_id=(section, gx, gy - 1), device_id_type=pl.DeviceIdType.MESH)

    @pl.when(has_right)
    def _():
        pl.semaphore_signal(barrier, inc=1, device_id=(section, gx, gy + 1), device_id_type=pl.DeviceIdType.MESH)

    neighbours = [has_low, has_high, has_left, has_right]
    pl.semaphore_wait(barrier, owners + sum(n.astype(jnp.int32) for n in neighbours))

    def side_copy(slot, target):
        return pltpu.make_async_remote_copy(
            src_ref=edges_ref,
            dst_ref=sides.at[slot],
            send_sem=side_send.at[slot],
            recv_sem=side_recv.at[slot],
            device_id=(section, gx, target),
            device_id_type=pl.DeviceIdType.MESH,
        )

    @pl.when(has_right)
    def _():
        side_copy(0, gy + 1).start()

    @pl.when(has_left)
    def _():
        side_copy(1, gy - 1).start()

    def slab_copy(start, slot, target):
        return pltpu.make_async_remote_copy(
            src_ref=cur_ref.at[:, pl.ds(start, HALO_ROWS), :],
            dst_ref=halo.at[slot],
            send_sem=halo_send.at[slot],
            recv_sem=halo_recv.at[slot],
            device_id=(section, target, gy),
            device_id_type=pl.DeviceIdType.MESH,
        )

    @pl.when(has_high)
    def _():
        slab_copy(ROWS - HALO_ROWS, 0, gx + 1).start()

    @pl.when(has_low)
    def _():
        slab_copy(0, 1, gx - 1).start()

    def send(d, carry):
        pltpu.make_async_remote_copy(
            src_ref=out_ref.at[pl.ds(d * CAP, CAP)],
            dst_ref=land.at[pl.ds(me * CAP, CAP)],
            send_sem=send_sem,
            recv_sem=recv_sem,
            device_id=(other, d // columns, d % columns),
            device_id_type=pl.DeviceIdType.MESH,
        ).start()
        return carry

    lax.fori_loop(0, owners, send, 0, unroll=8)
    whole = pltpu.make_async_remote_copy(
        src_ref=out_ref,
        dst_ref=land,
        send_sem=send_sem,
        recv_sem=recv_sem,
        device_id=(other, gx, gy),
        device_id_type=pl.DeviceIdType.MESH,
    )

    @pl.when(has_high)
    def _():
        slab_copy(ROWS - HALO_ROWS, 0, gx + 1).wait_send()
        slab_copy(0, 1, gx + 1).wait_recv()

    @pl.when(has_low)
    def _():
        slab_copy(0, 1, gx - 1).wait_send()
        slab_copy(ROWS - HALO_ROWS, 0, gx - 1).wait_recv()

    @pl.when(has_right)
    def _():
        side_copy(0, gy + 1).wait_send()
        side_copy(1, gy + 1).wait_recv()

    @pl.when(has_left)
    def _():
        side_copy(1, gy - 1).wait_send()
        side_copy(0, gy - 1).wait_recv()

    whole.wait_send()
    whole.wait_recv()
    in_ref[...] = land[...]
    low_ref[...] = halo[0]
    high_ref[...] = halo[1]
    low_rows_ref[...] = sides[0]
    high_rows_ref[...] = sides[1]


def exchange(current, edges, outgoing, owners, rows_of, columns):
    halo_shape = jax.ShapeDtypeStruct((3, HALO_ROWS, CY), jnp.float32)
    side_shape = jax.ShapeDtypeStruct(edges.shape, jnp.float32)
    return pl.pallas_call(
        functools.partial(exchange_kernel, (owners, rows_of, columns)),
        out_shape=(jax.ShapeDtypeStruct(outgoing.shape, jnp.float32), halo_shape, halo_shape, side_shape, side_shape),
        in_specs=[pl.BlockSpec(memory_space=pl.ANY)] * 2 + [pl.BlockSpec(memory_space=pltpu.VMEM)],
        out_specs=tuple(vmem_specs(5)),
        scratch_shapes=[
            pltpu.VMEM(outgoing.shape, jnp.float32),
            pltpu.VMEM((2, 3, HALO_ROWS, CY), jnp.float32),
            pltpu.VMEM((2,) + edges.shape, jnp.float32),
            pltpu.SemaphoreType.DMA(()),
            pltpu.SemaphoreType.DMA(()),
            pltpu.SemaphoreType.DMA((2,)),
            pltpu.SemaphoreType.DMA((2,)),
            pltpu.SemaphoreType.DMA((2,)),
            pltpu.SemaphoreType.DMA((2,)),
        ],
        compiler_params=pltpu.CompilerParams(collective_id=0, has_side_effects=True),
    )(current, edges, outgoing)


def route(payload):
    tile_data, tile_rows = payload
    width = tile_data.shape[-1]
    received_data, received_rows = (
        lax.all_to_all(tile_data, ("gx", "gy"), split_axis=0, concat_axis=0, tiled=True),
        lax.all_to_all(tile_rows, ("gx", "gy"), split_axis=0, concat_axis=0, tiled=True),
    )
    return (received_data.reshape(-1, width), received_rows.reshape(-1))


def deliver(outgoing, send_rows):
    routed = route((outgoing, send_rows))
    return from_partner((routed[0], routed[1]), "sec", 0)


def on_device(state, previous, coeff, wet_mask, link_dest, link_rows, link_weight):
    section = lax.axis_index("sec")
    owners = lax.axis_size("gx") * lax.axis_size("gy")
    fine_rows = REFINE * CX
    current = state[0, :, 0, 0].reshape(3, ROWS, CY)
    earlier = previous[0, :, 0, 0].reshape(3, ROWS, CY)
    factors = coeff[0, :, 0, 0].reshape(2, ROWS, CY)
    wet = wet_mask[0, 0].reshape(ROWS, CY)
    targets = link_dest.reshape(-1)
    pairs = link_rows.reshape(-1, 2)
    source_rows = pairs[:, 0]
    landing = pairs[:, 1]
    weights = link_weight.reshape(-1)
    one_hot = (targets[:, None] == jnp.arange(owners, dtype=jnp.int32)[None, :]).astype(jnp.int32)
    before = jnp.cumsum(one_hot, axis=0) - one_hot
    slot_index = jnp.sum(before * one_hot, axis=1)
    position = targets * CAP + slot_index
    send_rows = jnp.zeros((owners * CAP,), jnp.int32).at[position].set(landing).reshape(owners, CAP)
    slot_rows = jnp.full((owners * CAP,), -1, jnp.int32).at[position].set(source_rows)
    slot_weights = jnp.zeros((owners * CAP,), jnp.float32).at[position].set(weights)
    pick = jnp.where(slot_rows[:, None] == jnp.arange(fine_rows, dtype=jnp.int32)[None, :], slot_weights[:, None], 0.0)
    arrived_rows = deliver(jnp.zeros((owners, CAP, CY), jnp.float32), send_rows)[1].reshape(1, -1)
    outgoing, edges = lax.cond(
        section == 0,
        lambda: prepare(elastic_tiles, current, pick),
        lambda: prepare(shallow_tiles, current, pick),
    )
    for step_index in range(STEPS):
        arrived, low_x, high_x, low_y, high_y = exchange(
            current, edges, outgoing, owners, lax.axis_size("gx"), lax.axis_size("gy")
        )

        def elastic_branch():
            scratch = [
                pltpu.VMEM((3, PAD_ROWS, CY), jnp.float32),
                pltpu.VMEM((3, ROWS + 2 * EDGE, 1), jnp.float32),
                pltpu.VMEM((3, ROWS + 2 * EDGE, 1), jnp.float32),
            ]
            return run_step(elastic_kernel, scratch, current, earlier, factors, low_x, high_x, low_y, high_y,
                            arrived_rows, arrived, pick)

        def shallow_branch():
            scratch = [
                pltpu.VMEM((3, PAD_ROWS, CY), jnp.float32),
                pltpu.VMEM((ROWS, CY), jnp.float32),
                pltpu.VMEM((3, ROWS + 2 * EDGE, 1), jnp.float32),
                pltpu.VMEM((3, ROWS + 2 * EDGE, 1), jnp.float32),
            ]
            return run_step(shallow_kernel, scratch, current, earlier, factors, wet, low_x, high_x, low_y, high_y,
                            arrived_rows, arrived, pick)

        updated, outgoing, edges = lax.cond(section == 0, elastic_branch, shallow_branch)
        earlier, current = (current, updated)
    return current.reshape(1, 3, 1, 1, -1)


def solution(mesh):
    placed = (
        P("sec", None, "gx", "gy", None),
        P("sec", None, "gx", "gy", None),
        P("sec", None, "gx", "gy", None),
        P("gx", "gy", None),
        P("sec", "gx", "gy", None, None),
        P("sec", "gx", "gy", None, None),
        P("sec", "gx", "gy", None),
    )
    return jax.shard_map(
        on_device,
        mesh=mesh,
        in_specs=placed,
        out_specs=P("sec", None, "gx", "gy", None),
        check_vma=False,
    )
```

```python
import functools

import jax
import jax.numpy as jnp
from jax import lax
from jax.experimental import pallas as pl
from jax.experimental.pallas import tpu as pltpu
from jax.sharding import PartitionSpec as P

CX = 8
CY = 128
REFINE = 10
NL = 100
STEPS = 4
CAP = 4

ROWS = CX * NL
BASE = 104
PAD_ROWS = BASE + ROWS + BASE
CHUNK = 40
EDGE = 16
HALO_ROWS = NL + 4
EDGE_LANES = 896


def from_partner(value, axis, stride):
    return lax.ppermute(value, axis, [(i, i ^ 1 << stride) for i in range(lax.axis_size(axis))])


def shift_pairs(axis):
    count = lax.axis_size(axis)
    forward = [(i, i + 1) for i in range(count - 1)]
    backward = [(target, source) for source, target in forward]
    return forward, backward


def fill_scratch(scratch, cur_ref, low_ref, high_ref, fields):
    for f in range(fields):
        scratch[f, pl.ds(BASE - HALO_ROWS, HALO_ROWS), :] = low_ref[f]
        scratch[f, pl.ds(BASE, ROWS), :] = cur_ref[f]
        scratch[f, pl.ds(BASE + ROWS, HALO_ROWS), :] = high_ref[f]


def lane_index(rows):
    return lax.broadcasted_iota(jnp.int32, (rows, CY), 1)


def row_mask(r0, rows, period, phase):
    local = lax.broadcasted_iota(jnp.int32, (rows, CY), 0)
    mask = jnp.zeros((rows, CY), jnp.bool_)
    for r in range(rows):
        if (r0 + r) % period == phase:
            mask = mask | (local == r)
    return mask


def exact_dot(a, b):
    return jnp.dot(a, b, precision=lax.Precision.HIGHEST, preferred_element_type=jnp.float32)


def landing_sum(rows_ref, arrived_ref, count):
    slots = rows_ref.shape[1]
    one_hot = (lax.broadcasted_iota(jnp.int32, (count, slots), 0) == rows_ref[...]).astype(jnp.float32)
    return exact_dot(one_hot, arrived_ref[...])


def edge_rows(out_ref, edges_ref):
    rows = lax.broadcasted_iota(jnp.int32, (8, CY), 0)
    lanes = lax.broadcasted_iota(jnp.int32, (8, CY), 1)
    select = (((rows == 0) & (lanes == CY - 1)) | ((rows == 1) & (lanes == 0))).astype(jnp.float32)
    for f in range(3):
        picked = lax.dot_general(select, out_ref[f], (((1,), (1,)), ((), ())), precision=lax.Precision.HIGHEST,
                                 preferred_element_type=jnp.float32)
        edges_ref[f] = jnp.zeros(edges_ref.shape[1:], jnp.float32)
        edges_ref[f, :, pl.ds(0, ROWS)] = picked


def fill_sides(low_rows_ref, high_rows_ref, left_pad, right_pad):
    for f in range(3):
        left_pad[f, pl.ds(EDGE, ROWS), :] = jnp.transpose(low_rows_ref[f])[:ROWS, 0:1]
        right_pad[f, pl.ds(EDGE, ROWS), :] = jnp.transpose(high_rows_ref[f])[:ROWS, 1:2]


def spread(cb):
    coarse = lax.broadcasted_iota(jnp.int32, (CY, CY), 0)
    fine = lax.broadcasted_iota(jnp.int32, (CY, CY), 1) + cb * CY
    return ((fine >= coarse * REFINE) & (fine < coarse * REFINE + REFINE)).astype(jnp.float32)


def elastic_kernel(cur_ref, prev_ref, coef_ref, low_ref, high_ref, low_rows_ref, high_rows_ref, rows_ref, arrived_ref,
                   pick_ref, out_ref, tiles_ref, edges_ref, scratch, left_pad, right_pad):
    fill_scratch(scratch, cur_ref, low_ref, high_ref, 3)
    fill_sides(low_rows_ref, high_rows_ref, left_pad, right_pad)
    force = landing_sum(rows_ref, arrived_ref, CX)
    lanes = lane_index(CHUNK)
    first_lane = lanes == 0
    last_lane = lanes == CY - 1
    own_axis = (0, 2, 1)
    for r0 in range(0, ROWS, CHUNK):
        top_layer = row_mask(r0, CHUNK, NL, 0)
        bottom_layer = row_mask(r0, CHUNK, NL, NL - 1)
        shear = coef_ref[0, pl.ds(r0, CHUNK), :]
        lame = coef_ref[1, pl.ds(r0, CHUNK), :]
        stiffness = lame + 2.0 * shear
        for c in range(3):
            at = BASE + r0
            v = scratch[c, pl.ds(at, CHUNK), :]
            along_first = scratch[c, pl.ds(at + NL, CHUNK), :] - 2.0 * v + scratch[c, pl.ds(at - NL, CHUNK), :]
            deeper = jnp.where(bottom_layer, 0.0, scratch[c, pl.ds(at + 1, CHUNK), :])
            shallower = jnp.where(top_layer, 0.0, scratch[c, pl.ds(at - 1, CHUNK), :])
            along_depth = deeper - 2.0 * v + shallower
            after = jnp.where(last_lane, right_pad[c, pl.ds(EDGE + r0, CHUNK), :], pltpu.roll(v, CY - 1, 1))
            before = jnp.where(first_lane, left_pad[c, pl.ds(EDGE + r0, CHUNK), :], pltpu.roll(v, 1, 1))
            along_second = after - 2.0 * v + before
            factors = [stiffness if own_axis[c] == axis_index else shear for axis_index in range(3)]
            acceleration = factors[0] * along_first + factors[1] * along_depth + factors[2] * along_second
            out_ref[c, pl.ds(r0, CHUNK), :] = 2.0 * v - prev_ref[c, pl.ds(r0, CHUNK), :] + acceleration
    for x in range(CX):
        out_ref[2, pl.ds(x * NL, 1), :] = out_ref[2, pl.ds(x * NL, 1), :] + force[x : x + 1]
    elastic_tiles(out_ref, pick_ref, tiles_ref)
    edge_rows(out_ref, edges_ref)


def shallow_kernel(cur_ref, prev_ref, coef_ref, wet_ref, low_ref, high_ref, low_rows_ref, high_rows_ref, rows_ref,
                   arrived_ref, pick_ref, out_ref, tiles_ref, edges_ref, scratch, source_ref, left_pad, right_pad):
    fill_scratch(scratch, cur_ref, low_ref, high_ref, 3)
    fill_sides(low_rows_ref, high_rows_ref, left_pad, right_pad)
    coarse_source = landing_sum(rows_ref, arrived_ref, REFINE * CX)
    for cb in range(REFINE):
        source_ref[pl.ds(cb, REFINE * CX, stride=REFINE), :] = exact_dot(coarse_source, spread(cb))
    lanes = lane_index(CHUNK)
    first_lane = lanes == 0
    last_lane = lanes == CY - 1
    first_block = row_mask(0, CHUNK, REFINE, 0)
    last_block = row_mask(0, CHUNK, REFINE, REFINE - 1)
    for r0 in range(0, ROWS, CHUNK):
        at = BASE + r0

        def rows_diff(f):
            return scratch[f, pl.ds(at + REFINE, CHUNK), :] - scratch[f, pl.ds(at - REFINE, CHUNK), :]

        def columns_diff(f):
            v = scratch[f, pl.ds(at, CHUNK), :]
            wrap_after = jnp.where(last_block, right_pad[f, pl.ds(EDGE + r0 - (REFINE - 1), CHUNK), :],
                                   pltpu.roll(scratch[f, pl.ds(at + 1, CHUNK), :], CY - 1, 1))
            wrap_before = jnp.where(first_block, left_pad[f, pl.ds(EDGE + r0 + REFINE - 1, CHUNK), :],
                                    pltpu.roll(scratch[f, pl.ds(at - 1, CHUNK), :], 1, 1))
            after = jnp.where(last_lane, wrap_after, pltpu.roll(v, CY - 1, 1))
            before = jnp.where(first_lane, wrap_before, pltpu.roll(v, 1, 1))
            return after - before

        wave = coef_ref[0, pl.ds(r0, CHUNK), :]
        area = coef_ref[1, pl.ds(r0, CHUNK), :]
        wet = wet_ref[pl.ds(r0, CHUNK), :].astype(jnp.float32)
        eta_r = rows_diff(0)
        eta_c = columns_diff(0)
        out_ref[1, pl.ds(r0, CHUNK), :] = wet * (prev_ref[1, pl.ds(r0, CHUNK), :] - wave * eta_r)
        out_ref[2, pl.ds(r0, CHUNK), :] = wet * (prev_ref[2, pl.ds(r0, CHUNK), :] - wave * eta_c)
        divergence = rows_diff(1) + columns_diff(2)
        out_ref[0, pl.ds(r0, CHUNK), :] = wet * (
            prev_ref[0, pl.ds(r0, CHUNK), :] - area * divergence + source_ref[pl.ds(r0, CHUNK), :]
        )
    shallow_tiles(out_ref, pick_ref, tiles_ref)
    edge_rows(out_ref, edges_ref)


def shallow_tiles(field_ref, pick_ref, tiles_ref):
    total = jnp.zeros((REFINE * CX, CY), jnp.float32)
    for cb in range(REFINE):
        total = total + exact_dot(field_ref[0, pl.ds(cb, REFINE * CX, stride=REFINE), :], spread(cb).T)
    tiles_ref[...] = exact_dot(pick_ref[...], total / REFINE)


def elastic_tiles(field_ref, pick_ref, tiles_ref):
    uplift = field_ref[2, pl.ds(0, CX, stride=NL), :]
    tiles_ref[...] = exact_dot(pick_ref[:, :CX], uplift)


def prepare_kernel(tiles_of, cur_ref, pick_ref, tiles_ref, edges_ref):
    tiles_of(cur_ref, pick_ref, tiles_ref)
    edge_rows(cur_ref, edges_ref)


def prepare(tiles_of, current, pick):
    return pl.pallas_call(
        functools.partial(prepare_kernel, tiles_of),
        out_shape=(
            jax.ShapeDtypeStruct((pick.shape[0], CY), jnp.float32),
            jax.ShapeDtypeStruct((3, 8, EDGE_LANES), jnp.float32),
        ),
        in_specs=vmem_specs(2),
        out_specs=tuple(vmem_specs(2)),
    )(current, pick)


def vmem_specs(count):
    return [pl.BlockSpec(memory_space=pltpu.VMEM)] * count


def run_step(kernel, scratch_shapes, *operands):
    slots = operands[-1].shape[0]
    return pl.pallas_call(
        kernel,
        out_shape=(
            jax.ShapeDtypeStruct((3, ROWS, CY), jnp.float32),
            jax.ShapeDtypeStruct((slots, CY), jnp.float32),
            jax.ShapeDtypeStruct((3, 8, EDGE_LANES), jnp.float32),
        ),
        in_specs=vmem_specs(len(operands)),
        out_specs=tuple(vmem_specs(3)),
        scratch_shapes=scratch_shapes,
    )(*operands)


def exchange_kernel(sizes, cur_ref, edges_ref, out_ref, in_ref, low_ref, high_ref, low_rows_ref, high_rows_ref,
                    mid, land, halo, sides, first_send, first_recv, second_send, second_recv, own_sem,
                    halo_send, halo_recv, side_send, side_recv):
    rows_of, columns = sizes
    section = lax.axis_index("sec")
    other = 1 - section
    gx = lax.axis_index("gx")
    gy = lax.axis_index("gy")
    group = rows_of * CAP
    has_low = gx > 0
    has_high = gx < rows_of - 1
    has_left = gy > 0
    has_right = gy < columns - 1
    halo[...] = jnp.zeros_like(halo)
    sides[...] = jnp.zeros_like(sides)
    barrier = pltpu.get_barrier_semaphore()
    for j in range(columns):
        pl.semaphore_signal(barrier, inc=1, device_id=(other, gx, j), device_id_type=pl.DeviceIdType.MESH)
    for i in range(rows_of):
        @pl.when(gx != i)
        def _():
            pl.semaphore_signal(barrier, inc=1, device_id=(section, i, gy), device_id_type=pl.DeviceIdType.MESH)

    @pl.when(has_left)
    def _():
        pl.semaphore_signal(barrier, inc=1, device_id=(section, gx, gy - 1), device_id_type=pl.DeviceIdType.MESH)

    @pl.when(has_right)
    def _():
        pl.semaphore_signal(barrier, inc=1, device_id=(section, gx, gy + 1), device_id_type=pl.DeviceIdType.MESH)

    pl.semaphore_wait(barrier, columns + rows_of - 1 + has_left.astype(jnp.int32) + has_right.astype(jnp.int32))

    def slab_copy(start, slot, target):
        return pltpu.make_async_remote_copy(
            src_ref=cur_ref.at[:, pl.ds(start, HALO_ROWS), :],
            dst_ref=halo.at[slot],
            send_sem=halo_send.at[slot],
            recv_sem=halo_recv.at[slot],
            device_id=(section, target, gy),
            device_id_type=pl.DeviceIdType.MESH,
        )

    def side_copy(slot, target):
        return pltpu.make_async_remote_copy(
            src_ref=edges_ref,
            dst_ref=sides.at[slot],
            send_sem=side_send.at[slot],
            recv_sem=side_recv.at[slot],
            device_id=(section, gx, target),
            device_id_type=pl.DeviceIdType.MESH,
        )

    @pl.when(has_high)
    def _():
        slab_copy(ROWS - HALO_ROWS, 0, gx + 1).start()

    @pl.when(has_low)
    def _():
        slab_copy(0, 1, gx - 1).start()

    @pl.when(has_right)
    def _():
        side_copy(0, gy + 1).start()

    @pl.when(has_left)
    def _():
        side_copy(1, gy - 1).start()

    for j in range(columns):
        pltpu.make_async_remote_copy(
            src_ref=out_ref.at[pl.ds(j * group, group)],
            dst_ref=mid.at[gy],
            send_sem=first_send,
            recv_sem=first_recv,
            device_id=(other, gx, j),
            device_id_type=pl.DeviceIdType.MESH,
        ).start()
    first = pltpu.make_async_remote_copy(
        src_ref=mid, dst_ref=mid, send_sem=first_send, recv_sem=first_recv,
        device_id=(other, gx, gy), device_id_type=pl.DeviceIdType.MESH,
    )
    first.wait_recv()
    own = pltpu.make_async_copy(mid.at[:, pl.ds(gx * CAP, CAP)], land.at[gx], own_sem)
    own.start()
    for i in range(rows_of):
        @pl.when(gx != i)
        def _():
            pltpu.make_async_remote_copy(
                src_ref=mid.at[:, pl.ds(i * CAP, CAP)],
                dst_ref=land.at[gx],
                send_sem=second_send,
                recv_sem=second_recv,
                device_id=(section, i, gy),
                device_id_type=pl.DeviceIdType.MESH,
            ).start()
    first.wait_send()
    second = pltpu.make_async_remote_copy(
        src_ref=land.at[pl.ds(0, rows_of - 1)], dst_ref=land.at[pl.ds(0, rows_of - 1)],
        send_sem=second_send, recv_sem=second_recv,
        device_id=(section, gx, gy), device_id_type=pl.DeviceIdType.MESH,
    )

    @pl.when(has_high)
    def _():
        slab_copy(ROWS - HALO_ROWS, 0, gx + 1).wait_send()
        slab_copy(0, 1, gx + 1).wait_recv()

    @pl.when(has_low)
    def _():
        slab_copy(0, 1, gx - 1).wait_send()
        slab_copy(ROWS - HALO_ROWS, 0, gx - 1).wait_recv()

    @pl.when(has_right)
    def _():
        side_copy(0, gy + 1).wait_send()
        side_copy(1, gy + 1).wait_recv()

    @pl.when(has_left)
    def _():
        side_copy(1, gy - 1).wait_send()
        side_copy(0, gy - 1).wait_recv()

    own.wait()
    second.wait_send()
    second.wait_recv()
    in_ref[...] = land[...].reshape(in_ref.shape)
    low_ref[...] = halo[0]
    high_ref[...] = halo[1]
    low_rows_ref[...] = sides[0]
    high_rows_ref[...] = sides[1]


def exchange(current, edges, outgoing, rows_of, columns):
    halo_shape = jax.ShapeDtypeStruct((3, HALO_ROWS, CY), jnp.float32)
    side_shape = jax.ShapeDtypeStruct(edges.shape, jnp.float32)
    return pl.pallas_call(
        functools.partial(exchange_kernel, (rows_of, columns)),
        out_shape=(jax.ShapeDtypeStruct(outgoing.shape, jnp.float32), halo_shape, halo_shape, side_shape, side_shape),
        in_specs=[pl.BlockSpec(memory_space=pl.ANY)] * 2 + [pl.BlockSpec(memory_space=pltpu.VMEM)],
        out_specs=tuple(vmem_specs(5)),
        scratch_shapes=[
            pltpu.VMEM((columns, rows_of * CAP, CY), jnp.float32),
            pltpu.VMEM((rows_of, columns, CAP, CY), jnp.float32),
            pltpu.VMEM((2, 3, HALO_ROWS, CY), jnp.float32),
            pltpu.VMEM((2,) + edges.shape, jnp.float32),
            pltpu.SemaphoreType.DMA(()),
            pltpu.SemaphoreType.DMA(()),
            pltpu.SemaphoreType.DMA(()),
            pltpu.SemaphoreType.DMA(()),
            pltpu.SemaphoreType.DMA(()),
            pltpu.SemaphoreType.DMA((2,)),
            pltpu.SemaphoreType.DMA((2,)),
            pltpu.SemaphoreType.DMA((2,)),
            pltpu.SemaphoreType.DMA((2,)),
        ],
        compiler_params=pltpu.CompilerParams(collective_id=0, has_side_effects=True),
    )(current, edges, outgoing)


def route(payload):
    tile_data, tile_rows = payload
    width = tile_data.shape[-1]
    received_data, received_rows = (
        lax.all_to_all(tile_data, ("gx", "gy"), split_axis=0, concat_axis=0, tiled=True),
        lax.all_to_all(tile_rows, ("gx", "gy"), split_axis=0, concat_axis=0, tiled=True),
    )
    return (received_data.reshape(-1, width), received_rows.reshape(-1))


def deliver(outgoing, send_rows):
    routed = route((outgoing, send_rows))
    return from_partner((routed[0], routed[1]), "sec", 0)


def on_device(state, previous, coeff, wet_mask, link_dest, link_rows, link_weight):
    section = lax.axis_index("sec")
    owners = lax.axis_size("gx") * lax.axis_size("gy")
    fine_rows = REFINE * CX
    current = state[0, :, 0, 0].reshape(3, ROWS, CY)
    earlier = previous[0, :, 0, 0].reshape(3, ROWS, CY)
    factors = coeff[0, :, 0, 0].reshape(2, ROWS, CY)
    wet = wet_mask[0, 0].reshape(ROWS, CY)
    targets = link_dest.reshape(-1)
    pairs = link_rows.reshape(-1, 2)
    source_rows = pairs[:, 0]
    landing = pairs[:, 1]
    weights = link_weight.reshape(-1)
    one_hot = (targets[:, None] == jnp.arange(owners, dtype=jnp.int32)[None, :]).astype(jnp.int32)
    before = jnp.cumsum(one_hot, axis=0) - one_hot
    slot_index = jnp.sum(before * one_hot, axis=1)
    position = targets * CAP + slot_index
    send_rows = jnp.zeros((owners * CAP,), jnp.int32).at[position].set(landing).reshape(owners, CAP)
    rows_of, columns = lax.axis_size("gx"), lax.axis_size("gy")
    staged = ((targets % columns) * rows_of + targets // columns) * CAP + slot_index
    slot_rows = jnp.full((owners * CAP,), -1, jnp.int32).at[staged].set(source_rows)
    slot_weights = jnp.zeros((owners * CAP,), jnp.float32).at[staged].set(weights)
    pick = jnp.where(slot_rows[:, None] == jnp.arange(fine_rows, dtype=jnp.int32)[None, :], slot_weights[:, None], 0.0)
    arrived_rows = deliver(jnp.zeros((owners, CAP, CY), jnp.float32), send_rows)[1].reshape(1, -1)
    outgoing, edges = lax.cond(
        section == 0,
        lambda: prepare(elastic_tiles, current, pick),
        lambda: prepare(shallow_tiles, current, pick),
    )
    for step_index in range(STEPS):
        arrived, low_x, high_x, low_y, high_y = exchange(
            current, edges, outgoing, lax.axis_size("gx"), lax.axis_size("gy")
        )

        def elastic_branch():
            scratch = [
                pltpu.VMEM((3, PAD_ROWS, CY), jnp.float32),
                pltpu.VMEM((3, ROWS + 2 * EDGE, 1), jnp.float32),
                pltpu.VMEM((3, ROWS + 2 * EDGE, 1), jnp.float32),
            ]
            return run_step(elastic_kernel, scratch, current, earlier, factors, low_x, high_x, low_y, high_y,
                            arrived_rows, arrived, pick)

        def shallow_branch():
            scratch = [
                pltpu.VMEM((3, PAD_ROWS, CY), jnp.float32),
                pltpu.VMEM((ROWS, CY), jnp.float32),
                pltpu.VMEM((3, ROWS + 2 * EDGE, 1), jnp.float32),
                pltpu.VMEM((3, ROWS + 2 * EDGE, 1), jnp.float32),
            ]
            return run_step(shallow_kernel, scratch, current, earlier, factors, wet, low_x, high_x, low_y, high_y,
                            arrived_rows, arrived, pick)

        updated, outgoing, edges = lax.cond(section == 0, elastic_branch, shallow_branch)
        earlier, current = (current, updated)
    return current.reshape(1, 3, 1, 1, -1)


def solution(mesh):
    placed = (
        P("sec", None, "gx", "gy", None),
        P("sec", None, "gx", "gy", None),
        P("sec", None, "gx", "gy", None),
        P("gx", "gy", None),
        P("sec", "gx", "gy", None, None),
        P("sec", "gx", "gy", None, None),
        P("sec", "gx", "gy", None),
    )
    return jax.shard_map(
        on_device,
        mesh=mesh,
        in_specs=placed,
        out_specs=P("sec", None, "gx", "gy", None),
        check_vma=False,
    )
```

```python
import functools

import jax
import jax.numpy as jnp
from jax import lax
from jax.experimental import pallas as pl
from jax.experimental.pallas import tpu as pltpu
from jax.sharding import PartitionSpec as P

CX = 8
CY = 128
REFINE = 10
NL = 100
STEPS = 4
CAP = 4

ROWS = CX * NL
BASE = 104
PAD_ROWS = BASE + ROWS + BASE
CHUNK = 40
EDGE = 16
HALO_ROWS = NL + 4
EDGE_LANES = 896


def from_partner(value, axis, stride):
    return lax.ppermute(value, axis, [(i, i ^ 1 << stride) for i in range(lax.axis_size(axis))])


def shift_pairs(axis):
    count = lax.axis_size(axis)
    forward = [(i, i + 1) for i in range(count - 1)]
    backward = [(target, source) for source, target in forward]
    return forward, backward


def fill_scratch(scratch, cur_ref, low_ref, high_ref, fields):
    for f in range(fields):
        scratch[f, pl.ds(BASE - HALO_ROWS, HALO_ROWS), :] = low_ref[f]
        scratch[f, pl.ds(BASE, ROWS), :] = cur_ref[f]
        scratch[f, pl.ds(BASE + ROWS, HALO_ROWS), :] = high_ref[f]


def lane_index(rows):
    return lax.broadcasted_iota(jnp.int32, (rows, CY), 1)


def row_mask(r0, rows, period, phase):
    local = lax.broadcasted_iota(jnp.int32, (rows, CY), 0)
    mask = jnp.zeros((rows, CY), jnp.bool_)
    for r in range(rows):
        if (r0 + r) % period == phase:
            mask = mask | (local == r)
    return mask


def exact_dot(a, b):
    return jnp.dot(a, b, precision=lax.Precision.HIGHEST, preferred_element_type=jnp.float32)


def select_dot(a, b):
    return jnp.dot(a, b, precision=lax.Precision.HIGH, preferred_element_type=jnp.float32)


def landing_sum(rows_ref, arrived_ref, count):
    slots = rows_ref.shape[1]
    one_hot = (lax.broadcasted_iota(jnp.int32, (count, slots), 0) == rows_ref[...]).astype(jnp.float32)
    return exact_dot(one_hot, arrived_ref[...])


def edge_rows(out_ref, edges_ref):
    rows = lax.broadcasted_iota(jnp.int32, (8, CY), 0)
    lanes = lax.broadcasted_iota(jnp.int32, (8, CY), 1)
    select = (((rows == 0) & (lanes == CY - 1)) | ((rows == 1) & (lanes == 0))).astype(jnp.float32)
    for f in range(3):
        picked = lax.dot_general(select, out_ref[f], (((1,), (1,)), ((), ())), precision=lax.Precision.HIGHEST,
                                 preferred_element_type=jnp.float32)
        edges_ref[f] = jnp.zeros(edges_ref.shape[1:], jnp.float32)
        edges_ref[f, :, pl.ds(0, ROWS)] = picked


def fill_sides(low_rows_ref, high_rows_ref, left_pad, right_pad):
    for f in range(3):
        left_pad[f, pl.ds(EDGE, ROWS), :] = jnp.transpose(low_rows_ref[f])[:ROWS, 0:1]
        right_pad[f, pl.ds(EDGE, ROWS), :] = jnp.transpose(high_rows_ref[f])[:ROWS, 1:2]


def spread(cb):
    coarse = lax.broadcasted_iota(jnp.int32, (CY, CY), 0)
    fine = lax.broadcasted_iota(jnp.int32, (CY, CY), 1) + cb * CY
    return ((fine >= coarse * REFINE) & (fine < coarse * REFINE + REFINE)).astype(jnp.float32)


def elastic_kernel(cur_ref, prev_ref, coef_ref, low_ref, high_ref, low_rows_ref, high_rows_ref, rows_ref, arrived_ref,
                   pick_ref, out_ref, tiles_ref, edges_ref, scratch, left_pad, right_pad):
    fill_scratch(scratch, cur_ref, low_ref, high_ref, 3)
    fill_sides(low_rows_ref, high_rows_ref, left_pad, right_pad)
    force = landing_sum(rows_ref, arrived_ref, CX)
    lanes = lane_index(CHUNK)
    first_lane = lanes == 0
    last_lane = lanes == CY - 1
    own_axis = (0, 2, 1)
    for r0 in range(0, ROWS, CHUNK):
        top_layer = row_mask(r0, CHUNK, NL, 0)
        bottom_layer = row_mask(r0, CHUNK, NL, NL - 1)
        shear = coef_ref[0, pl.ds(r0, CHUNK), :]
        lame = coef_ref[1, pl.ds(r0, CHUNK), :]
        stiffness = lame + 2.0 * shear
        for c in range(3):
            at = BASE + r0
            v = scratch[c, pl.ds(at, CHUNK), :]
            along_first = scratch[c, pl.ds(at + NL, CHUNK), :] - 2.0 * v + scratch[c, pl.ds(at - NL, CHUNK), :]
            deeper = jnp.where(bottom_layer, 0.0, scratch[c, pl.ds(at + 1, CHUNK), :])
            shallower = jnp.where(top_layer, 0.0, scratch[c, pl.ds(at - 1, CHUNK), :])
            along_depth = deeper - 2.0 * v + shallower
            after = jnp.where(last_lane, right_pad[c, pl.ds(EDGE + r0, CHUNK), :], pltpu.roll(v, CY - 1, 1))
            before = jnp.where(first_lane, left_pad[c, pl.ds(EDGE + r0, CHUNK), :], pltpu.roll(v, 1, 1))
            along_second = after - 2.0 * v + before
            factors = [stiffness if own_axis[c] == axis_index else shear for axis_index in range(3)]
            acceleration = factors[0] * along_first + factors[1] * along_depth + factors[2] * along_second
            out_ref[c, pl.ds(r0, CHUNK), :] = 2.0 * v - prev_ref[c, pl.ds(r0, CHUNK), :] + acceleration
    for x in range(CX):
        out_ref[2, pl.ds(x * NL, 1), :] = out_ref[2, pl.ds(x * NL, 1), :] + force[x : x + 1]
    elastic_tiles(out_ref, pick_ref, tiles_ref)
    edge_rows(out_ref, edges_ref)


def shallow_kernel(cur_ref, prev_ref, coef_ref, wet_ref, low_ref, high_ref, low_rows_ref, high_rows_ref, rows_ref,
                   arrived_ref, pick_ref, out_ref, tiles_ref, edges_ref, scratch, source_ref, left_pad, right_pad):
    fill_scratch(scratch, cur_ref, low_ref, high_ref, 3)
    fill_sides(low_rows_ref, high_rows_ref, left_pad, right_pad)
    coarse_source = landing_sum(rows_ref, arrived_ref, REFINE * CX)
    for cb in range(REFINE):
        source_ref[pl.ds(cb, REFINE * CX, stride=REFINE), :] = select_dot(coarse_source, spread(cb))
    lanes = lane_index(CHUNK)
    first_lane = lanes == 0
    last_lane = lanes == CY - 1
    first_block = row_mask(0, CHUNK, REFINE, 0)
    last_block = row_mask(0, CHUNK, REFINE, REFINE - 1)
    for r0 in range(0, ROWS, CHUNK):
        at = BASE + r0

        def rows_diff(f):
            return scratch[f, pl.ds(at + REFINE, CHUNK), :] - scratch[f, pl.ds(at - REFINE, CHUNK), :]

        def columns_diff(f):
            v = scratch[f, pl.ds(at, CHUNK), :]
            wrap_after = jnp.where(last_block, right_pad[f, pl.ds(EDGE + r0 - (REFINE - 1), CHUNK), :],
                                   pltpu.roll(scratch[f, pl.ds(at + 1, CHUNK), :], CY - 1, 1))
            wrap_before = jnp.where(first_block, left_pad[f, pl.ds(EDGE + r0 + REFINE - 1, CHUNK), :],
                                    pltpu.roll(scratch[f, pl.ds(at - 1, CHUNK), :], 1, 1))
            after = jnp.where(last_lane, wrap_after, pltpu.roll(v, CY - 1, 1))
            before = jnp.where(first_lane, wrap_before, pltpu.roll(v, 1, 1))
            return after - before

        wave = coef_ref[0, pl.ds(r0, CHUNK), :]
        area = coef_ref[1, pl.ds(r0, CHUNK), :]
        wet = wet_ref[pl.ds(r0, CHUNK), :].astype(jnp.float32)
        eta_r = rows_diff(0)
        eta_c = columns_diff(0)
        out_ref[1, pl.ds(r0, CHUNK), :] = wet * (prev_ref[1, pl.ds(r0, CHUNK), :] - wave * eta_r)
        out_ref[2, pl.ds(r0, CHUNK), :] = wet * (prev_ref[2, pl.ds(r0, CHUNK), :] - wave * eta_c)
        divergence = rows_diff(1) + columns_diff(2)
        out_ref[0, pl.ds(r0, CHUNK), :] = wet * (
            prev_ref[0, pl.ds(r0, CHUNK), :] - area * divergence + source_ref[pl.ds(r0, CHUNK), :]
        )
    shallow_tiles(out_ref, pick_ref, tiles_ref)
    edge_rows(out_ref, edges_ref)


def shallow_tiles(field_ref, pick_ref, tiles_ref):
    total = jnp.zeros((REFINE * CX, CY), jnp.float32)
    for cb in range(REFINE):
        total = total + select_dot(field_ref[0, pl.ds(cb, REFINE * CX, stride=REFINE), :], spread(cb).T)
    tiles_ref[...] = exact_dot(pick_ref[...], total / REFINE)


def elastic_tiles(field_ref, pick_ref, tiles_ref):
    uplift = field_ref[2, pl.ds(0, CX, stride=NL), :]
    tiles_ref[...] = exact_dot(pick_ref[:, :CX], uplift)


def prepare_kernel(tiles_of, cur_ref, pick_ref, tiles_ref, edges_ref):
    tiles_of(cur_ref, pick_ref, tiles_ref)
    edge_rows(cur_ref, edges_ref)


def prepare(tiles_of, current, pick):
    return pl.pallas_call(
        functools.partial(prepare_kernel, tiles_of),
        out_shape=(
            jax.ShapeDtypeStruct((pick.shape[0], CY), jnp.float32),
            jax.ShapeDtypeStruct((3, 8, EDGE_LANES), jnp.float32),
        ),
        in_specs=vmem_specs(2),
        out_specs=tuple(vmem_specs(2)),
    )(current, pick)


def vmem_specs(count):
    return [pl.BlockSpec(memory_space=pltpu.VMEM)] * count


def run_step(kernel, scratch_shapes, *operands):
    slots = operands[-1].shape[0]
    return pl.pallas_call(
        kernel,
        out_shape=(
            jax.ShapeDtypeStruct((3, ROWS, CY), jnp.float32),
            jax.ShapeDtypeStruct((slots, CY), jnp.float32),
            jax.ShapeDtypeStruct((3, 8, EDGE_LANES), jnp.float32),
        ),
        in_specs=vmem_specs(len(operands)),
        out_specs=tuple(vmem_specs(3)),
        scratch_shapes=scratch_shapes,
    )(*operands)


def exchange_kernel(sizes, cur_ref, edges_ref, out_ref, in_ref, low_ref, high_ref, low_rows_ref, high_rows_ref,
                    land, halo, sides, send_sem, recv_sem, halo_send, halo_recv, side_send, side_recv):
    owners, rows_of, columns = sizes
    other = 1 - lax.axis_index("sec")
    section = lax.axis_index("sec")
    gx = lax.axis_index("gx")
    gy = lax.axis_index("gy")
    me = gx * columns + gy
    has_low = gx > 0
    has_high = gx < rows_of - 1
    has_left = gy > 0
    has_right = gy < columns - 1
    halo[...] = jnp.zeros_like(halo)
    sides[...] = jnp.zeros_like(sides)
    barrier = pltpu.get_barrier_semaphore()
    def greet(d, carry):
        pl.semaphore_signal(barrier, inc=1, device_id=(other, d // columns, d % columns),
                            device_id_type=pl.DeviceIdType.MESH)
        return carry

    lax.fori_loop(0, owners, greet, 0, unroll=8)

    @pl.when(has_low)
    def _():
        pl.semaphore_signal(barrier, inc=1, device_id=(section, gx - 1, gy), device_id_type=pl.DeviceIdType.MESH)

    @pl.when(has_high)
    def _():
        pl.semaphore_signal(barrier, inc=1, device_id=(section, gx + 1, gy), device_id_type=pl.DeviceIdType.MESH)

    @pl.when(has_left)
    def _():
        pl.semaphore_signal(barrier, inc=1, device_id=(section, gx, gy - 1), device_id_type=pl.DeviceIdType.MESH)

    @pl.when(has_right)
    def _():
        pl.semaphore_signal(barrier, inc=1, device_id=(section, gx, gy + 1), device_id_type=pl.DeviceIdType.MESH)

    neighbours = [has_low, has_high, has_left, has_right]
    pl.semaphore_wait(barrier, owners + sum(n.astype(jnp.int32) for n in neighbours))

    def side_copy(slot, target):
        return pltpu.make_async_remote_copy(
            src_ref=edges_ref,
            dst_ref=sides.at[slot],
            send_sem=side_send.at[slot],
            recv_sem=side_recv.at[slot],
            device_id=(section, gx, target),
            device_id_type=pl.DeviceIdType.MESH,
        )

    @pl.when(has_right)
    def _():
        side_copy(0, gy + 1).start()

    @pl.when(has_left)
    def _():
        side_copy(1, gy - 1).start()

    def slab_copy(start, slot, target):
        return pltpu.make_async_remote_copy(
            src_ref=cur_ref.at[:, pl.ds(start, HALO_ROWS), :],
            dst_ref=halo.at[slot],
            send_sem=halo_send.at[slot],
            recv_sem=halo_recv.at[slot],
            device_id=(section, target, gy),
            device_id_type=pl.DeviceIdType.MESH,
        )

    @pl.when(has_high)
    def _():
        slab_copy(ROWS - HALO_ROWS, 0, gx + 1).start()

    @pl.when(has_low)
    def _():
        slab_copy(0, 1, gx - 1).start()

    def send(d, carry):
        pltpu.make_async_remote_copy(
            src_ref=out_ref.at[pl.ds(d * CAP, CAP)],
            dst_ref=land.at[pl.ds(me * CAP, CAP)],
            send_sem=send_sem,
            recv_sem=recv_sem,
            device_id=(other, d // columns, d % columns),
            device_id_type=pl.DeviceIdType.MESH,
        ).start()
        return carry

    lax.fori_loop(0, owners, send, 0, unroll=8)
    whole = pltpu.make_async_remote_copy(
        src_ref=out_ref,
        dst_ref=land,
        send_sem=send_sem,
        recv_sem=recv_sem,
        device_id=(other, gx, gy),
        device_id_type=pl.DeviceIdType.MESH,
    )

    @pl.when(has_high)
    def _():
        slab_copy(ROWS - HALO_ROWS, 0, gx + 1).wait_send()
        slab_copy(0, 1, gx + 1).wait_recv()

    @pl.when(has_low)
    def _():
        slab_copy(0, 1, gx - 1).wait_send()
        slab_copy(ROWS - HALO_ROWS, 0, gx - 1).wait_recv()

    @pl.when(has_right)
    def _():
        side_copy(0, gy + 1).wait_send()
        side_copy(1, gy + 1).wait_recv()

    @pl.when(has_left)
    def _():
        side_copy(1, gy - 1).wait_send()
        side_copy(0, gy - 1).wait_recv()

    whole.wait_send()
    whole.wait_recv()
    in_ref[...] = land[...]
    low_ref[...] = halo[0]
    high_ref[...] = halo[1]
    low_rows_ref[...] = sides[0]
    high_rows_ref[...] = sides[1]


def exchange(current, edges, outgoing, owners, rows_of, columns):
    halo_shape = jax.ShapeDtypeStruct((3, HALO_ROWS, CY), jnp.float32)
    side_shape = jax.ShapeDtypeStruct(edges.shape, jnp.float32)
    return pl.pallas_call(
        functools.partial(exchange_kernel, (owners, rows_of, columns)),
        out_shape=(jax.ShapeDtypeStruct(outgoing.shape, jnp.float32), halo_shape, halo_shape, side_shape, side_shape),
        in_specs=[pl.BlockSpec(memory_space=pl.ANY)] * 2 + [pl.BlockSpec(memory_space=pltpu.VMEM)],
        out_specs=tuple(vmem_specs(5)),
        scratch_shapes=[
            pltpu.VMEM(outgoing.shape, jnp.float32),
            pltpu.VMEM((2, 3, HALO_ROWS, CY), jnp.float32),
            pltpu.VMEM((2,) + edges.shape, jnp.float32),
            pltpu.SemaphoreType.DMA(()),
            pltpu.SemaphoreType.DMA(()),
            pltpu.SemaphoreType.DMA((2,)),
            pltpu.SemaphoreType.DMA((2,)),
            pltpu.SemaphoreType.DMA((2,)),
            pltpu.SemaphoreType.DMA((2,)),
        ],
        compiler_params=pltpu.CompilerParams(collective_id=0, has_side_effects=True),
    )(current, edges, outgoing)


def route(payload):
    tile_data, tile_rows = payload
    width = tile_data.shape[-1]
    received_data, received_rows = (
        lax.all_to_all(tile_data, ("gx", "gy"), split_axis=0, concat_axis=0, tiled=True),
        lax.all_to_all(tile_rows, ("gx", "gy"), split_axis=0, concat_axis=0, tiled=True),
    )
    return (received_data.reshape(-1, width), received_rows.reshape(-1))


def deliver(outgoing, send_rows):
    routed = route((outgoing, send_rows))
    return from_partner((routed[0], routed[1]), "sec", 0)


def on_device(state, previous, coeff, wet_mask, link_dest, link_rows, link_weight):
    section = lax.axis_index("sec")
    owners = lax.axis_size("gx") * lax.axis_size("gy")
    fine_rows = REFINE * CX
    current = state[0, :, 0, 0].reshape(3, ROWS, CY)
    earlier = previous[0, :, 0, 0].reshape(3, ROWS, CY)
    factors = coeff[0, :, 0, 0].reshape(2, ROWS, CY)
    wet = wet_mask[0, 0].reshape(ROWS, CY)
    targets = link_dest.reshape(-1)
    pairs = link_rows.reshape(-1, 2)
    source_rows = pairs[:, 0]
    landing = pairs[:, 1]
    weights = link_weight.reshape(-1)
    one_hot = (targets[:, None] == jnp.arange(owners, dtype=jnp.int32)[None, :]).astype(jnp.int32)
    before = jnp.cumsum(one_hot, axis=0) - one_hot
    slot_index = jnp.sum(before * one_hot, axis=1)
    position = targets * CAP + slot_index
    send_rows = jnp.zeros((owners * CAP,), jnp.int32).at[position].set(landing).reshape(owners, CAP)
    slot_rows = jnp.full((owners * CAP,), -1, jnp.int32).at[position].set(source_rows)
    slot_weights = jnp.zeros((owners * CAP,), jnp.float32).at[position].set(weights)
    pick = jnp.where(slot_rows[:, None] == jnp.arange(fine_rows, dtype=jnp.int32)[None, :], slot_weights[:, None], 0.0)
    arrived_rows = deliver(jnp.zeros((owners, CAP, CY), jnp.float32), send_rows)[1].reshape(1, -1)
    outgoing, edges = lax.cond(
        section == 0,
        lambda: prepare(elastic_tiles, current, pick),
        lambda: prepare(shallow_tiles, current, pick),
    )
    for step_index in range(STEPS):
        arrived, low_x, high_x, low_y, high_y = exchange(
            current, edges, outgoing, owners, lax.axis_size("gx"), lax.axis_size("gy")
        )

        def elastic_branch():
            scratch = [
                pltpu.VMEM((3, PAD_ROWS, CY), jnp.float32),
                pltpu.VMEM((3, ROWS + 2 * EDGE, 1), jnp.float32),
                pltpu.VMEM((3, ROWS + 2 * EDGE, 1), jnp.float32),
            ]
            return run_step(elastic_kernel, scratch, current, earlier, factors, low_x, high_x, low_y, high_y,
                            arrived_rows, arrived, pick)

        def shallow_branch():
            scratch = [
                pltpu.VMEM((3, PAD_ROWS, CY), jnp.float32),
                pltpu.VMEM((ROWS, CY), jnp.float32),
                pltpu.VMEM((3, ROWS + 2 * EDGE, 1), jnp.float32),
                pltpu.VMEM((3, ROWS + 2 * EDGE, 1), jnp.float32),
            ]
            return run_step(shallow_kernel, scratch, current, earlier, factors, wet, low_x, high_x, low_y, high_y,
                            arrived_rows, arrived, pick)

        updated, outgoing, edges = lax.cond(section == 0, elastic_branch, shallow_branch)
        earlier, current = (current, updated)
    return current.reshape(1, 3, 1, 1, -1)


def solution(mesh):
    placed = (
        P("sec", None, "gx", "gy", None),
        P("sec", None, "gx", "gy", None),
        P("sec", None, "gx", "gy", None),
        P("gx", "gy", None),
        P("sec", "gx", "gy", None, None),
        P("sec", "gx", "gy", None, None),
        P("sec", "gx", "gy", None),
    )
    return jax.shard_map(
        on_device,
        mesh=mesh,
        in_specs=placed,
        out_specs=P("sec", None, "gx", "gy", None),
        check_vma=False,
    )
```

```python
import functools

import jax
import jax.numpy as jnp
from jax import lax
from jax.experimental import pallas as pl
from jax.experimental.pallas import tpu as pltpu
from jax.sharding import PartitionSpec as P

CX = 8
CY = 128
REFINE = 10
NL = 100
STEPS = 4
CAP = 4

ROWS = CX * NL
BASE = 104
PAD_ROWS = BASE + ROWS + BASE
CHUNK = 40
EDGE = 16
HALO_ROWS = NL + 4
EDGE_LANES = 896


def from_partner(value, axis, stride):
    return lax.ppermute(value, axis, [(i, i ^ 1 << stride) for i in range(lax.axis_size(axis))])


def shift_pairs(axis):
    count = lax.axis_size(axis)
    forward = [(i, i + 1) for i in range(count - 1)]
    backward = [(target, source) for source, target in forward]
    return forward, backward


def fill_scratch(scratch, cur_ref, low_ref, high_ref, fields):
    for f in range(fields):
        scratch[f, pl.ds(BASE - HALO_ROWS, HALO_ROWS), :] = low_ref[f]
        scratch[f, pl.ds(BASE, ROWS), :] = cur_ref[f]
        scratch[f, pl.ds(BASE + ROWS, HALO_ROWS), :] = high_ref[f]


def lane_index(rows):
    return lax.broadcasted_iota(jnp.int32, (rows, CY), 1)


def row_mask(r0, rows, period, phase):
    local = lax.broadcasted_iota(jnp.int32, (rows, CY), 0)
    mask = jnp.zeros((rows, CY), jnp.bool_)
    for r in range(rows):
        if (r0 + r) % period == phase:
            mask = mask | (local == r)
    return mask


def exact_dot(a, b):
    return jnp.dot(a, b, precision=lax.Precision.HIGHEST, preferred_element_type=jnp.float32)


def select_dot(a, b):
    return jnp.dot(a, b, precision=lax.Precision.HIGH, preferred_element_type=jnp.float32)


def landing_sum(rows_ref, arrived_ref, count):
    slots = rows_ref.shape[1]
    one_hot = (lax.broadcasted_iota(jnp.int32, (count, slots), 0) == rows_ref[...]).astype(jnp.float32)
    return exact_dot(one_hot, arrived_ref[...])


def edge_rows(out_ref, edges_ref):
    rows = lax.broadcasted_iota(jnp.int32, (8, CY), 0)
    lanes = lax.broadcasted_iota(jnp.int32, (8, CY), 1)
    select = (((rows == 0) & (lanes == CY - 1)) | ((rows == 1) & (lanes == 0))).astype(jnp.float32)
    for f in range(3):
        picked = lax.dot_general(select, out_ref[f], (((1,), (1,)), ((), ())), precision=lax.Precision.HIGHEST,
                                 preferred_element_type=jnp.float32)
        edges_ref[f] = jnp.zeros(edges_ref.shape[1:], jnp.float32)
        edges_ref[f, :, pl.ds(0, ROWS)] = picked


def fill_sides(low_rows_ref, high_rows_ref, left_pad, right_pad):
    for f in range(3):
        left_pad[f, pl.ds(EDGE, ROWS), :] = jnp.transpose(low_rows_ref[f])[:ROWS, 0:1]
        right_pad[f, pl.ds(EDGE, ROWS), :] = jnp.transpose(high_rows_ref[f])[:ROWS, 1:2]


def spread(cb):
    coarse = lax.broadcasted_iota(jnp.int32, (CY, CY), 0)
    fine = lax.broadcasted_iota(jnp.int32, (CY, CY), 1) + cb * CY
    return ((fine >= coarse * REFINE) & (fine < coarse * REFINE + REFINE)).astype(jnp.float32)


def elastic_kernel(cur_ref, prev_ref, coef_ref, low_ref, high_ref, low_rows_ref, high_rows_ref, rows_ref, arrived_ref,
                   pick_ref, out_ref, tiles_ref, edges_ref, scratch, left_pad, right_pad):
    fill_scratch(scratch, cur_ref, low_ref, high_ref, 3)
    fill_sides(low_rows_ref, high_rows_ref, left_pad, right_pad)
    force = landing_sum(rows_ref, arrived_ref, CX)
    lanes = lane_index(CHUNK)
    first_lane = lanes == 0
    last_lane = lanes == CY - 1
    own_axis = (0, 2, 1)
    for r0 in range(0, ROWS, CHUNK):
        top_layer = row_mask(r0, CHUNK, NL, 0)
        bottom_layer = row_mask(r0, CHUNK, NL, NL - 1)
        shear = coef_ref[0, pl.ds(r0, CHUNK), :]
        lame = coef_ref[1, pl.ds(r0, CHUNK), :]
        stiffness = lame + 2.0 * shear
        for c in range(3):
            at = BASE + r0
            v = scratch[c, pl.ds(at, CHUNK), :]
            along_first = scratch[c, pl.ds(at + NL, CHUNK), :] - 2.0 * v + scratch[c, pl.ds(at - NL, CHUNK), :]
            deeper = jnp.where(bottom_layer, 0.0, scratch[c, pl.ds(at + 1, CHUNK), :])
            shallower = jnp.where(top_layer, 0.0, scratch[c, pl.ds(at - 1, CHUNK), :])
            along_depth = deeper - 2.0 * v + shallower
            after = jnp.where(last_lane, right_pad[c, pl.ds(EDGE + r0, CHUNK), :], pltpu.roll(v, CY - 1, 1))
            before = jnp.where(first_lane, left_pad[c, pl.ds(EDGE + r0, CHUNK), :], pltpu.roll(v, 1, 1))
            along_second = after - 2.0 * v + before
            factors = [stiffness if own_axis[c] == axis_index else shear for axis_index in range(3)]
            acceleration = factors[0] * along_first + factors[1] * along_depth + factors[2] * along_second
            out_ref[c, pl.ds(r0, CHUNK), :] = 2.0 * v - prev_ref[c, pl.ds(r0, CHUNK), :] + acceleration
    for x in range(CX):
        out_ref[2, pl.ds(x * NL, 1), :] = out_ref[2, pl.ds(x * NL, 1), :] + force[x : x + 1]
    elastic_tiles(out_ref, pick_ref, tiles_ref)
    edge_rows(out_ref, edges_ref)


def shallow_kernel(cur_ref, prev_ref, coef_ref, wet_ref, low_ref, high_ref, low_rows_ref, high_rows_ref, rows_ref,
                   arrived_ref, pick_ref, out_ref, tiles_ref, edges_ref, scratch, source_ref, left_pad, right_pad):
    fill_scratch(scratch, cur_ref, low_ref, high_ref, 3)
    fill_sides(low_rows_ref, high_rows_ref, left_pad, right_pad)
    coarse_source = landing_sum(rows_ref, arrived_ref, REFINE * CX)
    for cb in range(REFINE):
        source_ref[pl.ds(cb, REFINE * CX, stride=REFINE), :] = select_dot(coarse_source, spread(cb))
    lanes = lane_index(CHUNK)
    first_lane = lanes == 0
    last_lane = lanes == CY - 1
    first_block = row_mask(0, CHUNK, REFINE, 0)
    last_block = row_mask(0, CHUNK, REFINE, REFINE - 1)
    for r0 in range(0, ROWS, CHUNK):
        at = BASE + r0

        def rows_diff(f):
            return scratch[f, pl.ds(at + REFINE, CHUNK), :] - scratch[f, pl.ds(at - REFINE, CHUNK), :]

        def columns_diff(f):
            v = scratch[f, pl.ds(at, CHUNK), :]
            wrap_after = jnp.where(last_block, right_pad[f, pl.ds(EDGE + r0 - (REFINE - 1), CHUNK), :],
                                   pltpu.roll(scratch[f, pl.ds(at + 1, CHUNK), :], CY - 1, 1))
            wrap_before = jnp.where(first_block, left_pad[f, pl.ds(EDGE + r0 + REFINE - 1, CHUNK), :],
                                    pltpu.roll(scratch[f, pl.ds(at - 1, CHUNK), :], 1, 1))
            after = jnp.where(last_lane, wrap_after, pltpu.roll(v, CY - 1, 1))
            before = jnp.where(first_lane, wrap_before, pltpu.roll(v, 1, 1))
            return after - before

        wave = coef_ref[0, pl.ds(r0, CHUNK), :]
        area = coef_ref[1, pl.ds(r0, CHUNK), :]
        wet = wet_ref[pl.ds(r0, CHUNK), :].astype(jnp.float32)
        eta_r = rows_diff(0)
        eta_c = columns_diff(0)
        out_ref[1, pl.ds(r0, CHUNK), :] = wet * (prev_ref[1, pl.ds(r0, CHUNK), :] - wave * eta_r)
        out_ref[2, pl.ds(r0, CHUNK), :] = wet * (prev_ref[2, pl.ds(r0, CHUNK), :] - wave * eta_c)
        divergence = rows_diff(1) + columns_diff(2)
        out_ref[0, pl.ds(r0, CHUNK), :] = wet * (
            prev_ref[0, pl.ds(r0, CHUNK), :] - area * divergence + source_ref[pl.ds(r0, CHUNK), :]
        )
    shallow_tiles(out_ref, pick_ref, tiles_ref)
    edge_rows(out_ref, edges_ref)


def shallow_tiles(field_ref, pick_ref, tiles_ref):
    total = jnp.zeros((REFINE * CX, CY), jnp.float32)
    for cb in range(REFINE):
        total = total + select_dot(field_ref[0, pl.ds(cb, REFINE * CX, stride=REFINE), :], spread(cb).T)
    tiles_ref[...] = exact_dot(pick_ref[...], total / REFINE)


def elastic_tiles(field_ref, pick_ref, tiles_ref):
    uplift = field_ref[2, pl.ds(0, CX, stride=NL), :]
    tiles_ref[...] = exact_dot(pick_ref[:, :CX], uplift)


def prepare_kernel(tiles_of, cur_ref, pick_ref, tiles_ref, edges_ref):
    tiles_of(cur_ref, pick_ref, tiles_ref)
    edge_rows(cur_ref, edges_ref)


def prepare(tiles_of, current, pick):
    return pl.pallas_call(
        functools.partial(prepare_kernel, tiles_of),
        out_shape=(
            jax.ShapeDtypeStruct((pick.shape[0], CY), jnp.float32),
            jax.ShapeDtypeStruct((3, 8, EDGE_LANES), jnp.float32),
        ),
        in_specs=vmem_specs(2),
        out_specs=tuple(vmem_specs(2)),
    )(current, pick)


def vmem_specs(count):
    return [pl.BlockSpec(memory_space=pltpu.VMEM)] * count


def run_step(kernel, scratch_shapes, *operands):
    slots = operands[-1].shape[0]
    return pl.pallas_call(
        kernel,
        out_shape=(
            jax.ShapeDtypeStruct((3, ROWS, CY), jnp.float32),
            jax.ShapeDtypeStruct((slots, CY), jnp.float32),
            jax.ShapeDtypeStruct((3, 8, EDGE_LANES), jnp.float32),
        ),
        in_specs=vmem_specs(len(operands)),
        out_specs=tuple(vmem_specs(3)),
        scratch_shapes=scratch_shapes,
    )(*operands)


def exchange_kernel(sizes, cur_ref, edges_ref, out_ref, in_ref, low_ref, high_ref, low_rows_ref, high_rows_ref,
                    land, halo, sides, send_sem, recv_sem, halo_send, halo_recv, side_send, side_recv):
    owners, rows_of, columns = sizes
    other = 1 - lax.axis_index("sec")
    section = lax.axis_index("sec")
    gx = lax.axis_index("gx")
    gy = lax.axis_index("gy")
    me = gx * columns + gy
    has_low = gx > 0
    has_high = gx < rows_of - 1
    has_left = gy > 0
    has_right = gy < columns - 1
    halo[...] = jnp.zeros_like(halo)
    sides[...] = jnp.zeros_like(sides)
    barrier = pltpu.get_barrier_semaphore()
    def greet(d, carry):
        pl.semaphore_signal(barrier, inc=1, device_id=(other, d // columns, d % columns),
                            device_id_type=pl.DeviceIdType.MESH)
        return carry

    lax.fori_loop(0, owners, greet, 0, unroll=8)

    @pl.when(has_low)
    def _():
        pl.semaphore_signal(barrier, inc=1, device_id=(section, gx - 1, gy), device_id_type=pl.DeviceIdType.MESH)

    @pl.when(has_high)
    def _():
        pl.semaphore_signal(barrier, inc=1, device_id=(section, gx + 1, gy), device_id_type=pl.DeviceIdType.MESH)

    @pl.when(has_left)
    def _():
        pl.semaphore_signal(barrier, inc=1, device_id=(section, gx, gy - 1), device_id_type=pl.DeviceIdType.MESH)

    @pl.when(has_right)
    def _():
        pl.semaphore_signal(barrier, inc=1, device_id=(section, gx, gy + 1), device_id_type=pl.DeviceIdType.MESH)

    neighbours = [has_low, has_high, has_left, has_right]
    pl.semaphore_wait(barrier, owners + sum(n.astype(jnp.int32) for n in neighbours))

    def side_copy(slot, target):
        return pltpu.make_async_remote_copy(
            src_ref=edges_ref,
            dst_ref=sides.at[slot],
            send_sem=side_send.at[slot],
            recv_sem=side_recv.at[slot],
            device_id=(section, gx, target),
            device_id_type=pl.DeviceIdType.MESH,
        )

    @pl.when(has_right)
    def _():
        side_copy(0, gy + 1).start()

    @pl.when(has_left)
    def _():
        side_copy(1, gy - 1).start()

    def slab_copy(start, slot, target):
        return pltpu.make_async_remote_copy(
            src_ref=cur_ref.at[:, pl.ds(start, HALO_ROWS), :],
            dst_ref=halo.at[slot],
            send_sem=halo_send.at[slot],
            recv_sem=halo_recv.at[slot],
            device_id=(section, target, gy),
            device_id_type=pl.DeviceIdType.MESH,
        )

    @pl.when(has_high)
    def _():
        slab_copy(ROWS - HALO_ROWS, 0, gx + 1).start()

    @pl.when(has_low)
    def _():
        slab_copy(0, 1, gx - 1).start()

    def send(d, carry):
        pltpu.make_async_remote_copy(
            src_ref=out_ref.at[pl.ds(d * CAP, CAP)],
            dst_ref=land.at[pl.ds(me * CAP, CAP)],
            send_sem=send_sem,
            recv_sem=recv_sem,
            device_id=(other, d // columns, d % columns),
            device_id_type=pl.DeviceIdType.MESH,
        ).start()
        return carry

    lax.fori_loop(0, owners, send, 0, unroll=8)
    whole = pltpu.make_async_remote_copy(
        src_ref=out_ref,
        dst_ref=land,
        send_sem=send_sem,
        recv_sem=recv_sem,
        device_id=(other, gx, gy),
        device_id_type=pl.DeviceIdType.MESH,
    )

    @pl.when(has_high)
    def _():
        slab_copy(ROWS - HALO_ROWS, 0, gx + 1).wait_send()
        slab_copy(0, 1, gx + 1).wait_recv()

    @pl.when(has_low)
    def _():
        slab_copy(0, 1, gx - 1).wait_send()
        slab_copy(ROWS - HALO_ROWS, 0, gx - 1).wait_recv()

    @pl.when(has_right)
    def _():
        side_copy(0, gy + 1).wait_send()
        side_copy(1, gy + 1).wait_recv()

    @pl.when(has_left)
    def _():
        side_copy(1, gy - 1).wait_send()
        side_copy(0, gy - 1).wait_recv()

    whole.wait_send()
    whole.wait_recv()
    in_ref[...] = land[...]
    low_ref[...] = halo[0]
    high_ref[...] = halo[1]
    low_rows_ref[...] = sides[0]
    high_rows_ref[...] = sides[1]


def exchange(current, edges, outgoing, owners, rows_of, columns):
    halo_shape = jax.ShapeDtypeStruct((3, HALO_ROWS, CY), jnp.float32)
    side_shape = jax.ShapeDtypeStruct(edges.shape, jnp.float32)
    return pl.pallas_call(
        functools.partial(exchange_kernel, (owners, rows_of, columns)),
        out_shape=(jax.ShapeDtypeStruct(outgoing.shape, jnp.float32), halo_shape, halo_shape, side_shape, side_shape),
        in_specs=[pl.BlockSpec(memory_space=pl.ANY)] * 2 + [pl.BlockSpec(memory_space=pltpu.VMEM)],
        out_specs=tuple(vmem_specs(5)),
        scratch_shapes=[
            pltpu.VMEM(outgoing.shape, jnp.float32),
            pltpu.VMEM((2, 3, HALO_ROWS, CY), jnp.float32),
            pltpu.VMEM((2,) + edges.shape, jnp.float32),
            pltpu.SemaphoreType.DMA(()),
            pltpu.SemaphoreType.DMA(()),
            pltpu.SemaphoreType.DMA((2,)),
            pltpu.SemaphoreType.DMA((2,)),
            pltpu.SemaphoreType.DMA((2,)),
            pltpu.SemaphoreType.DMA((2,)),
        ],
        compiler_params=pltpu.CompilerParams(collective_id=outgoing.shape[1] // CY - 1, has_side_effects=True),
    )(current, edges, outgoing)


def route(payload):
    tile_data, tile_rows = payload
    width = tile_data.shape[-1]
    received_data, received_rows = (
        lax.all_to_all(tile_data, ("gx", "gy"), split_axis=0, concat_axis=0, tiled=True),
        lax.all_to_all(tile_rows, ("gx", "gy"), split_axis=0, concat_axis=0, tiled=True),
    )
    return (received_data.reshape(-1, width), received_rows.reshape(-1))


def deliver(outgoing, send_rows):
    routed = route((outgoing, send_rows))
    return from_partner((routed[0], routed[1]), "sec", 0)


def on_device(state, previous, coeff, wet_mask, link_dest, link_rows, link_weight):
    section = lax.axis_index("sec")
    owners = lax.axis_size("gx") * lax.axis_size("gy")
    fine_rows = REFINE * CX
    current = state[0, :, 0, 0].reshape(3, ROWS, CY)
    earlier = previous[0, :, 0, 0].reshape(3, ROWS, CY)
    factors = coeff[0, :, 0, 0].reshape(2, ROWS, CY)
    wet = wet_mask[0, 0].reshape(ROWS, CY)
    targets = link_dest.reshape(-1)
    pairs = link_rows.reshape(-1, 2)
    source_rows = pairs[:, 0]
    landing = pairs[:, 1]
    weights = link_weight.reshape(-1)
    one_hot = (targets[:, None] == jnp.arange(owners, dtype=jnp.int32)[None, :]).astype(jnp.int32)
    before = jnp.cumsum(one_hot, axis=0) - one_hot
    slot_index = jnp.sum(before * one_hot, axis=1)
    position = targets * CAP + slot_index
    send_rows = jnp.zeros((owners * CAP,), jnp.int32).at[position].set(landing).reshape(owners, CAP)
    slot_rows = jnp.full((owners * CAP,), -1, jnp.int32).at[position].set(source_rows)
    slot_weights = jnp.zeros((owners * CAP,), jnp.float32).at[position].set(weights)
    pick = jnp.where(slot_rows[:, None] == jnp.arange(fine_rows, dtype=jnp.int32)[None, :], slot_weights[:, None], 0.0)
    outgoing, edges = lax.cond(
        section == 0,
        lambda: prepare(elastic_tiles, current, pick),
        lambda: prepare(shallow_tiles, current, pick),
    )
    row_lanes = jnp.broadcast_to(send_rows.reshape(-1, 1).astype(jnp.float32), (owners * CAP, CY))
    outgoing = jnp.concatenate([outgoing, row_lanes], axis=1)
    for step_index in range(STEPS):
        arrived, low_x, high_x, low_y, high_y = exchange(
            current, edges, outgoing, owners, lax.axis_size("gx"), lax.axis_size("gy")
        )
        if step_index == 0:
            arrived_rows = arrived[:, CY].astype(jnp.int32).reshape(1, -1)
            arrived = arrived[:, :CY]

        def elastic_branch():
            scratch = [
                pltpu.VMEM((3, PAD_ROWS, CY), jnp.float32),
                pltpu.VMEM((3, ROWS + 2 * EDGE, 1), jnp.float32),
                pltpu.VMEM((3, ROWS + 2 * EDGE, 1), jnp.float32),
            ]
            return run_step(elastic_kernel, scratch, current, earlier, factors, low_x, high_x, low_y, high_y,
                            arrived_rows, arrived, pick)

        def shallow_branch():
            scratch = [
                pltpu.VMEM((3, PAD_ROWS, CY), jnp.float32),
                pltpu.VMEM((ROWS, CY), jnp.float32),
                pltpu.VMEM((3, ROWS + 2 * EDGE, 1), jnp.float32),
                pltpu.VMEM((3, ROWS + 2 * EDGE, 1), jnp.float32),
            ]
            return run_step(shallow_kernel, scratch, current, earlier, factors, wet, low_x, high_x, low_y, high_y,
                            arrived_rows, arrived, pick)

        updated, outgoing, edges = lax.cond(section == 0, elastic_branch, shallow_branch)
        earlier, current = (current, updated)
    return current.reshape(1, 3, 1, 1, -1)


def solution(mesh):
    placed = (
        P("sec", None, "gx", "gy", None),
        P("sec", None, "gx", "gy", None),
        P("sec", None, "gx", "gy", None),
        P("gx", "gy", None),
        P("sec", "gx", "gy", None, None),
        P("sec", "gx", "gy", None, None),
        P("sec", "gx", "gy", None),
    )
    return jax.shard_map(
        on_device,
        mesh=mesh,
        in_specs=placed,
        out_specs=P("sec", None, "gx", "gy", None),
        check_vma=False,
    )
```

```python
import functools

import jax
import jax.numpy as jnp
from jax import lax
from jax.experimental import pallas as pl
from jax.experimental.pallas import tpu as pltpu
from jax.sharding import PartitionSpec as P

CX = 8
CY = 128
REFINE = 10
NL = 100
STEPS = 4
CAP = 4

ROWS = CX * NL
BASE = 104
PAD_ROWS = BASE + ROWS + BASE
CHUNK = 40
EDGE = 16
HALO_ROWS = NL + 4
EDGE_LANES = 896


def from_partner(value, axis, stride):
    return lax.ppermute(value, axis, [(i, i ^ 1 << stride) for i in range(lax.axis_size(axis))])


def shift_pairs(axis):
    count = lax.axis_size(axis)
    forward = [(i, i + 1) for i in range(count - 1)]
    backward = [(target, source) for source, target in forward]
    return forward, backward


def fill_scratch(scratch, cur_ref, low_ref, high_ref, fields):
    for f in range(fields):
        scratch[f, pl.ds(BASE - HALO_ROWS, HALO_ROWS), :] = low_ref[f]
        scratch[f, pl.ds(BASE, ROWS), :] = cur_ref[f]
        scratch[f, pl.ds(BASE + ROWS, HALO_ROWS), :] = high_ref[f]


def lane_index(rows):
    return lax.broadcasted_iota(jnp.int32, (rows, CY), 1)


def row_mask(r0, rows, period, phase):
    local = lax.broadcasted_iota(jnp.int32, (rows, CY), 0)
    mask = jnp.zeros((rows, CY), jnp.bool_)
    for r in range(rows):
        if (r0 + r) % period == phase:
            mask = mask | (local == r)
    return mask


def exact_dot(a, b):
    return jnp.dot(a, b, precision=lax.Precision.HIGHEST, preferred_element_type=jnp.float32)


def select_dot(a, b):
    return jnp.dot(a, b, precision=lax.Precision.HIGH, preferred_element_type=jnp.float32)


def landing_sum(rows_ref, arrived_ref, count):
    slots = rows_ref.shape[1]
    one_hot = (lax.broadcasted_iota(jnp.int32, (count, slots), 0) == rows_ref[...]).astype(jnp.float32)
    return exact_dot(one_hot, arrived_ref[...])


def edge_rows(out_ref, edges_ref):
    rows = lax.broadcasted_iota(jnp.int32, (8, CY), 0)
    lanes = lax.broadcasted_iota(jnp.int32, (8, CY), 1)
    select = (((rows == 0) & (lanes == CY - 1)) | ((rows == 1) & (lanes == 0))).astype(jnp.float32)
    for f in range(3):
        picked = lax.dot_general(select, out_ref[f], (((1,), (1,)), ((), ())), precision=lax.Precision.HIGHEST,
                                 preferred_element_type=jnp.float32)
        edges_ref[f] = jnp.zeros(edges_ref.shape[1:], jnp.float32)
        edges_ref[f, :, pl.ds(0, ROWS)] = picked


def fill_sides(low_rows_ref, high_rows_ref, left_pad, right_pad):
    for f in range(3):
        left_pad[f, pl.ds(EDGE, ROWS), :] = jnp.transpose(low_rows_ref[f])[:ROWS, 0:1]
        right_pad[f, pl.ds(EDGE, ROWS), :] = jnp.transpose(high_rows_ref[f])[:ROWS, 1:2]


def spread(cb):
    coarse = lax.broadcasted_iota(jnp.int32, (CY, CY), 0)
    fine = lax.broadcasted_iota(jnp.int32, (CY, CY), 1) + cb * CY
    return ((fine >= coarse * REFINE) & (fine < coarse * REFINE + REFINE)).astype(jnp.float32)


def elastic_kernel(cur_ref, prev_ref, coef_ref, low_ref, high_ref, low_rows_ref, high_rows_ref, rows_ref, arrived_ref,
                   pick_ref, out_ref, tiles_ref, edges_ref, scratch, left_pad, right_pad):
    fill_scratch(scratch, cur_ref, low_ref, high_ref, 3)
    fill_sides(low_rows_ref, high_rows_ref, left_pad, right_pad)
    force = landing_sum(rows_ref, arrived_ref, CX)
    lanes = lane_index(CHUNK)
    first_lane = lanes == 0
    last_lane = lanes == CY - 1
    own_axis = (0, 2, 1)
    for r0 in range(0, ROWS, CHUNK):
        top_layer = row_mask(r0, CHUNK, NL, 0)
        bottom_layer = row_mask(r0, CHUNK, NL, NL - 1)
        shear = coef_ref[0, pl.ds(r0, CHUNK), :]
        lame = coef_ref[1, pl.ds(r0, CHUNK), :]
        stiffness = lame + 2.0 * shear
        for c in range(3):
            at = BASE + r0
            v = scratch[c, pl.ds(at, CHUNK), :]
            along_first = scratch[c, pl.ds(at + NL, CHUNK), :] - 2.0 * v + scratch[c, pl.ds(at - NL, CHUNK), :]
            deeper = jnp.where(bottom_layer, 0.0, scratch[c, pl.ds(at + 1, CHUNK), :])
            shallower = jnp.where(top_layer, 0.0, scratch[c, pl.ds(at - 1, CHUNK), :])
            along_depth = deeper - 2.0 * v + shallower
            after = jnp.where(last_lane, right_pad[c, pl.ds(EDGE + r0, CHUNK), :], pltpu.roll(v, CY - 1, 1))
            before = jnp.where(first_lane, left_pad[c, pl.ds(EDGE + r0, CHUNK), :], pltpu.roll(v, 1, 1))
            along_second = after - 2.0 * v + before
            factors = [stiffness if own_axis[c] == axis_index else shear for axis_index in range(3)]
            acceleration = factors[0] * along_first + factors[1] * along_depth + factors[2] * along_second
            out_ref[c, pl.ds(r0, CHUNK), :] = 2.0 * v - prev_ref[c, pl.ds(r0, CHUNK), :] + acceleration
    for x in range(CX):
        out_ref[2, pl.ds(x * NL, 1), :] = out_ref[2, pl.ds(x * NL, 1), :] + force[x : x + 1]
    elastic_tiles(out_ref, pick_ref, tiles_ref)
    edge_rows(out_ref, edges_ref)


def shallow_kernel(cur_ref, prev_ref, coef_ref, wet_ref, low_ref, high_ref, low_rows_ref, high_rows_ref, rows_ref,
                   arrived_ref, pick_ref, out_ref, tiles_ref, edges_ref, scratch, source_ref, left_pad, right_pad):
    fill_scratch(scratch, cur_ref, low_ref, high_ref, 3)
    fill_sides(low_rows_ref, high_rows_ref, left_pad, right_pad)
    coarse_source = landing_sum(rows_ref, arrived_ref, REFINE * CX)
    for cb in range(REFINE):
        source_ref[pl.ds(cb, REFINE * CX, stride=REFINE), :] = select_dot(coarse_source, spread(cb))
    lanes = lane_index(CHUNK)
    first_lane = lanes == 0
    last_lane = lanes == CY - 1
    first_block = row_mask(0, CHUNK, REFINE, 0)
    last_block = row_mask(0, CHUNK, REFINE, REFINE - 1)
    for r0 in range(0, ROWS, CHUNK):
        at = BASE + r0

        def rows_diff(f):
            return scratch[f, pl.ds(at + REFINE, CHUNK), :] - scratch[f, pl.ds(at - REFINE, CHUNK), :]

        def columns_diff(f):
            v = scratch[f, pl.ds(at, CHUNK), :]
            wrap_after = jnp.where(last_block, right_pad[f, pl.ds(EDGE + r0 - (REFINE - 1), CHUNK), :],
                                   pltpu.roll(scratch[f, pl.ds(at + 1, CHUNK), :], CY - 1, 1))
            wrap_before = jnp.where(first_block, left_pad[f, pl.ds(EDGE + r0 + REFINE - 1, CHUNK), :],
                                    pltpu.roll(scratch[f, pl.ds(at - 1, CHUNK), :], 1, 1))
            after = jnp.where(last_lane, wrap_after, pltpu.roll(v, CY - 1, 1))
            before = jnp.where(first_lane, wrap_before, pltpu.roll(v, 1, 1))
            return after - before

        wave = coef_ref[0, pl.ds(r0, CHUNK), :]
        area = coef_ref[1, pl.ds(r0, CHUNK), :]
        wet = wet_ref[pl.ds(r0, CHUNK), :].astype(jnp.float32)
        eta_r = rows_diff(0)
        eta_c = columns_diff(0)
        out_ref[1, pl.ds(r0, CHUNK), :] = wet * (prev_ref[1, pl.ds(r0, CHUNK), :] - wave * eta_r)
        out_ref[2, pl.ds(r0, CHUNK), :] = wet * (prev_ref[2, pl.ds(r0, CHUNK), :] - wave * eta_c)
        divergence = rows_diff(1) + columns_diff(2)
        out_ref[0, pl.ds(r0, CHUNK), :] = wet * (
            prev_ref[0, pl.ds(r0, CHUNK), :] - area * divergence + source_ref[pl.ds(r0, CHUNK), :]
        )
    shallow_tiles(out_ref, pick_ref, tiles_ref)
    edge_rows(out_ref, edges_ref)


def shallow_tiles(field_ref, pick_ref, tiles_ref):
    total = jnp.zeros((REFINE * CX, CY), jnp.float32)
    for cb in range(REFINE):
        total = total + select_dot(field_ref[0, pl.ds(cb, REFINE * CX, stride=REFINE), :], spread(cb).T)
    tiles_ref[...] = exact_dot(pick_ref[...], total / REFINE)


def elastic_tiles(field_ref, pick_ref, tiles_ref):
    uplift = field_ref[2, pl.ds(0, CX, stride=NL), :]
    tiles_ref[...] = exact_dot(pick_ref[:, :CX], uplift)


def prepare_kernel(tiles_of, cur_ref, pick_ref, tiles_ref, edges_ref):
    tiles_of(cur_ref, pick_ref, tiles_ref)
    edge_rows(cur_ref, edges_ref)


def prepare(tiles_of, current, pick):
    return pl.pallas_call(
        functools.partial(prepare_kernel, tiles_of),
        out_shape=(
            jax.ShapeDtypeStruct((pick.shape[0], CY), jnp.float32),
            jax.ShapeDtypeStruct((3, 8, EDGE_LANES), jnp.float32),
        ),
        in_specs=vmem_specs(2),
        out_specs=tuple(vmem_specs(2)),
    )(current, pick)


def vmem_specs(count):
    return [pl.BlockSpec(memory_space=pltpu.VMEM)] * count


def run_step(kernel, scratch_shapes, *operands):
    slots = operands[-1].shape[0]
    return pl.pallas_call(
        kernel,
        out_shape=(
            jax.ShapeDtypeStruct((3, ROWS, CY), jnp.float32),
            jax.ShapeDtypeStruct((slots, CY), jnp.float32),
            jax.ShapeDtypeStruct((3, 8, EDGE_LANES), jnp.float32),
        ),
        in_specs=vmem_specs(len(operands)),
        out_specs=tuple(vmem_specs(3)),
        scratch_shapes=scratch_shapes,
    )(*operands)


def exchange_kernel(sizes, cur_ref, edges_ref, out_ref, in_ref, low_ref, high_ref, low_rows_ref, high_rows_ref,
                    land, halo, sides, send_sem, recv_sem, halo_send, halo_recv, side_send, side_recv):
    owners, rows_of, columns = sizes
    other = 1 - lax.axis_index("sec")
    section = lax.axis_index("sec")
    gx = lax.axis_index("gx")
    gy = lax.axis_index("gy")
    me = gx * columns + gy
    has_low = gx > 0
    has_high = gx < rows_of - 1
    has_left = gy > 0
    has_right = gy < columns - 1
    halo[...] = jnp.zeros_like(halo)
    sides[...] = jnp.zeros_like(sides)
    barrier = pltpu.get_barrier_semaphore()
    def greet(i, carry):
        d = (me + i) % owners
        pl.semaphore_signal(barrier, inc=1, device_id=(other, d // columns, d % columns),
                            device_id_type=pl.DeviceIdType.MESH)
        return carry

    lax.fori_loop(0, owners, greet, 0, unroll=8)

    @pl.when(has_low)
    def _():
        pl.semaphore_signal(barrier, inc=1, device_id=(section, gx - 1, gy), device_id_type=pl.DeviceIdType.MESH)

    @pl.when(has_high)
    def _():
        pl.semaphore_signal(barrier, inc=1, device_id=(section, gx + 1, gy), device_id_type=pl.DeviceIdType.MESH)

    @pl.when(has_left)
    def _():
        pl.semaphore_signal(barrier, inc=1, device_id=(section, gx, gy - 1), device_id_type=pl.DeviceIdType.MESH)

    @pl.when(has_right)
    def _():
        pl.semaphore_signal(barrier, inc=1, device_id=(section, gx, gy + 1), device_id_type=pl.DeviceIdType.MESH)

    neighbours = [has_low, has_high, has_left, has_right]
    pl.semaphore_wait(barrier, owners + sum(n.astype(jnp.int32) for n in neighbours))

    def side_copy(slot, target):
        return pltpu.make_async_remote_copy(
            src_ref=edges_ref,
            dst_ref=sides.at[slot],
            send_sem=side_send.at[slot],
            recv_sem=side_recv.at[slot],
            device_id=(section, gx, target),
            device_id_type=pl.DeviceIdType.MESH,
        )

    @pl.when(has_right)
    def _():
        side_copy(0, gy + 1).start()

    @pl.when(has_left)
    def _():
        side_copy(1, gy - 1).start()

    def slab_copy(start, slot, target):
        return pltpu.make_async_remote_copy(
            src_ref=cur_ref.at[:, pl.ds(start, HALO_ROWS), :],
            dst_ref=halo.at[slot],
            send_sem=halo_send.at[slot],
            recv_sem=halo_recv.at[slot],
            device_id=(section, target, gy),
            device_id_type=pl.DeviceIdType.MESH,
        )

    @pl.when(has_high)
    def _():
        slab_copy(ROWS - HALO_ROWS, 0, gx + 1).start()

    @pl.when(has_low)
    def _():
        slab_copy(0, 1, gx - 1).start()

    def send(i, carry):
        d = (me + i) % owners
        pltpu.make_async_remote_copy(
            src_ref=out_ref.at[pl.ds(d * CAP, CAP)],
            dst_ref=land.at[pl.ds(me * CAP, CAP)],
            send_sem=send_sem,
            recv_sem=recv_sem,
            device_id=(other, d // columns, d % columns),
            device_id_type=pl.DeviceIdType.MESH,
        ).start()
        return carry

    lax.fori_loop(0, owners, send, 0, unroll=8)
    whole = pltpu.make_async_remote_copy(
        src_ref=out_ref,
        dst_ref=land,
        send_sem=send_sem,
        recv_sem=recv_sem,
        device_id=(other, gx, gy),
        device_id_type=pl.DeviceIdType.MESH,
    )

    @pl.when(has_high)
    def _():
        slab_copy(ROWS - HALO_ROWS, 0, gx + 1).wait_send()
        slab_copy(0, 1, gx + 1).wait_recv()

    @pl.when(has_low)
    def _():
        slab_copy(0, 1, gx - 1).wait_send()
        slab_copy(ROWS - HALO_ROWS, 0, gx - 1).wait_recv()

    @pl.when(has_right)
    def _():
        side_copy(0, gy + 1).wait_send()
        side_copy(1, gy + 1).wait_recv()

    @pl.when(has_left)
    def _():
        side_copy(1, gy - 1).wait_send()
        side_copy(0, gy - 1).wait_recv()

    whole.wait_send()
    whole.wait_recv()
    in_ref[...] = land[...]
    low_ref[...] = halo[0]
    high_ref[...] = halo[1]
    low_rows_ref[...] = sides[0]
    high_rows_ref[...] = sides[1]


def exchange(current, edges, outgoing, owners, rows_of, columns):
    halo_shape = jax.ShapeDtypeStruct((3, HALO_ROWS, CY), jnp.float32)
    side_shape = jax.ShapeDtypeStruct(edges.shape, jnp.float32)
    return pl.pallas_call(
        functools.partial(exchange_kernel, (owners, rows_of, columns)),
        out_shape=(jax.ShapeDtypeStruct(outgoing.shape, jnp.float32), halo_shape, halo_shape, side_shape, side_shape),
        in_specs=[pl.BlockSpec(memory_space=pl.ANY)] * 2 + [pl.BlockSpec(memory_space=pltpu.VMEM)],
        out_specs=tuple(vmem_specs(5)),
        scratch_shapes=[
            pltpu.VMEM(outgoing.shape, jnp.float32),
            pltpu.VMEM((2, 3, HALO_ROWS, CY), jnp.float32),
            pltpu.VMEM((2,) + edges.shape, jnp.float32),
            pltpu.SemaphoreType.DMA(()),
            pltpu.SemaphoreType.DMA(()),
            pltpu.SemaphoreType.DMA((2,)),
            pltpu.SemaphoreType.DMA((2,)),
            pltpu.SemaphoreType.DMA((2,)),
            pltpu.SemaphoreType.DMA((2,)),
        ],
        compiler_params=pltpu.CompilerParams(collective_id=outgoing.shape[1] // CY - 1, has_side_effects=True),
    )(current, edges, outgoing)


def route(payload):
    tile_data, tile_rows = payload
    width = tile_data.shape[-1]
    received_data, received_rows = (
        lax.all_to_all(tile_data, ("gx", "gy"), split_axis=0, concat_axis=0, tiled=True),
        lax.all_to_all(tile_rows, ("gx", "gy"), split_axis=0, concat_axis=0, tiled=True),
    )
    return (received_data.reshape(-1, width), received_rows.reshape(-1))


def deliver(outgoing, send_rows):
    routed = route((outgoing, send_rows))
    return from_partner((routed[0], routed[1]), "sec", 0)


def on_device(state, previous, coeff, wet_mask, link_dest, link_rows, link_weight):
    section = lax.axis_index("sec")
    owners = lax.axis_size("gx") * lax.axis_size("gy")
    fine_rows = REFINE * CX
    current = state[0, :, 0, 0].reshape(3, ROWS, CY)
    earlier = previous[0, :, 0, 0].reshape(3, ROWS, CY)
    factors = coeff[0, :, 0, 0].reshape(2, ROWS, CY)
    wet = wet_mask[0, 0].reshape(ROWS, CY)
    targets = link_dest.reshape(-1)
    pairs = link_rows.reshape(-1, 2)
    source_rows = pairs[:, 0]
    landing = pairs[:, 1]
    weights = link_weight.reshape(-1)
    one_hot = (targets[:, None] == jnp.arange(owners, dtype=jnp.int32)[None, :]).astype(jnp.int32)
    before = jnp.cumsum(one_hot, axis=0) - one_hot
    slot_index = jnp.sum(before * one_hot, axis=1)
    position = targets * CAP + slot_index
    send_rows = jnp.zeros((owners * CAP,), jnp.int32).at[position].set(landing).reshape(owners, CAP)
    slot_rows = jnp.full((owners * CAP,), -1, jnp.int32).at[position].set(source_rows)
    slot_weights = jnp.zeros((owners * CAP,), jnp.float32).at[position].set(weights)
    pick = jnp.where(slot_rows[:, None] == jnp.arange(fine_rows, dtype=jnp.int32)[None, :], slot_weights[:, None], 0.0)
    outgoing, edges = lax.cond(
        section == 0,
        lambda: prepare(elastic_tiles, current, pick),
        lambda: prepare(shallow_tiles, current, pick),
    )
    row_lanes = jnp.broadcast_to(send_rows.reshape(-1, 1).astype(jnp.float32), (owners * CAP, CY))
    outgoing = jnp.concatenate([outgoing, row_lanes], axis=1)
    for step_index in range(STEPS):
        arrived, low_x, high_x, low_y, high_y = exchange(
            current, edges, outgoing, owners, lax.axis_size("gx"), lax.axis_size("gy")
        )
        if step_index == 0:
            arrived_rows = arrived[:, CY].astype(jnp.int32).reshape(1, -1)
            arrived = arrived[:, :CY]

        def elastic_branch():
            scratch = [
                pltpu.VMEM((3, PAD_ROWS, CY), jnp.float32),
                pltpu.VMEM((3, ROWS + 2 * EDGE, 1), jnp.float32),
                pltpu.VMEM((3, ROWS + 2 * EDGE, 1), jnp.float32),
            ]
            return run_step(elastic_kernel, scratch, current, earlier, factors, low_x, high_x, low_y, high_y,
                            arrived_rows, arrived, pick)

        def shallow_branch():
            scratch = [
                pltpu.VMEM((3, PAD_ROWS, CY), jnp.float32),
                pltpu.VMEM((ROWS, CY), jnp.float32),
                pltpu.VMEM((3, ROWS + 2 * EDGE, 1), jnp.float32),
                pltpu.VMEM((3, ROWS + 2 * EDGE, 1), jnp.float32),
            ]
            return run_step(shallow_kernel, scratch, current, earlier, factors, wet, low_x, high_x, low_y, high_y,
                            arrived_rows, arrived, pick)

        updated, outgoing, edges = lax.cond(section == 0, elastic_branch, shallow_branch)
        earlier, current = (current, updated)
    return current.reshape(1, 3, 1, 1, -1)


def solution(mesh):
    placed = (
        P("sec", None, "gx", "gy", None),
        P("sec", None, "gx", "gy", None),
        P("sec", None, "gx", "gy", None),
        P("gx", "gy", None),
        P("sec", "gx", "gy", None, None),
        P("sec", "gx", "gy", None, None),
        P("sec", "gx", "gy", None),
    )
    return jax.shard_map(
        on_device,
        mesh=mesh,
        in_specs=placed,
        out_specs=P("sec", None, "gx", "gy", None),
        check_vma=False,
    )
```

```python
import functools

import jax
import jax.numpy as jnp
from jax import lax
from jax.experimental import pallas as pl
from jax.experimental.pallas import tpu as pltpu
from jax.sharding import PartitionSpec as P

CX = 8
CY = 128
REFINE = 10
NL = 100
STEPS = 4
CAP = 4

ROWS = CX * NL
BASE = 104
PAD_ROWS = BASE + ROWS + BASE
CHUNK = 40
EDGE = 16
HALO_ROWS = NL + 4
EDGE_LANES = 896


def from_partner(value, axis, stride):
    return lax.ppermute(value, axis, [(i, i ^ 1 << stride) for i in range(lax.axis_size(axis))])


def shift_pairs(axis):
    count = lax.axis_size(axis)
    forward = [(i, i + 1) for i in range(count - 1)]
    backward = [(target, source) for source, target in forward]
    return forward, backward


def fill_scratch(scratch, cur_ref, low_ref, high_ref, fields):
    for f in range(fields):
        scratch[f, pl.ds(BASE - HALO_ROWS, HALO_ROWS), :] = low_ref[f]
        scratch[f, pl.ds(BASE, ROWS), :] = cur_ref[f]
        scratch[f, pl.ds(BASE + ROWS, HALO_ROWS), :] = high_ref[f]


def lane_index(rows):
    return lax.broadcasted_iota(jnp.int32, (rows, CY), 1)


def row_mask(r0, rows, period, phase):
    local = lax.broadcasted_iota(jnp.int32, (rows, CY), 0)
    mask = jnp.zeros((rows, CY), jnp.bool_)
    for r in range(rows):
        if (r0 + r) % period == phase:
            mask = mask | (local == r)
    return mask


def exact_dot(a, b):
    return jnp.dot(a, b, precision=lax.Precision.HIGHEST, preferred_element_type=jnp.float32)


def select_dot(a, b):
    return jnp.dot(a, b, precision=lax.Precision.HIGH, preferred_element_type=jnp.float32)


def landing_sum(rows_ref, arrived_ref, count):
    slots = rows_ref.shape[1]
    one_hot = (lax.broadcasted_iota(jnp.int32, (count, slots), 0) == rows_ref[...]).astype(jnp.float32)
    return select_dot(one_hot, arrived_ref[...])


def edge_rows(out_ref, edges_ref):
    rows = lax.broadcasted_iota(jnp.int32, (8, CY), 0)
    lanes = lax.broadcasted_iota(jnp.int32, (8, CY), 1)
    select = (((rows == 0) & (lanes == CY - 1)) | ((rows == 1) & (lanes == 0))).astype(jnp.float32)
    for f in range(3):
        picked = lax.dot_general(select, out_ref[f], (((1,), (1,)), ((), ())), precision=lax.Precision.HIGHEST,
                                 preferred_element_type=jnp.float32)
        edges_ref[f] = jnp.zeros(edges_ref.shape[1:], jnp.float32)
        edges_ref[f, :, pl.ds(0, ROWS)] = picked


def fill_sides(low_rows_ref, high_rows_ref, left_pad, right_pad):
    for f in range(3):
        left_pad[f, pl.ds(EDGE, ROWS), :] = jnp.transpose(low_rows_ref[f])[:ROWS, 0:1]
        right_pad[f, pl.ds(EDGE, ROWS), :] = jnp.transpose(high_rows_ref[f])[:ROWS, 1:2]


def spread(cb):
    coarse = lax.broadcasted_iota(jnp.int32, (CY, CY), 0)
    fine = lax.broadcasted_iota(jnp.int32, (CY, CY), 1) + cb * CY
    return ((fine >= coarse * REFINE) & (fine < coarse * REFINE + REFINE)).astype(jnp.float32)


def elastic_kernel(cur_ref, prev_ref, coef_ref, low_ref, high_ref, low_rows_ref, high_rows_ref, rows_ref, arrived_ref,
                   pick_ref, out_ref, tiles_ref, edges_ref, scratch, left_pad, right_pad):
    fill_scratch(scratch, cur_ref, low_ref, high_ref, 3)
    fill_sides(low_rows_ref, high_rows_ref, left_pad, right_pad)
    force = landing_sum(rows_ref, arrived_ref, CX)
    lanes = lane_index(CHUNK)
    first_lane = lanes == 0
    last_lane = lanes == CY - 1
    own_axis = (0, 2, 1)
    for r0 in range(0, ROWS, CHUNK):
        top_layer = row_mask(r0, CHUNK, NL, 0)
        bottom_layer = row_mask(r0, CHUNK, NL, NL - 1)
        shear = coef_ref[0, pl.ds(r0, CHUNK), :]
        lame = coef_ref[1, pl.ds(r0, CHUNK), :]
        stiffness = lame + 2.0 * shear
        for c in range(3):
            at = BASE + r0
            v = scratch[c, pl.ds(at, CHUNK), :]
            along_first = scratch[c, pl.ds(at + NL, CHUNK), :] - 2.0 * v + scratch[c, pl.ds(at - NL, CHUNK), :]
            deeper = jnp.where(bottom_layer, 0.0, scratch[c, pl.ds(at + 1, CHUNK), :])
            shallower = jnp.where(top_layer, 0.0, scratch[c, pl.ds(at - 1, CHUNK), :])
            along_depth = deeper - 2.0 * v + shallower
            after = jnp.where(last_lane, right_pad[c, pl.ds(EDGE + r0, CHUNK), :], pltpu.roll(v, CY - 1, 1))
            before = jnp.where(first_lane, left_pad[c, pl.ds(EDGE + r0, CHUNK), :], pltpu.roll(v, 1, 1))
            along_second = after - 2.0 * v + before
            factors = [stiffness if own_axis[c] == axis_index else shear for axis_index in range(3)]
            acceleration = factors[0] * along_first + factors[1] * along_depth + factors[2] * along_second
            out_ref[c, pl.ds(r0, CHUNK), :] = 2.0 * v - prev_ref[c, pl.ds(r0, CHUNK), :] + acceleration
    for x in range(CX):
        out_ref[2, pl.ds(x * NL, 1), :] = out_ref[2, pl.ds(x * NL, 1), :] + force[x : x + 1]
    elastic_tiles(out_ref, pick_ref, tiles_ref)
    edge_rows(out_ref, edges_ref)


def shallow_kernel(cur_ref, prev_ref, coef_ref, wet_ref, low_ref, high_ref, low_rows_ref, high_rows_ref, rows_ref,
                   arrived_ref, pick_ref, out_ref, tiles_ref, edges_ref, scratch, source_ref, left_pad, right_pad):
    fill_scratch(scratch, cur_ref, low_ref, high_ref, 3)
    fill_sides(low_rows_ref, high_rows_ref, left_pad, right_pad)
    coarse_source = landing_sum(rows_ref, arrived_ref, REFINE * CX)
    for cb in range(REFINE):
        source_ref[pl.ds(cb, REFINE * CX, stride=REFINE), :] = select_dot(coarse_source, spread(cb))
    lanes = lane_index(CHUNK)
    first_lane = lanes == 0
    last_lane = lanes == CY - 1
    first_block = row_mask(0, CHUNK, REFINE, 0)
    last_block = row_mask(0, CHUNK, REFINE, REFINE - 1)
    for r0 in range(0, ROWS, CHUNK):
        at = BASE + r0

        def rows_diff(f):
            return scratch[f, pl.ds(at + REFINE, CHUNK), :] - scratch[f, pl.ds(at - REFINE, CHUNK), :]

        def columns_diff(f):
            v = scratch[f, pl.ds(at, CHUNK), :]
            wrap_after = jnp.where(last_block, right_pad[f, pl.ds(EDGE + r0 - (REFINE - 1), CHUNK), :],
                                   pltpu.roll(scratch[f, pl.ds(at + 1, CHUNK), :], CY - 1, 1))
            wrap_before = jnp.where(first_block, left_pad[f, pl.ds(EDGE + r0 + REFINE - 1, CHUNK), :],
                                    pltpu.roll(scratch[f, pl.ds(at - 1, CHUNK), :], 1, 1))
            after = jnp.where(last_lane, wrap_after, pltpu.roll(v, CY - 1, 1))
            before = jnp.where(first_lane, wrap_before, pltpu.roll(v, 1, 1))
            return after - before

        wave = coef_ref[0, pl.ds(r0, CHUNK), :]
        area = coef_ref[1, pl.ds(r0, CHUNK), :]
        wet = wet_ref[pl.ds(r0, CHUNK), :].astype(jnp.float32)
        eta_r = rows_diff(0)
        eta_c = columns_diff(0)
        out_ref[1, pl.ds(r0, CHUNK), :] = wet * (prev_ref[1, pl.ds(r0, CHUNK), :] - wave * eta_r)
        out_ref[2, pl.ds(r0, CHUNK), :] = wet * (prev_ref[2, pl.ds(r0, CHUNK), :] - wave * eta_c)
        divergence = rows_diff(1) + columns_diff(2)
        out_ref[0, pl.ds(r0, CHUNK), :] = wet * (
            prev_ref[0, pl.ds(r0, CHUNK), :] - area * divergence + source_ref[pl.ds(r0, CHUNK), :]
        )
    shallow_tiles(out_ref, pick_ref, tiles_ref)
    edge_rows(out_ref, edges_ref)


def shallow_tiles(field_ref, pick_ref, tiles_ref):
    total = jnp.zeros((REFINE * CX, CY), jnp.float32)
    for cb in range(REFINE):
        total = total + select_dot(field_ref[0, pl.ds(cb, REFINE * CX, stride=REFINE), :], spread(cb).T)
    tiles_ref[...] = exact_dot(pick_ref[...], total / REFINE)


def elastic_tiles(field_ref, pick_ref, tiles_ref):
    uplift = field_ref[2, pl.ds(0, CX, stride=NL), :]
    tiles_ref[...] = exact_dot(pick_ref[:, :CX], uplift)


def prepare_kernel(tiles_of, cur_ref, pick_ref, tiles_ref, edges_ref):
    tiles_of(cur_ref, pick_ref, tiles_ref)
    edge_rows(cur_ref, edges_ref)


def prepare(tiles_of, current, pick):
    return pl.pallas_call(
        functools.partial(prepare_kernel, tiles_of),
        out_shape=(
            jax.ShapeDtypeStruct((pick.shape[0], CY), jnp.float32),
            jax.ShapeDtypeStruct((3, 8, EDGE_LANES), jnp.float32),
        ),
        in_specs=vmem_specs(2),
        out_specs=tuple(vmem_specs(2)),
    )(current, pick)


def vmem_specs(count):
    return [pl.BlockSpec(memory_space=pltpu.VMEM)] * count


def run_step(kernel, scratch_shapes, *operands):
    slots = operands[-1].shape[0]
    return pl.pallas_call(
        kernel,
        out_shape=(
            jax.ShapeDtypeStruct((3, ROWS, CY), jnp.float32),
            jax.ShapeDtypeStruct((slots, CY), jnp.float32),
            jax.ShapeDtypeStruct((3, 8, EDGE_LANES), jnp.float32),
        ),
        in_specs=vmem_specs(len(operands)),
        out_specs=tuple(vmem_specs(3)),
        scratch_shapes=scratch_shapes,
    )(*operands)


def exchange_kernel(sizes, cur_ref, edges_ref, out_ref, in_ref, low_ref, high_ref, low_rows_ref, high_rows_ref,
                    land, halo, sides, send_sem, recv_sem, halo_send, halo_recv, side_send, side_recv):
    owners, rows_of, columns = sizes
    other = 1 - lax.axis_index("sec")
    section = lax.axis_index("sec")
    gx = lax.axis_index("gx")
    gy = lax.axis_index("gy")
    me = gx * columns + gy
    has_low = gx > 0
    has_high = gx < rows_of - 1
    has_left = gy > 0
    has_right = gy < columns - 1
    halo[...] = jnp.zeros_like(halo)
    sides[...] = jnp.zeros_like(sides)
    barrier = pltpu.get_barrier_semaphore()
    def greet(d, carry):
        pl.semaphore_signal(barrier, inc=1, device_id=(other, d // columns, d % columns),
                            device_id_type=pl.DeviceIdType.MESH)
        return carry

    lax.fori_loop(0, owners, greet, 0, unroll=8)

    @pl.when(has_low)
    def _():
        pl.semaphore_signal(barrier, inc=1, device_id=(section, gx - 1, gy), device_id_type=pl.DeviceIdType.MESH)

    @pl.when(has_high)
    def _():
        pl.semaphore_signal(barrier, inc=1, device_id=(section, gx + 1, gy), device_id_type=pl.DeviceIdType.MESH)

    @pl.when(has_left)
    def _():
        pl.semaphore_signal(barrier, inc=1, device_id=(section, gx, gy - 1), device_id_type=pl.DeviceIdType.MESH)

    @pl.when(has_right)
    def _():
        pl.semaphore_signal(barrier, inc=1, device_id=(section, gx, gy + 1), device_id_type=pl.DeviceIdType.MESH)

    neighbours = [has_low, has_high, has_left, has_right]
    pl.semaphore_wait(barrier, owners + sum(n.astype(jnp.int32) for n in neighbours))

    def side_copy(slot, target):
        return pltpu.make_async_remote_copy(
            src_ref=edges_ref,
            dst_ref=sides.at[slot],
            send_sem=side_send.at[slot],
            recv_sem=side_recv.at[slot],
            device_id=(section, gx, target),
            device_id_type=pl.DeviceIdType.MESH,
        )

    @pl.when(has_right)
    def _():
        side_copy(0, gy + 1).start()

    @pl.when(has_left)
    def _():
        side_copy(1, gy - 1).start()

    def slab_copy(start, slot, target):
        return pltpu.make_async_remote_copy(
            src_ref=cur_ref.at[:, pl.ds(start, HALO_ROWS), :],
            dst_ref=halo.at[slot],
            send_sem=halo_send.at[slot],
            recv_sem=halo_recv.at[slot],
            device_id=(section, target, gy),
            device_id_type=pl.DeviceIdType.MESH,
        )

    @pl.when(has_high)
    def _():
        slab_copy(ROWS - HALO_ROWS, 0, gx + 1).start()

    @pl.when(has_low)
    def _():
        slab_copy(0, 1, gx - 1).start()

    def send(d, carry):
        pltpu.make_async_remote_copy(
            src_ref=out_ref.at[pl.ds(d * CAP, CAP)],
            dst_ref=land.at[pl.ds(me * CAP, CAP)],
            send_sem=send_sem,
            recv_sem=recv_sem,
            device_id=(other, d // columns, d % columns),
            device_id_type=pl.DeviceIdType.MESH,
        ).start()
        return carry

    lax.fori_loop(0, owners, send, 0, unroll=8)
    whole = pltpu.make_async_remote_copy(
        src_ref=out_ref,
        dst_ref=land,
        send_sem=send_sem,
        recv_sem=recv_sem,
        device_id=(other, gx, gy),
        device_id_type=pl.DeviceIdType.MESH,
    )

    @pl.when(has_high)
    def _():
        slab_copy(ROWS - HALO_ROWS, 0, gx + 1).wait_send()
        slab_copy(0, 1, gx + 1).wait_recv()

    @pl.when(has_low)
    def _():
        slab_copy(0, 1, gx - 1).wait_send()
        slab_copy(ROWS - HALO_ROWS, 0, gx - 1).wait_recv()

    @pl.when(has_right)
    def _():
        side_copy(0, gy + 1).wait_send()
        side_copy(1, gy + 1).wait_recv()

    @pl.when(has_left)
    def _():
        side_copy(1, gy - 1).wait_send()
        side_copy(0, gy - 1).wait_recv()

    whole.wait_send()
    whole.wait_recv()
    in_ref[...] = land[...]
    low_ref[...] = halo[0]
    high_ref[...] = halo[1]
    low_rows_ref[...] = sides[0]
    high_rows_ref[...] = sides[1]


def exchange(current, edges, outgoing, owners, rows_of, columns):
    halo_shape = jax.ShapeDtypeStruct((3, HALO_ROWS, CY), jnp.float32)
    side_shape = jax.ShapeDtypeStruct(edges.shape, jnp.float32)
    return pl.pallas_call(
        functools.partial(exchange_kernel, (owners, rows_of, columns)),
        out_shape=(jax.ShapeDtypeStruct(outgoing.shape, jnp.float32), halo_shape, halo_shape, side_shape, side_shape),
        in_specs=[pl.BlockSpec(memory_space=pl.ANY)] * 2 + [pl.BlockSpec(memory_space=pltpu.VMEM)],
        out_specs=tuple(vmem_specs(5)),
        scratch_shapes=[
            pltpu.VMEM(outgoing.shape, jnp.float32),
            pltpu.VMEM((2, 3, HALO_ROWS, CY), jnp.float32),
            pltpu.VMEM((2,) + edges.shape, jnp.float32),
            pltpu.SemaphoreType.DMA(()),
            pltpu.SemaphoreType.DMA(()),
            pltpu.SemaphoreType.DMA((2,)),
            pltpu.SemaphoreType.DMA((2,)),
            pltpu.SemaphoreType.DMA((2,)),
            pltpu.SemaphoreType.DMA((2,)),
        ],
        compiler_params=pltpu.CompilerParams(collective_id=outgoing.shape[1] // CY - 1, has_side_effects=True),
    )(current, edges, outgoing)


def route(payload):
    tile_data, tile_rows = payload
    width = tile_data.shape[-1]
    received_data, received_rows = (
        lax.all_to_all(tile_data, ("gx", "gy"), split_axis=0, concat_axis=0, tiled=True),
        lax.all_to_all(tile_rows, ("gx", "gy"), split_axis=0, concat_axis=0, tiled=True),
    )
    return (received_data.reshape(-1, width), received_rows.reshape(-1))


def deliver(outgoing, send_rows):
    routed = route((outgoing, send_rows))
    return from_partner((routed[0], routed[1]), "sec", 0)


def on_device(state, previous, coeff, wet_mask, link_dest, link_rows, link_weight):
    section = lax.axis_index("sec")
    owners = lax.axis_size("gx") * lax.axis_size("gy")
    fine_rows = REFINE * CX
    current = state[0, :, 0, 0].reshape(3, ROWS, CY)
    earlier = previous[0, :, 0, 0].reshape(3, ROWS, CY)
    factors = coeff[0, :, 0, 0].reshape(2, ROWS, CY)
    wet = wet_mask[0, 0].reshape(ROWS, CY)
    targets = link_dest.reshape(-1)
    pairs = link_rows.reshape(-1, 2)
    source_rows = pairs[:, 0]
    landing = pairs[:, 1]
    weights = link_weight.reshape(-1)
    one_hot = (targets[:, None] == jnp.arange(owners, dtype=jnp.int32)[None, :]).astype(jnp.int32)
    before = jnp.cumsum(one_hot, axis=0) - one_hot
    slot_index = jnp.sum(before * one_hot, axis=1)
    position = targets * CAP + slot_index
    send_rows = jnp.zeros((owners * CAP,), jnp.int32).at[position].set(landing).reshape(owners, CAP)
    slot_rows = jnp.full((owners * CAP,), -1, jnp.int32).at[position].set(source_rows)
    slot_weights = jnp.zeros((owners * CAP,), jnp.float32).at[position].set(weights)
    pick = jnp.where(slot_rows[:, None] == jnp.arange(fine_rows, dtype=jnp.int32)[None, :], slot_weights[:, None], 0.0)
    outgoing, edges = lax.cond(
        section == 0,
        lambda: prepare(elastic_tiles, current, pick),
        lambda: prepare(shallow_tiles, current, pick),
    )
    row_lanes = jnp.broadcast_to(send_rows.reshape(-1, 1).astype(jnp.float32), (owners * CAP, CY))
    outgoing = jnp.concatenate([outgoing, row_lanes], axis=1)
    for step_index in range(STEPS):
        arrived, low_x, high_x, low_y, high_y = exchange(
            current, edges, outgoing, owners, lax.axis_size("gx"), lax.axis_size("gy")
        )
        if step_index == 0:
            arrived_rows = arrived[:, CY].astype(jnp.int32).reshape(1, -1)
            arrived = arrived[:, :CY]

        def elastic_branch():
            scratch = [
                pltpu.VMEM((3, PAD_ROWS, CY), jnp.float32),
                pltpu.VMEM((3, ROWS + 2 * EDGE, 1), jnp.float32),
                pltpu.VMEM((3, ROWS + 2 * EDGE, 1), jnp.float32),
            ]
            return run_step(elastic_kernel, scratch, current, earlier, factors, low_x, high_x, low_y, high_y,
                            arrived_rows, arrived, pick)

        def shallow_branch():
            scratch = [
                pltpu.VMEM((3, PAD_ROWS, CY), jnp.float32),
                pltpu.VMEM((ROWS, CY), jnp.float32),
                pltpu.VMEM((3, ROWS + 2 * EDGE, 1), jnp.float32),
                pltpu.VMEM((3, ROWS + 2 * EDGE, 1), jnp.float32),
            ]
            return run_step(shallow_kernel, scratch, current, earlier, factors, wet, low_x, high_x, low_y, high_y,
                            arrived_rows, arrived, pick)

        updated, outgoing, edges = lax.cond(section == 0, elastic_branch, shallow_branch)
        earlier, current = (current, updated)
    return current.reshape(1, 3, 1, 1, -1)


def solution(mesh):
    placed = (
        P("sec", None, "gx", "gy", None),
        P("sec", None, "gx", "gy", None),
        P("sec", None, "gx", "gy", None),
        P("gx", "gy", None),
        P("sec", "gx", "gy", None, None),
        P("sec", "gx", "gy", None, None),
        P("sec", "gx", "gy", None),
    )
    return jax.shard_map(
        on_device,
        mesh=mesh,
        in_specs=placed,
        out_specs=P("sec", None, "gx", "gy", None),
        check_vma=False,
    )
```

```python
import functools

import jax
import jax.numpy as jnp
from jax import lax
from jax.experimental import pallas as pl
from jax.experimental.pallas import tpu as pltpu
from jax.sharding import PartitionSpec as P

CX = 8
CY = 128
REFINE = 10
NL = 100
STEPS = 4
CAP = 4

ROWS = CX * NL
BASE = 104
PAD_ROWS = BASE + ROWS + BASE
CHUNK = 40
EDGE = 16
HALO_ROWS = NL + 4
EDGE_LANES = 896


def from_partner(value, axis, stride):
    return lax.ppermute(value, axis, [(i, i ^ 1 << stride) for i in range(lax.axis_size(axis))])


def shift_pairs(axis):
    count = lax.axis_size(axis)
    forward = [(i, i + 1) for i in range(count - 1)]
    backward = [(target, source) for source, target in forward]
    return forward, backward


def fill_scratch(scratch, cur_ref, low_ref, high_ref, fields):
    for f in range(fields):
        scratch[f, pl.ds(BASE - HALO_ROWS, HALO_ROWS), :] = low_ref[f]
        scratch[f, pl.ds(BASE, ROWS), :] = cur_ref[f]
        scratch[f, pl.ds(BASE + ROWS, HALO_ROWS), :] = high_ref[f]


def lane_index(rows):
    return lax.broadcasted_iota(jnp.int32, (rows, CY), 1)


def row_mask(r0, rows, period, phase):
    local = lax.broadcasted_iota(jnp.int32, (rows, CY), 0)
    mask = jnp.zeros((rows, CY), jnp.bool_)
    for r in range(rows):
        if (r0 + r) % period == phase:
            mask = mask | (local == r)
    return mask


def exact_dot(a, b):
    return jnp.dot(a, b, precision=lax.Precision.HIGHEST, preferred_element_type=jnp.float32)


def select_dot(a, b):
    return jnp.dot(a, b, precision=lax.Precision.HIGH, preferred_element_type=jnp.float32)


def landing_sum(rows_ref, arrived_ref, count):
    slots = rows_ref.shape[1]
    one_hot = (lax.broadcasted_iota(jnp.int32, (count, slots), 0) == rows_ref[...]).astype(jnp.float32)
    return exact_dot(one_hot, arrived_ref[...])


def edge_rows(out_ref, edges_ref):
    rows = lax.broadcasted_iota(jnp.int32, (8, CY), 0)
    lanes = lax.broadcasted_iota(jnp.int32, (8, CY), 1)
    select = (((rows == 0) & (lanes == CY - 1)) | ((rows == 1) & (lanes == 0))).astype(jnp.float32)
    for f in range(3):
        picked = lax.dot_general(select, out_ref[f], (((1,), (1,)), ((), ())), precision=lax.Precision.HIGHEST,
                                 preferred_element_type=jnp.float32)
        edges_ref[f] = jnp.zeros(edges_ref.shape[1:], jnp.float32)
        edges_ref[f, :, pl.ds(0, ROWS)] = picked


def fill_sides(low_rows_ref, high_rows_ref, left_pad, right_pad):
    for f in range(3):
        left_pad[f, pl.ds(EDGE, ROWS), :] = jnp.transpose(low_rows_ref[f])[:ROWS, 0:1]
        right_pad[f, pl.ds(EDGE, ROWS), :] = jnp.transpose(high_rows_ref[f])[:ROWS, 1:2]


def spread(cb):
    coarse = lax.broadcasted_iota(jnp.int32, (CY, CY), 0)
    fine = lax.broadcasted_iota(jnp.int32, (CY, CY), 1) + cb * CY
    return ((fine >= coarse * REFINE) & (fine < coarse * REFINE + REFINE)).astype(jnp.float32)


def elastic_kernel(cur_ref, prev_ref, coef_ref, low_ref, high_ref, low_rows_ref, high_rows_ref, rows_ref, arrived_ref,
                   pick_ref, out_ref, tiles_ref, edges_ref, scratch, left_pad, right_pad):
    fill_scratch(scratch, cur_ref, low_ref, high_ref, 3)
    fill_sides(low_rows_ref, high_rows_ref, left_pad, right_pad)
    force = landing_sum(rows_ref, arrived_ref, CX)
    lanes = lane_index(CHUNK)
    first_lane = lanes == 0
    last_lane = lanes == CY - 1
    own_axis = (0, 2, 1)
    for r0 in range(0, ROWS, CHUNK):
        top_layer = row_mask(r0, CHUNK, NL, 0)
        bottom_layer = row_mask(r0, CHUNK, NL, NL - 1)
        shear = coef_ref[0, pl.ds(r0, CHUNK), :]
        lame = coef_ref[1, pl.ds(r0, CHUNK), :]
        stiffness = lame + 2.0 * shear
        for c in range(3):
            at = BASE + r0
            v = scratch[c, pl.ds(at, CHUNK), :]
            along_first = scratch[c, pl.ds(at + NL, CHUNK), :] - 2.0 * v + scratch[c, pl.ds(at - NL, CHUNK), :]
            deeper = jnp.where(bottom_layer, 0.0, scratch[c, pl.ds(at + 1, CHUNK), :])
            shallower = jnp.where(top_layer, 0.0, scratch[c, pl.ds(at - 1, CHUNK), :])
            along_depth = deeper - 2.0 * v + shallower
            after = jnp.where(last_lane, right_pad[c, pl.ds(EDGE + r0, CHUNK), :], pltpu.roll(v, CY - 1, 1))
            before = jnp.where(first_lane, left_pad[c, pl.ds(EDGE + r0, CHUNK), :], pltpu.roll(v, 1, 1))
            along_second = after - 2.0 * v + before
            factors = [stiffness if own_axis[c] == axis_index else shear for axis_index in range(3)]
            acceleration = factors[0] * along_first + factors[1] * along_depth + factors[2] * along_second
            out_ref[c, pl.ds(r0, CHUNK), :] = 2.0 * v - prev_ref[c, pl.ds(r0, CHUNK), :] + acceleration
    for x in range(CX):
        out_ref[2, pl.ds(x * NL, 1), :] = out_ref[2, pl.ds(x * NL, 1), :] + force[x : x + 1]
    elastic_tiles(out_ref, pick_ref, tiles_ref)
    edge_rows(out_ref, edges_ref)


def shallow_kernel(cur_ref, prev_hbm, coef_hbm, wet_hbm, low_ref, high_ref, low_rows_ref, high_rows_ref, rows_ref,
                   arrived_ref, pick_ref, out_ref, tiles_ref, edges_ref, scratch, source_ref, left_pad, right_pad,
                   prev_ref, coef_ref, wet_ref, load_sem):
    loads = [
        pltpu.make_async_copy(prev_hbm, prev_ref, load_sem.at[0]),
        pltpu.make_async_copy(coef_hbm, coef_ref, load_sem.at[1]),
        pltpu.make_async_copy(wet_hbm, wet_ref, load_sem.at[2]),
    ]
    for load in loads:
        load.start()
    fill_scratch(scratch, cur_ref, low_ref, high_ref, 3)
    fill_sides(low_rows_ref, high_rows_ref, left_pad, right_pad)
    coarse_source = landing_sum(rows_ref, arrived_ref, REFINE * CX)
    for cb in range(REFINE):
        source_ref[pl.ds(cb, REFINE * CX, stride=REFINE), :] = select_dot(coarse_source, spread(cb))
    for load in loads:
        load.wait()
    lanes = lane_index(CHUNK)
    first_lane = lanes == 0
    last_lane = lanes == CY - 1
    first_block = row_mask(0, CHUNK, REFINE, 0)
    last_block = row_mask(0, CHUNK, REFINE, REFINE - 1)
    for r0 in range(0, ROWS, CHUNK):
        at = BASE + r0

        def rows_diff(f):
            return scratch[f, pl.ds(at + REFINE, CHUNK), :] - scratch[f, pl.ds(at - REFINE, CHUNK), :]

        def columns_diff(f):
            v = scratch[f, pl.ds(at, CHUNK), :]
            wrap_after = jnp.where(last_block, right_pad[f, pl.ds(EDGE + r0 - (REFINE - 1), CHUNK), :],
                                   pltpu.roll(scratch[f, pl.ds(at + 1, CHUNK), :], CY - 1, 1))
            wrap_before = jnp.where(first_block, left_pad[f, pl.ds(EDGE + r0 + REFINE - 1, CHUNK), :],
                                    pltpu.roll(scratch[f, pl.ds(at - 1, CHUNK), :], 1, 1))
            after = jnp.where(last_lane, wrap_after, pltpu.roll(v, CY - 1, 1))
            before = jnp.where(first_lane, wrap_before, pltpu.roll(v, 1, 1))
            return after - before

        wave = coef_ref[0, pl.ds(r0, CHUNK), :]
        area = coef_ref[1, pl.ds(r0, CHUNK), :]
        wet = wet_ref[pl.ds(r0, CHUNK), :].astype(jnp.float32)
        eta_r = rows_diff(0)
        eta_c = columns_diff(0)
        out_ref[1, pl.ds(r0, CHUNK), :] = wet * (prev_ref[1, pl.ds(r0, CHUNK), :] - wave * eta_r)
        out_ref[2, pl.ds(r0, CHUNK), :] = wet * (prev_ref[2, pl.ds(r0, CHUNK), :] - wave * eta_c)
        divergence = rows_diff(1) + columns_diff(2)
        out_ref[0, pl.ds(r0, CHUNK), :] = wet * (
            prev_ref[0, pl.ds(r0, CHUNK), :] - area * divergence + source_ref[pl.ds(r0, CHUNK), :]
        )
    shallow_tiles(out_ref, pick_ref, tiles_ref)
    edge_rows(out_ref, edges_ref)


def shallow_tiles(field_ref, pick_ref, tiles_ref):
    total = jnp.zeros((REFINE * CX, CY), jnp.float32)
    for cb in range(REFINE):
        total = total + select_dot(field_ref[0, pl.ds(cb, REFINE * CX, stride=REFINE), :], spread(cb).T)
    tiles_ref[...] = exact_dot(pick_ref[...], total / REFINE)


def elastic_tiles(field_ref, pick_ref, tiles_ref):
    uplift = field_ref[2, pl.ds(0, CX, stride=NL), :]
    tiles_ref[...] = exact_dot(pick_ref[:, :CX], uplift)


def prepare_kernel(tiles_of, cur_ref, pick_ref, tiles_ref, edges_ref):
    tiles_of(cur_ref, pick_ref, tiles_ref)
    edge_rows(cur_ref, edges_ref)


def prepare(tiles_of, current, pick):
    return pl.pallas_call(
        functools.partial(prepare_kernel, tiles_of),
        out_shape=(
            jax.ShapeDtypeStruct((pick.shape[0], CY), jnp.float32),
            jax.ShapeDtypeStruct((3, 8, EDGE_LANES), jnp.float32),
        ),
        in_specs=vmem_specs(2),
        out_specs=tuple(vmem_specs(2)),
    )(current, pick)


def vmem_specs(count):
    return [pl.BlockSpec(memory_space=pltpu.VMEM)] * count


def run_step(kernel, scratch_shapes, *operands, in_hbm=()):
    slots = operands[-1].shape[0]
    specs = [pl.BlockSpec(memory_space=pl.ANY) if i in in_hbm else pl.BlockSpec(memory_space=pltpu.VMEM)
             for i in range(len(operands))]
    return pl.pallas_call(
        kernel,
        out_shape=(
            jax.ShapeDtypeStruct((3, ROWS, CY), jnp.float32),
            jax.ShapeDtypeStruct((slots, CY), jnp.float32),
            jax.ShapeDtypeStruct((3, 8, EDGE_LANES), jnp.float32),
        ),
        in_specs=specs,
        out_specs=tuple(vmem_specs(3)),
        scratch_shapes=scratch_shapes,
    )(*operands)


def exchange_kernel(sizes, cur_ref, edges_ref, out_ref, in_ref, low_ref, high_ref, low_rows_ref, high_rows_ref,
                    land, halo, sides, send_sem, recv_sem, halo_send, halo_recv, side_send, side_recv):
    owners, rows_of, columns = sizes
    other = 1 - lax.axis_index("sec")
    section = lax.axis_index("sec")
    gx = lax.axis_index("gx")
    gy = lax.axis_index("gy")
    me = gx * columns + gy
    has_low = gx > 0
    has_high = gx < rows_of - 1
    has_left = gy > 0
    has_right = gy < columns - 1
    halo[...] = jnp.zeros_like(halo)
    sides[...] = jnp.zeros_like(sides)
    barrier = pltpu.get_barrier_semaphore()
    def greet(d, carry):
        pl.semaphore_signal(barrier, inc=1, device_id=(other, d // columns, d % columns),
                            device_id_type=pl.DeviceIdType.MESH)
        return carry

    lax.fori_loop(0, owners, greet, 0, unroll=8)

    @pl.when(has_low)
    def _():
        pl.semaphore_signal(barrier, inc=1, device_id=(section, gx - 1, gy), device_id_type=pl.DeviceIdType.MESH)

    @pl.when(has_high)
    def _():
        pl.semaphore_signal(barrier, inc=1, device_id=(section, gx + 1, gy), device_id_type=pl.DeviceIdType.MESH)

    @pl.when(has_left)
    def _():
        pl.semaphore_signal(barrier, inc=1, device_id=(section, gx, gy - 1), device_id_type=pl.DeviceIdType.MESH)

    @pl.when(has_right)
    def _():
        pl.semaphore_signal(barrier, inc=1, device_id=(section, gx, gy + 1), device_id_type=pl.DeviceIdType.MESH)

    neighbours = [has_low, has_high, has_left, has_right]
    pl.semaphore_wait(barrier, owners + sum(n.astype(jnp.int32) for n in neighbours))

    def side_copy(slot, target):
        return pltpu.make_async_remote_copy(
            src_ref=edges_ref,
            dst_ref=sides.at[slot],
            send_sem=side_send.at[slot],
            recv_sem=side_recv.at[slot],
            device_id=(section, gx, target),
            device_id_type=pl.DeviceIdType.MESH,
        )

    @pl.when(has_right)
    def _():
        side_copy(0, gy + 1).start()

    @pl.when(has_left)
    def _():
        side_copy(1, gy - 1).start()

    def slab_copy(start, slot, target):
        return pltpu.make_async_remote_copy(
            src_ref=cur_ref.at[:, pl.ds(start, HALO_ROWS), :],
            dst_ref=halo.at[slot],
            send_sem=halo_send.at[slot],
            recv_sem=halo_recv.at[slot],
            device_id=(section, target, gy),
            device_id_type=pl.DeviceIdType.MESH,
        )

    @pl.when(has_high)
    def _():
        slab_copy(ROWS - HALO_ROWS, 0, gx + 1).start()

    @pl.when(has_low)
    def _():
        slab_copy(0, 1, gx - 1).start()

    def send(d, carry):
        pltpu.make_async_remote_copy(
            src_ref=out_ref.at[pl.ds(d * CAP, CAP)],
            dst_ref=land.at[pl.ds(me * CAP, CAP)],
            send_sem=send_sem,
            recv_sem=recv_sem,
            device_id=(other, d // columns, d % columns),
            device_id_type=pl.DeviceIdType.MESH,
        ).start()
        return carry

    lax.fori_loop(0, owners, send, 0, unroll=8)
    whole = pltpu.make_async_remote_copy(
        src_ref=out_ref,
        dst_ref=land,
        send_sem=send_sem,
        recv_sem=recv_sem,
        device_id=(other, gx, gy),
        device_id_type=pl.DeviceIdType.MESH,
    )

    @pl.when(has_high)
    def _():
        slab_copy(ROWS - HALO_ROWS, 0, gx + 1).wait_send()
        slab_copy(0, 1, gx + 1).wait_recv()

    @pl.when(has_low)
    def _():
        slab_copy(0, 1, gx - 1).wait_send()
        slab_copy(ROWS - HALO_ROWS, 0, gx - 1).wait_recv()

    @pl.when(has_right)
    def _():
        side_copy(0, gy + 1).wait_send()
        side_copy(1, gy + 1).wait_recv()

    @pl.when(has_left)
    def _():
        side_copy(1, gy - 1).wait_send()
        side_copy(0, gy - 1).wait_recv()

    whole.wait_send()
    whole.wait_recv()
    in_ref[...] = land[...]
    low_ref[...] = halo[0]
    high_ref[...] = halo[1]
    low_rows_ref[...] = sides[0]
    high_rows_ref[...] = sides[1]


def exchange(current, edges, outgoing, owners, rows_of, columns):
    halo_shape = jax.ShapeDtypeStruct((3, HALO_ROWS, CY), jnp.float32)
    side_shape = jax.ShapeDtypeStruct(edges.shape, jnp.float32)
    return pl.pallas_call(
        functools.partial(exchange_kernel, (owners, rows_of, columns)),
        out_shape=(jax.ShapeDtypeStruct(outgoing.shape, jnp.float32), halo_shape, halo_shape, side_shape, side_shape),
        in_specs=[pl.BlockSpec(memory_space=pl.ANY)] * 2 + [pl.BlockSpec(memory_space=pltpu.VMEM)],
        out_specs=tuple(vmem_specs(5)),
        scratch_shapes=[
            pltpu.VMEM(outgoing.shape, jnp.float32),
            pltpu.VMEM((2, 3, HALO_ROWS, CY), jnp.float32),
            pltpu.VMEM((2,) + edges.shape, jnp.float32),
            pltpu.SemaphoreType.DMA(()),
            pltpu.SemaphoreType.DMA(()),
            pltpu.SemaphoreType.DMA((2,)),
            pltpu.SemaphoreType.DMA((2,)),
            pltpu.SemaphoreType.DMA((2,)),
            pltpu.SemaphoreType.DMA((2,)),
        ],
        compiler_params=pltpu.CompilerParams(collective_id=outgoing.shape[1] // CY - 1, has_side_effects=True),
    )(current, edges, outgoing)


def route(payload):
    tile_data, tile_rows = payload
    width = tile_data.shape[-1]
    received_data, received_rows = (
        lax.all_to_all(tile_data, ("gx", "gy"), split_axis=0, concat_axis=0, tiled=True),
        lax.all_to_all(tile_rows, ("gx", "gy"), split_axis=0, concat_axis=0, tiled=True),
    )
    return (received_data.reshape(-1, width), received_rows.reshape(-1))


def deliver(outgoing, send_rows):
    routed = route((outgoing, send_rows))
    return from_partner((routed[0], routed[1]), "sec", 0)


def on_device(state, previous, coeff, wet_mask, link_dest, link_rows, link_weight):
    section = lax.axis_index("sec")
    owners = lax.axis_size("gx") * lax.axis_size("gy")
    fine_rows = REFINE * CX
    current = state[0, :, 0, 0].reshape(3, ROWS, CY)
    earlier = previous[0, :, 0, 0].reshape(3, ROWS, CY)
    factors = coeff[0, :, 0, 0].reshape(2, ROWS, CY)
    wet = wet_mask[0, 0].reshape(ROWS, CY)
    targets = link_dest.reshape(-1)
    pairs = link_rows.reshape(-1, 2)
    source_rows = pairs[:, 0]
    landing = pairs[:, 1]
    weights = link_weight.reshape(-1)
    one_hot = (targets[:, None] == jnp.arange(owners, dtype=jnp.int32)[None, :]).astype(jnp.int32)
    before = jnp.cumsum(one_hot, axis=0) - one_hot
    slot_index = jnp.sum(before * one_hot, axis=1)
    position = targets * CAP + slot_index
    send_rows = jnp.zeros((owners * CAP,), jnp.int32).at[position].set(landing).reshape(owners, CAP)
    slot_rows = jnp.full((owners * CAP,), -1, jnp.int32).at[position].set(source_rows)
    slot_weights = jnp.zeros((owners * CAP,), jnp.float32).at[position].set(weights)
    pick = jnp.where(slot_rows[:, None] == jnp.arange(fine_rows, dtype=jnp.int32)[None, :], slot_weights[:, None], 0.0)
    outgoing, edges = lax.cond(
        section == 0,
        lambda: prepare(elastic_tiles, current, pick),
        lambda: prepare(shallow_tiles, current, pick),
    )
    row_lanes = jnp.broadcast_to(send_rows.reshape(-1, 1).astype(jnp.float32), (owners * CAP, CY))
    outgoing = jnp.concatenate([outgoing, row_lanes], axis=1)
    for step_index in range(STEPS):
        arrived, low_x, high_x, low_y, high_y = exchange(
            current, edges, outgoing, owners, lax.axis_size("gx"), lax.axis_size("gy")
        )
        if step_index == 0:
            arrived_rows = arrived[:, CY].astype(jnp.int32).reshape(1, -1)
            arrived = arrived[:, :CY]

        def elastic_branch():
            scratch = [
                pltpu.VMEM((3, PAD_ROWS, CY), jnp.float32),
                pltpu.VMEM((3, ROWS + 2 * EDGE, 1), jnp.float32),
                pltpu.VMEM((3, ROWS + 2 * EDGE, 1), jnp.float32),
            ]
            return run_step(elastic_kernel, scratch, current, earlier, factors, low_x, high_x, low_y, high_y,
                            arrived_rows, arrived, pick)

        def shallow_branch():
            scratch = [
                pltpu.VMEM((3, PAD_ROWS, CY), jnp.float32),
                pltpu.VMEM((ROWS, CY), jnp.float32),
                pltpu.VMEM((3, ROWS + 2 * EDGE, 1), jnp.float32),
                pltpu.VMEM((3, ROWS + 2 * EDGE, 1), jnp.float32),
                pltpu.VMEM((3, ROWS, CY), jnp.float32),
                pltpu.VMEM((2, ROWS, CY), jnp.float32),
                pltpu.VMEM((ROWS, CY), jnp.int32),
                pltpu.SemaphoreType.DMA((3,)),
            ]
            return run_step(shallow_kernel, scratch, current, earlier, factors, wet, low_x, high_x, low_y, high_y,
                            arrived_rows, arrived, pick, in_hbm=(1, 2, 3))

        updated, outgoing, edges = lax.cond(section == 0, elastic_branch, shallow_branch)
        earlier, current = (current, updated)
    return current.reshape(1, 3, 1, 1, -1)


def solution(mesh):
    placed = (
        P("sec", None, "gx", "gy", None),
        P("sec", None, "gx", "gy", None),
        P("sec", None, "gx", "gy", None),
        P("gx", "gy", None),
        P("sec", "gx", "gy", None, None),
        P("sec", "gx", "gy", None, None),
        P("sec", "gx", "gy", None),
    )
    return jax.shard_map(
        on_device,
        mesh=mesh,
        in_specs=placed,
        out_specs=P("sec", None, "gx", "gy", None),
        check_vma=False,
    )
```

```python
import functools

import jax
import jax.numpy as jnp
from jax import lax
from jax.experimental import pallas as pl
from jax.experimental.pallas import tpu as pltpu
from jax.sharding import PartitionSpec as P

CX = 8
CY = 128
REFINE = 10
NL = 100
STEPS = 4
CAP = 4

ROWS = CX * NL
BASE = 104
PAD_ROWS = BASE + ROWS + BASE
CHUNK = 80
EDGE = 16
HALO_ROWS = NL + 4
EDGE_LANES = 896


def from_partner(value, axis, stride):
    return lax.ppermute(value, axis, [(i, i ^ 1 << stride) for i in range(lax.axis_size(axis))])


def shift_pairs(axis):
    count = lax.axis_size(axis)
    forward = [(i, i + 1) for i in range(count - 1)]
    backward = [(target, source) for source, target in forward]
    return forward, backward


def fill_scratch(scratch, cur_ref, low_ref, high_ref, fields):
    for f in range(fields):
        scratch[f, pl.ds(BASE - HALO_ROWS, HALO_ROWS), :] = low_ref[f]
        scratch[f, pl.ds(BASE, ROWS), :] = cur_ref[f]
        scratch[f, pl.ds(BASE + ROWS, HALO_ROWS), :] = high_ref[f]


def lane_index(rows):
    return lax.broadcasted_iota(jnp.int32, (rows, CY), 1)


def row_mask(r0, rows, period, phase):
    local = lax.broadcasted_iota(jnp.int32, (rows, CY), 0)
    mask = jnp.zeros((rows, CY), jnp.bool_)
    for r in range(rows):
        if (r0 + r) % period == phase:
            mask = mask | (local == r)
    return mask


def exact_dot(a, b):
    return jnp.dot(a, b, precision=lax.Precision.HIGHEST, preferred_element_type=jnp.float32)


def select_dot(a, b):
    return jnp.dot(a, b, precision=lax.Precision.HIGH, preferred_element_type=jnp.float32)


def landing_sum(rows_ref, arrived_ref, count):
    slots = rows_ref.shape[1]
    one_hot = (lax.broadcasted_iota(jnp.int32, (count, slots), 0) == rows_ref[...]).astype(jnp.float32)
    return exact_dot(one_hot, arrived_ref[...])


def edge_rows(out_ref, edges_ref):
    rows = lax.broadcasted_iota(jnp.int32, (8, CY), 0)
    lanes = lax.broadcasted_iota(jnp.int32, (8, CY), 1)
    select = (((rows == 0) & (lanes == CY - 1)) | ((rows == 1) & (lanes == 0))).astype(jnp.float32)
    for f in range(3):
        picked = lax.dot_general(select, out_ref[f], (((1,), (1,)), ((), ())), precision=lax.Precision.HIGHEST,
                                 preferred_element_type=jnp.float32)
        edges_ref[f] = jnp.zeros(edges_ref.shape[1:], jnp.float32)
        edges_ref[f, :, pl.ds(0, ROWS)] = picked


def fill_sides(low_rows_ref, high_rows_ref, left_pad, right_pad):
    for f in range(3):
        left_pad[f, pl.ds(EDGE, ROWS), :] = jnp.transpose(low_rows_ref[f])[:ROWS, 0:1]
        right_pad[f, pl.ds(EDGE, ROWS), :] = jnp.transpose(high_rows_ref[f])[:ROWS, 1:2]


def spread(cb):
    coarse = lax.broadcasted_iota(jnp.int32, (CY, CY), 0)
    fine = lax.broadcasted_iota(jnp.int32, (CY, CY), 1) + cb * CY
    return ((fine >= coarse * REFINE) & (fine < coarse * REFINE + REFINE)).astype(jnp.float32)


def elastic_kernel(cur_ref, prev_ref, coef_ref, low_ref, high_ref, low_rows_ref, high_rows_ref, rows_ref, arrived_ref,
                   pick_ref, out_ref, tiles_ref, edges_ref, scratch, left_pad, right_pad):
    fill_scratch(scratch, cur_ref, low_ref, high_ref, 3)
    fill_sides(low_rows_ref, high_rows_ref, left_pad, right_pad)
    force = landing_sum(rows_ref, arrived_ref, CX)
    lanes = lane_index(CHUNK)
    first_lane = lanes == 0
    last_lane = lanes == CY - 1
    own_axis = (0, 2, 1)
    for r0 in range(0, ROWS, CHUNK):
        top_layer = row_mask(r0, CHUNK, NL, 0)
        bottom_layer = row_mask(r0, CHUNK, NL, NL - 1)
        shear = coef_ref[0, pl.ds(r0, CHUNK), :]
        lame = coef_ref[1, pl.ds(r0, CHUNK), :]
        stiffness = lame + 2.0 * shear
        for c in range(3):
            at = BASE + r0
            v = scratch[c, pl.ds(at, CHUNK), :]
            along_first = scratch[c, pl.ds(at + NL, CHUNK), :] - 2.0 * v + scratch[c, pl.ds(at - NL, CHUNK), :]
            deeper = jnp.where(bottom_layer, 0.0, scratch[c, pl.ds(at + 1, CHUNK), :])
            shallower = jnp.where(top_layer, 0.0, scratch[c, pl.ds(at - 1, CHUNK), :])
            along_depth = deeper - 2.0 * v + shallower
            after = jnp.where(last_lane, right_pad[c, pl.ds(EDGE + r0, CHUNK), :], pltpu.roll(v, CY - 1, 1))
            before = jnp.where(first_lane, left_pad[c, pl.ds(EDGE + r0, CHUNK), :], pltpu.roll(v, 1, 1))
            along_second = after - 2.0 * v + before
            factors = [stiffness if own_axis[c] == axis_index else shear for axis_index in range(3)]
            acceleration = factors[0] * along_first + factors[1] * along_depth + factors[2] * along_second
            out_ref[c, pl.ds(r0, CHUNK), :] = 2.0 * v - prev_ref[c, pl.ds(r0, CHUNK), :] + acceleration
    for x in range(CX):
        out_ref[2, pl.ds(x * NL, 1), :] = out_ref[2, pl.ds(x * NL, 1), :] + force[x : x + 1]
    elastic_tiles(out_ref, pick_ref, tiles_ref)
    edge_rows(out_ref, edges_ref)


def shallow_kernel(cur_ref, prev_ref, coef_ref, wet_ref, low_ref, high_ref, low_rows_ref, high_rows_ref, rows_ref,
                   arrived_ref, pick_ref, out_ref, tiles_ref, edges_ref, scratch, source_ref, left_pad, right_pad):
    fill_scratch(scratch, cur_ref, low_ref, high_ref, 3)
    fill_sides(low_rows_ref, high_rows_ref, left_pad, right_pad)
    coarse_source = landing_sum(rows_ref, arrived_ref, REFINE * CX)
    for cb in range(REFINE):
        source_ref[pl.ds(cb, REFINE * CX, stride=REFINE), :] = select_dot(coarse_source, spread(cb))
    lanes = lane_index(CHUNK)
    first_lane = lanes == 0
    last_lane = lanes == CY - 1
    first_block = row_mask(0, CHUNK, REFINE, 0)
    last_block = row_mask(0, CHUNK, REFINE, REFINE - 1)
    for r0 in range(0, ROWS, CHUNK):
        at = BASE + r0

        def rows_diff(f):
            return scratch[f, pl.ds(at + REFINE, CHUNK), :] - scratch[f, pl.ds(at - REFINE, CHUNK), :]

        def columns_diff(f):
            v = scratch[f, pl.ds(at, CHUNK), :]
            wrap_after = jnp.where(last_block, right_pad[f, pl.ds(EDGE + r0 - (REFINE - 1), CHUNK), :],
                                   pltpu.roll(scratch[f, pl.ds(at + 1, CHUNK), :], CY - 1, 1))
            wrap_before = jnp.where(first_block, left_pad[f, pl.ds(EDGE + r0 + REFINE - 1, CHUNK), :],
                                    pltpu.roll(scratch[f, pl.ds(at - 1, CHUNK), :], 1, 1))
            after = jnp.where(last_lane, wrap_after, pltpu.roll(v, CY - 1, 1))
            before = jnp.where(first_lane, wrap_before, pltpu.roll(v, 1, 1))
            return after - before

        wave = coef_ref[0, pl.ds(r0, CHUNK), :]
        area = coef_ref[1, pl.ds(r0, CHUNK), :]
        wet = wet_ref[pl.ds(r0, CHUNK), :].astype(jnp.float32)
        eta_r = rows_diff(0)
        eta_c = columns_diff(0)
        out_ref[1, pl.ds(r0, CHUNK), :] = wet * (prev_ref[1, pl.ds(r0, CHUNK), :] - wave * eta_r)
        out_ref[2, pl.ds(r0, CHUNK), :] = wet * (prev_ref[2, pl.ds(r0, CHUNK), :] - wave * eta_c)
        divergence = rows_diff(1) + columns_diff(2)
        out_ref[0, pl.ds(r0, CHUNK), :] = wet * (
            prev_ref[0, pl.ds(r0, CHUNK), :] - area * divergence + source_ref[pl.ds(r0, CHUNK), :]
        )
    shallow_tiles(out_ref, pick_ref, tiles_ref)
    edge_rows(out_ref, edges_ref)


def shallow_tiles(field_ref, pick_ref, tiles_ref):
    total = jnp.zeros((REFINE * CX, CY), jnp.float32)
    for cb in range(REFINE):
        total = total + select_dot(field_ref[0, pl.ds(cb, REFINE * CX, stride=REFINE), :], spread(cb).T)
    tiles_ref[...] = exact_dot(pick_ref[...], total / REFINE)


def elastic_tiles(field_ref, pick_ref, tiles_ref):
    uplift = field_ref[2, pl.ds(0, CX, stride=NL), :]
    tiles_ref[...] = exact_dot(pick_ref[:, :CX], uplift)


def prepare_kernel(tiles_of, cur_ref, pick_ref, tiles_ref, edges_ref):
    tiles_of(cur_ref, pick_ref, tiles_ref)
    edge_rows(cur_ref, edges_ref)


def prepare(tiles_of, current, pick):
    return pl.pallas_call(
        functools.partial(prepare_kernel, tiles_of),
        out_shape=(
            jax.ShapeDtypeStruct((pick.shape[0], CY), jnp.float32),
            jax.ShapeDtypeStruct((3, 8, EDGE_LANES), jnp.float32),
        ),
        in_specs=vmem_specs(2),
        out_specs=tuple(vmem_specs(2)),
    )(current, pick)


def vmem_specs(count):
    return [pl.BlockSpec(memory_space=pltpu.VMEM)] * count


def run_step(kernel, scratch_shapes, *operands):
    slots = operands[-1].shape[0]
    return pl.pallas_call(
        kernel,
        out_shape=(
            jax.ShapeDtypeStruct((3, ROWS, CY), jnp.float32),
            jax.ShapeDtypeStruct((slots, CY), jnp.float32),
            jax.ShapeDtypeStruct((3, 8, EDGE_LANES), jnp.float32),
        ),
        in_specs=vmem_specs(len(operands)),
        out_specs=tuple(vmem_specs(3)),
        scratch_shapes=scratch_shapes,
    )(*operands)


def exchange_kernel(sizes, cur_ref, edges_ref, out_ref, in_ref, low_ref, high_ref, low_rows_ref, high_rows_ref,
                    land, halo, sides, send_sem, recv_sem, halo_send, halo_recv, side_send, side_recv):
    owners, rows_of, columns = sizes
    other = 1 - lax.axis_index("sec")
    section = lax.axis_index("sec")
    gx = lax.axis_index("gx")
    gy = lax.axis_index("gy")
    me = gx * columns + gy
    has_low = gx > 0
    has_high = gx < rows_of - 1
    has_left = gy > 0
    has_right = gy < columns - 1
    halo[...] = jnp.zeros_like(halo)
    sides[...] = jnp.zeros_like(sides)
    barrier = pltpu.get_barrier_semaphore()
    def greet(d, carry):
        pl.semaphore_signal(barrier, inc=1, device_id=(other, d // columns, d % columns),
                            device_id_type=pl.DeviceIdType.MESH)
        return carry

    lax.fori_loop(0, owners, greet, 0, unroll=8)

    @pl.when(has_low)
    def _():
        pl.semaphore_signal(barrier, inc=1, device_id=(section, gx - 1, gy), device_id_type=pl.DeviceIdType.MESH)

    @pl.when(has_high)
    def _():
        pl.semaphore_signal(barrier, inc=1, device_id=(section, gx + 1, gy), device_id_type=pl.DeviceIdType.MESH)

    @pl.when(has_left)
    def _():
        pl.semaphore_signal(barrier, inc=1, device_id=(section, gx, gy - 1), device_id_type=pl.DeviceIdType.MESH)

    @pl.when(has_right)
    def _():
        pl.semaphore_signal(barrier, inc=1, device_id=(section, gx, gy + 1), device_id_type=pl.DeviceIdType.MESH)

    neighbours = [has_low, has_high, has_left, has_right]
    pl.semaphore_wait(barrier, owners + sum(n.astype(jnp.int32) for n in neighbours))

    def side_copy(slot, target):
        return pltpu.make_async_remote_copy(
            src_ref=edges_ref,
            dst_ref=sides.at[slot],
            send_sem=side_send.at[slot],
            recv_sem=side_recv.at[slot],
            device_id=(section, gx, target),
            device_id_type=pl.DeviceIdType.MESH,
        )

    @pl.when(has_right)
    def _():
        side_copy(0, gy + 1).start()

    @pl.when(has_left)
    def _():
        side_copy(1, gy - 1).start()

    def slab_copy(start, slot, target):
        return pltpu.make_async_remote_copy(
            src_ref=cur_ref.at[:, pl.ds(start, HALO_ROWS), :],
            dst_ref=halo.at[slot],
            send_sem=halo_send.at[slot],
            recv_sem=halo_recv.at[slot],
            device_id=(section, target, gy),
            device_id_type=pl.DeviceIdType.MESH,
        )

    @pl.when(has_high)
    def _():
        slab_copy(ROWS - HALO_ROWS, 0, gx + 1).start()

    @pl.when(has_low)
    def _():
        slab_copy(0, 1, gx - 1).start()

    def send(d, carry):
        pltpu.make_async_remote_copy(
            src_ref=out_ref.at[pl.ds(d * CAP, CAP)],
            dst_ref=land.at[pl.ds(me * CAP, CAP)],
            send_sem=send_sem,
            recv_sem=recv_sem,
            device_id=(other, d // columns, d % columns),
            device_id_type=pl.DeviceIdType.MESH,
        ).start()
        return carry

    lax.fori_loop(0, owners, send, 0, unroll=8)
    whole = pltpu.make_async_remote_copy(
        src_ref=out_ref,
        dst_ref=land,
        send_sem=send_sem,
        recv_sem=recv_sem,
        device_id=(other, gx, gy),
        device_id_type=pl.DeviceIdType.MESH,
    )

    @pl.when(has_high)
    def _():
        slab_copy(ROWS - HALO_ROWS, 0, gx + 1).wait_send()
        slab_copy(0, 1, gx + 1).wait_recv()

    @pl.when(has_low)
    def _():
        slab_copy(0, 1, gx - 1).wait_send()
        slab_copy(ROWS - HALO_ROWS, 0, gx - 1).wait_recv()

    @pl.when(has_right)
    def _():
        side_copy(0, gy + 1).wait_send()
        side_copy(1, gy + 1).wait_recv()

    @pl.when(has_left)
    def _():
        side_copy(1, gy - 1).wait_send()
        side_copy(0, gy - 1).wait_recv()

    whole.wait_send()
    whole.wait_recv()
    in_ref[...] = land[...]
    low_ref[...] = halo[0]
    high_ref[...] = halo[1]
    low_rows_ref[...] = sides[0]
    high_rows_ref[...] = sides[1]


def exchange(current, edges, outgoing, owners, rows_of, columns):
    halo_shape = jax.ShapeDtypeStruct((3, HALO_ROWS, CY), jnp.float32)
    side_shape = jax.ShapeDtypeStruct(edges.shape, jnp.float32)
    return pl.pallas_call(
        functools.partial(exchange_kernel, (owners, rows_of, columns)),
        out_shape=(jax.ShapeDtypeStruct(outgoing.shape, jnp.float32), halo_shape, halo_shape, side_shape, side_shape),
        in_specs=[pl.BlockSpec(memory_space=pl.ANY)] * 2 + [pl.BlockSpec(memory_space=pltpu.VMEM)],
        out_specs=tuple(vmem_specs(5)),
        scratch_shapes=[
            pltpu.VMEM(outgoing.shape, jnp.float32),
            pltpu.VMEM((2, 3, HALO_ROWS, CY), jnp.float32),
            pltpu.VMEM((2,) + edges.shape, jnp.float32),
            pltpu.SemaphoreType.DMA(()),
            pltpu.SemaphoreType.DMA(()),
            pltpu.SemaphoreType.DMA((2,)),
            pltpu.SemaphoreType.DMA((2,)),
            pltpu.SemaphoreType.DMA((2,)),
            pltpu.SemaphoreType.DMA((2,)),
        ],
        compiler_params=pltpu.CompilerParams(collective_id=outgoing.shape[1] // CY - 1, has_side_effects=True),
    )(current, edges, outgoing)


def route(payload):
    tile_data, tile_rows = payload
    width = tile_data.shape[-1]
    received_data, received_rows = (
        lax.all_to_all(tile_data, ("gx", "gy"), split_axis=0, concat_axis=0, tiled=True),
        lax.all_to_all(tile_rows, ("gx", "gy"), split_axis=0, concat_axis=0, tiled=True),
    )
    return (received_data.reshape(-1, width), received_rows.reshape(-1))


def deliver(outgoing, send_rows):
    routed = route((outgoing, send_rows))
    return from_partner((routed[0], routed[1]), "sec", 0)


def on_device(state, previous, coeff, wet_mask, link_dest, link_rows, link_weight):
    section = lax.axis_index("sec")
    owners = lax.axis_size("gx") * lax.axis_size("gy")
    fine_rows = REFINE * CX
    current = state[0, :, 0, 0].reshape(3, ROWS, CY)
    earlier = previous[0, :, 0, 0].reshape(3, ROWS, CY)
    factors = coeff[0, :, 0, 0].reshape(2, ROWS, CY)
    wet = wet_mask[0, 0].reshape(ROWS, CY)
    targets = link_dest.reshape(-1)
    pairs = link_rows.reshape(-1, 2)
    source_rows = pairs[:, 0]
    landing = pairs[:, 1]
    weights = link_weight.reshape(-1)
    one_hot = (targets[:, None] == jnp.arange(owners, dtype=jnp.int32)[None, :]).astype(jnp.int32)
    before = jnp.cumsum(one_hot, axis=0) - one_hot
    slot_index = jnp.sum(before * one_hot, axis=1)
    position = targets * CAP + slot_index
    send_rows = jnp.zeros((owners * CAP,), jnp.int32).at[position].set(landing).reshape(owners, CAP)
    slot_rows = jnp.full((owners * CAP,), -1, jnp.int32).at[position].set(source_rows)
    slot_weights = jnp.zeros((owners * CAP,), jnp.float32).at[position].set(weights)
    pick = jnp.where(slot_rows[:, None] == jnp.arange(fine_rows, dtype=jnp.int32)[None, :], slot_weights[:, None], 0.0)
    outgoing, edges = lax.cond(
        section == 0,
        lambda: prepare(elastic_tiles, current, pick),
        lambda: prepare(shallow_tiles, current, pick),
    )
    row_lanes = jnp.broadcast_to(send_rows.reshape(-1, 1).astype(jnp.float32), (owners * CAP, CY))
    outgoing = jnp.concatenate([outgoing, row_lanes], axis=1)
    for step_index in range(STEPS):
        arrived, low_x, high_x, low_y, high_y = exchange(
            current, edges, outgoing, owners, lax.axis_size("gx"), lax.axis_size("gy")
        )
        if step_index == 0:
            arrived_rows = arrived[:, CY].astype(jnp.int32).reshape(1, -1)
            arrived = arrived[:, :CY]

        def elastic_branch():
            scratch = [
                pltpu.VMEM((3, PAD_ROWS, CY), jnp.float32),
                pltpu.VMEM((3, ROWS + 2 * EDGE, 1), jnp.float32),
                pltpu.VMEM((3, ROWS + 2 * EDGE, 1), jnp.float32),
            ]
            return run_step(elastic_kernel, scratch, current, earlier, factors, low_x, high_x, low_y, high_y,
                            arrived_rows, arrived, pick)

        def shallow_branch():
            scratch = [
                pltpu.VMEM((3, PAD_ROWS, CY), jnp.float32),
                pltpu.VMEM((ROWS, CY), jnp.float32),
                pltpu.VMEM((3, ROWS + 2 * EDGE, 1), jnp.float32),
                pltpu.VMEM((3, ROWS + 2 * EDGE, 1), jnp.float32),
            ]
            return run_step(shallow_kernel, scratch, current, earlier, factors, wet, low_x, high_x, low_y, high_y,
                            arrived_rows, arrived, pick)

        updated, outgoing, edges = lax.cond(section == 0, elastic_branch, shallow_branch)
        earlier, current = (current, updated)
    return current.reshape(1, 3, 1, 1, -1)


def solution(mesh):
    placed = (
        P("sec", None, "gx", "gy", None),
        P("sec", None, "gx", "gy", None),
        P("sec", None, "gx", "gy", None),
        P("gx", "gy", None),
        P("sec", "gx", "gy", None, None),
        P("sec", "gx", "gy", None, None),
        P("sec", "gx", "gy", None),
    )
    return jax.shard_map(
        on_device,
        mesh=mesh,
        in_specs=placed,
        out_specs=P("sec", None, "gx", "gy", None),
        check_vma=False,
    )
```

```python
import functools

import jax
import jax.numpy as jnp
from jax import lax
from jax.experimental import pallas as pl
from jax.experimental.pallas import tpu as pltpu
from jax.sharding import PartitionSpec as P

CX = 8
CY = 128
REFINE = 10
NL = 100
STEPS = 4
CAP = 4

ROWS = CX * NL
BASE = 104
PAD_ROWS = BASE + ROWS + BASE
CHUNK = 40
EDGE = 16
HALO_ROWS = NL + 4
EDGE_LANES = 896


def from_partner(value, axis, stride):
    return lax.ppermute(value, axis, [(i, i ^ 1 << stride) for i in range(lax.axis_size(axis))])


def shift_pairs(axis):
    count = lax.axis_size(axis)
    forward = [(i, i + 1) for i in range(count - 1)]
    backward = [(target, source) for source, target in forward]
    return forward, backward


def fill_scratch(scratch, cur_ref, low_ref, high_ref, fields):
    for f in range(fields):
        scratch[f, pl.ds(BASE - HALO_ROWS, HALO_ROWS), :] = low_ref[f]
        scratch[f, pl.ds(BASE, ROWS), :] = cur_ref[f]
        scratch[f, pl.ds(BASE + ROWS, HALO_ROWS), :] = high_ref[f]


def lane_index(rows):
    return lax.broadcasted_iota(jnp.int32, (rows, CY), 1)


def row_mask(r0, rows, period, phase):
    local = lax.broadcasted_iota(jnp.int32, (rows, CY), 0)
    mask = jnp.zeros((rows, CY), jnp.bool_)
    for r in range(rows):
        if (r0 + r) % period == phase:
            mask = mask | (local == r)
    return mask


def exact_dot(a, b):
    return jnp.dot(a, b, precision=lax.Precision.HIGHEST, preferred_element_type=jnp.float32)


def select_dot(a, b):
    return jnp.dot(a, b, precision=lax.Precision.HIGH, preferred_element_type=jnp.float32)


def landing_sum(rows_ref, arrived_ref, count):
    slots = rows_ref.shape[1]
    one_hot = (lax.broadcasted_iota(jnp.int32, (count, slots), 0) == rows_ref[...]).astype(jnp.float32)
    return exact_dot(one_hot, arrived_ref[...])


def edge_rows(out_ref, edges_ref):
    rows = lax.broadcasted_iota(jnp.int32, (8, CY), 0)
    lanes = lax.broadcasted_iota(jnp.int32, (8, CY), 1)
    select = (((rows == 0) & (lanes == CY - 1)) | ((rows == 1) & (lanes == 0))).astype(jnp.float32)
    for f in range(3):
        picked = lax.dot_general(select, out_ref[f], (((1,), (1,)), ((), ())), precision=lax.Precision.HIGHEST,
                                 preferred_element_type=jnp.float32)
        edges_ref[f] = jnp.zeros(edges_ref.shape[1:], jnp.float32)
        edges_ref[f, :, pl.ds(0, ROWS)] = picked


def fill_sides(low_rows_ref, high_rows_ref, left_pad, right_pad):
    for f in range(3):
        left_pad[f, pl.ds(EDGE, ROWS), :] = jnp.transpose(low_rows_ref[f])[:ROWS, 0:1]
        right_pad[f, pl.ds(EDGE, ROWS), :] = jnp.transpose(high_rows_ref[f])[:ROWS, 1:2]


def spread(cb):
    coarse = lax.broadcasted_iota(jnp.int32, (CY, CY), 0)
    fine = lax.broadcasted_iota(jnp.int32, (CY, CY), 1) + cb * CY
    return ((fine >= coarse * REFINE) & (fine < coarse * REFINE + REFINE)).astype(jnp.float32)


def elastic_kernel(cur_ref, prev_ref, coef_ref, low_ref, high_ref, low_rows_ref, high_rows_ref, rows_ref, arrived_ref,
                   pick_ref, out_ref, tiles_ref, edges_ref, scratch, left_pad, right_pad):
    fill_scratch(scratch, cur_ref, low_ref, high_ref, 3)
    fill_sides(low_rows_ref, high_rows_ref, left_pad, right_pad)
    force = landing_sum(rows_ref, arrived_ref, CX)
    lanes = lane_index(CHUNK)
    first_lane = lanes == 0
    last_lane = lanes == CY - 1
    own_axis = (0, 2, 1)
    for r0 in range(0, ROWS, CHUNK):
        top_layer = row_mask(r0, CHUNK, NL, 0)
        bottom_layer = row_mask(r0, CHUNK, NL, NL - 1)
        shear = coef_ref[0, pl.ds(r0, CHUNK), :]
        lame = coef_ref[1, pl.ds(r0, CHUNK), :]
        stiffness = lame + 2.0 * shear
        for c in range(3):
            at = BASE + r0
            v = scratch[c, pl.ds(at, CHUNK), :]
            along_first = scratch[c, pl.ds(at + NL, CHUNK), :] - 2.0 * v + scratch[c, pl.ds(at - NL, CHUNK), :]
            deeper = jnp.where(bottom_layer, 0.0, scratch[c, pl.ds(at + 1, CHUNK), :])
            shallower = jnp.where(top_layer, 0.0, scratch[c, pl.ds(at - 1, CHUNK), :])
            along_depth = deeper - 2.0 * v + shallower
            after = jnp.where(last_lane, right_pad[c, pl.ds(EDGE + r0, CHUNK), :], pltpu.roll(v, CY - 1, 1))
            before = jnp.where(first_lane, left_pad[c, pl.ds(EDGE + r0, CHUNK), :], pltpu.roll(v, 1, 1))
            along_second = after - 2.0 * v + before
            factors = [stiffness if own_axis[c] == axis_index else shear for axis_index in range(3)]
            acceleration = factors[0] * along_first + factors[1] * along_depth + factors[2] * along_second
            out_ref[c, pl.ds(r0, CHUNK), :] = 2.0 * v - prev_ref[c, pl.ds(r0, CHUNK), :] + acceleration
    for x in range(CX):
        out_ref[2, pl.ds(x * NL, 1), :] = out_ref[2, pl.ds(x * NL, 1), :] + force[x : x + 1]
    elastic_tiles(out_ref, pick_ref, tiles_ref)
    edge_rows(out_ref, edges_ref)


def shallow_kernel(cur_ref, prev_ref, coef_ref, wet_ref, low_ref, high_ref, low_rows_ref, high_rows_ref, rows_ref,
                   arrived_ref, pick_ref, out_ref, tiles_ref, edges_ref, scratch, source_ref, left_pad, right_pad):
    fill_scratch(scratch, cur_ref, low_ref, high_ref, 3)
    fill_sides(low_rows_ref, high_rows_ref, left_pad, right_pad)
    coarse_source = landing_sum(rows_ref, arrived_ref, REFINE * CX)
    for cb in range(REFINE):
        source_ref[pl.ds(cb, REFINE * CX, stride=REFINE), :] = select_dot(coarse_source, spread(cb))
    lanes = lane_index(CHUNK)
    first_lane = lanes == 0
    last_lane = lanes == CY - 1
    first_block = row_mask(0, CHUNK, REFINE, 0)
    last_block = row_mask(0, CHUNK, REFINE, REFINE - 1)
    for r0 in range(0, ROWS, CHUNK):
        at = BASE + r0

        def rows_diff(f):
            return scratch[f, pl.ds(at + REFINE, CHUNK), :] - scratch[f, pl.ds(at - REFINE, CHUNK), :]

        def columns_diff(f):
            v = scratch[f, pl.ds(at, CHUNK), :]
            wrap_after = jnp.where(last_block, right_pad[f, pl.ds(EDGE + r0 - (REFINE - 1), CHUNK), :],
                                   pltpu.roll(scratch[f, pl.ds(at + 1, CHUNK), :], CY - 1, 1))
            wrap_before = jnp.where(first_block, left_pad[f, pl.ds(EDGE + r0 + REFINE - 1, CHUNK), :],
                                    pltpu.roll(scratch[f, pl.ds(at - 1, CHUNK), :], 1, 1))
            after = jnp.where(last_lane, wrap_after, pltpu.roll(v, CY - 1, 1))
            before = jnp.where(first_lane, wrap_before, pltpu.roll(v, 1, 1))
            return after - before

        wave = coef_ref[0, pl.ds(r0, CHUNK), :]
        area = coef_ref[1, pl.ds(r0, CHUNK), :]
        wet = wet_ref[pl.ds(r0, CHUNK), :].astype(jnp.float32)
        eta_r = rows_diff(0)
        eta_c = columns_diff(0)
        out_ref[1, pl.ds(r0, CHUNK), :] = wet * (prev_ref[1, pl.ds(r0, CHUNK), :] - wave * eta_r)
        out_ref[2, pl.ds(r0, CHUNK), :] = wet * (prev_ref[2, pl.ds(r0, CHUNK), :] - wave * eta_c)
        divergence = rows_diff(1) + columns_diff(2)
        out_ref[0, pl.ds(r0, CHUNK), :] = wet * (
            prev_ref[0, pl.ds(r0, CHUNK), :] - area * divergence + source_ref[pl.ds(r0, CHUNK), :]
        )
    shallow_tiles(out_ref, pick_ref, tiles_ref)
    edge_rows(out_ref, edges_ref)


def shallow_tiles(field_ref, pick_ref, tiles_ref):
    total = jnp.zeros((REFINE * CX, CY), jnp.float32)
    for cb in range(REFINE):
        total = total + select_dot(field_ref[0, pl.ds(cb, REFINE * CX, stride=REFINE), :], spread(cb).T)
    tiles_ref[...] = exact_dot(pick_ref[...], total / REFINE)


def elastic_tiles(field_ref, pick_ref, tiles_ref):
    uplift = field_ref[2, pl.ds(0, CX, stride=NL), :]
    tiles_ref[...] = exact_dot(pick_ref[:, :CX], uplift)


def prepare_kernel(tiles_of, cur_ref, pick_ref, tiles_ref, edges_ref):
    tiles_of(cur_ref, pick_ref, tiles_ref)
    edge_rows(cur_ref, edges_ref)


def prepare(tiles_of, current, pick):
    return pl.pallas_call(
        functools.partial(prepare_kernel, tiles_of),
        out_shape=(
            jax.ShapeDtypeStruct((pick.shape[0], CY), jnp.float32),
            jax.ShapeDtypeStruct((3, 8, EDGE_LANES), jnp.float32),
        ),
        in_specs=vmem_specs(2),
        out_specs=tuple(vmem_specs(2)),
    )(current, pick)


def vmem_specs(count):
    return [pl.BlockSpec(memory_space=pltpu.VMEM)] * count


def run_step(kernel, scratch_shapes, *operands):
    slots = operands[-1].shape[0]
    return pl.pallas_call(
        kernel,
        out_shape=(
            jax.ShapeDtypeStruct((3, ROWS, CY), jnp.float32),
            jax.ShapeDtypeStruct((slots, CY), jnp.float32),
            jax.ShapeDtypeStruct((3, 8, EDGE_LANES), jnp.float32),
        ),
        in_specs=vmem_specs(len(operands)),
        out_specs=tuple(vmem_specs(3)),
        scratch_shapes=scratch_shapes,
    )(*operands)


def exchange_kernel(sizes, cur_ref, edges_ref, out_ref, in_ref, low_ref, high_ref, low_rows_ref, high_rows_ref,
                    land, halo, sides, send_sem, recv_sem, halo_send, halo_recv, side_send, side_recv):
    owners, rows_of, columns = sizes
    other = 1 - lax.axis_index("sec")
    section = lax.axis_index("sec")
    gx = lax.axis_index("gx")
    gy = lax.axis_index("gy")
    me = gx * columns + gy
    has_low = gx > 0
    has_high = gx < rows_of - 1
    has_left = gy > 0
    has_right = gy < columns - 1
    halo[...] = jnp.zeros_like(halo)
    sides[...] = jnp.zeros_like(sides)
    barrier = pltpu.get_barrier_semaphore()
    def greet(d, carry):
        pl.semaphore_signal(barrier, inc=1, device_id=(other, d // columns, d % columns),
                            device_id_type=pl.DeviceIdType.MESH)
        return carry

    lax.fori_loop(0, owners, greet, 0, unroll=True)

    @pl.when(has_low)
    def _():
        pl.semaphore_signal(barrier, inc=1, device_id=(section, gx - 1, gy), device_id_type=pl.DeviceIdType.MESH)

    @pl.when(has_high)
    def _():
        pl.semaphore_signal(barrier, inc=1, device_id=(section, gx + 1, gy), device_id_type=pl.DeviceIdType.MESH)

    @pl.when(has_left)
    def _():
        pl.semaphore_signal(barrier, inc=1, device_id=(section, gx, gy - 1), device_id_type=pl.DeviceIdType.MESH)

    @pl.when(has_right)
    def _():
        pl.semaphore_signal(barrier, inc=1, device_id=(section, gx, gy + 1), device_id_type=pl.DeviceIdType.MESH)

    neighbours = [has_low, has_high, has_left, has_right]
    pl.semaphore_wait(barrier, owners + sum(n.astype(jnp.int32) for n in neighbours))

    def side_copy(slot, target):
        return pltpu.make_async_remote_copy(
            src_ref=edges_ref,
            dst_ref=sides.at[slot],
            send_sem=side_send.at[slot],
            recv_sem=side_recv.at[slot],
            device_id=(section, gx, target),
            device_id_type=pl.DeviceIdType.MESH,
        )

    @pl.when(has_right)
    def _():
        side_copy(0, gy + 1).start()

    @pl.when(has_left)
    def _():
        side_copy(1, gy - 1).start()

    def slab_copy(start, slot, target):
        return pltpu.make_async_remote_copy(
            src_ref=cur_ref.at[:, pl.ds(start, HALO_ROWS), :],
            dst_ref=halo.at[slot],
            send_sem=halo_send.at[slot],
            recv_sem=halo_recv.at[slot],
            device_id=(section, target, gy),
            device_id_type=pl.DeviceIdType.MESH,
        )

    @pl.when(has_high)
    def _():
        slab_copy(ROWS - HALO_ROWS, 0, gx + 1).start()

    @pl.when(has_low)
    def _():
        slab_copy(0, 1, gx - 1).start()

    def send(d, carry):
        pltpu.make_async_remote_copy(
            src_ref=out_ref.at[pl.ds(d * CAP, CAP)],
            dst_ref=land.at[pl.ds(me * CAP, CAP)],
            send_sem=send_sem,
            recv_sem=recv_sem,
            device_id=(other, d // columns, d % columns),
            device_id_type=pl.DeviceIdType.MESH,
        ).start()
        return carry

    lax.fori_loop(0, owners, send, 0, unroll=True)
    whole = pltpu.make_async_remote_copy(
        src_ref=out_ref,
        dst_ref=land,
        send_sem=send_sem,
        recv_sem=recv_sem,
        device_id=(other, gx, gy),
        device_id_type=pl.DeviceIdType.MESH,
    )

    @pl.when(has_high)
    def _():
        slab_copy(ROWS - HALO_ROWS, 0, gx + 1).wait_send()
        slab_copy(0, 1, gx + 1).wait_recv()

    @pl.when(has_low)
    def _():
        slab_copy(0, 1, gx - 1).wait_send()
        slab_copy(ROWS - HALO_ROWS, 0, gx - 1).wait_recv()

    @pl.when(has_right)
    def _():
        side_copy(0, gy + 1).wait_send()
        side_copy(1, gy + 1).wait_recv()

    @pl.when(has_left)
    def _():
        side_copy(1, gy - 1).wait_send()
        side_copy(0, gy - 1).wait_recv()

    whole.wait_send()
    whole.wait_recv()
    in_ref[...] = land[...]
    low_ref[...] = halo[0]
    high_ref[...] = halo[1]
    low_rows_ref[...] = sides[0]
    high_rows_ref[...] = sides[1]


def exchange(current, edges, outgoing, owners, rows_of, columns):
    halo_shape = jax.ShapeDtypeStruct((3, HALO_ROWS, CY), jnp.float32)
    side_shape = jax.ShapeDtypeStruct(edges.shape, jnp.float32)
    return pl.pallas_call(
        functools.partial(exchange_kernel, (owners, rows_of, columns)),
        out_shape=(jax.ShapeDtypeStruct(outgoing.shape, jnp.float32), halo_shape, halo_shape, side_shape, side_shape),
        in_specs=[pl.BlockSpec(memory_space=pl.ANY)] * 2 + [pl.BlockSpec(memory_space=pltpu.VMEM)],
        out_specs=tuple(vmem_specs(5)),
        scratch_shapes=[
            pltpu.VMEM(outgoing.shape, jnp.float32),
            pltpu.VMEM((2, 3, HALO_ROWS, CY), jnp.float32),
            pltpu.VMEM((2,) + edges.shape, jnp.float32),
            pltpu.SemaphoreType.DMA(()),
            pltpu.SemaphoreType.DMA(()),
            pltpu.SemaphoreType.DMA((2,)),
            pltpu.SemaphoreType.DMA((2,)),
            pltpu.SemaphoreType.DMA((2,)),
            pltpu.SemaphoreType.DMA((2,)),
        ],
        compiler_params=pltpu.CompilerParams(collective_id=outgoing.shape[1] // CY - 1, has_side_effects=True),
    )(current, edges, outgoing)


def route(payload):
    tile_data, tile_rows = payload
    width = tile_data.shape[-1]
    received_data, received_rows = (
        lax.all_to_all(tile_data, ("gx", "gy"), split_axis=0, concat_axis=0, tiled=True),
        lax.all_to_all(tile_rows, ("gx", "gy"), split_axis=0, concat_axis=0, tiled=True),
    )
    return (received_data.reshape(-1, width), received_rows.reshape(-1))


def deliver(outgoing, send_rows):
    routed = route((outgoing, send_rows))
    return from_partner((routed[0], routed[1]), "sec", 0)


def on_device(state, previous, coeff, wet_mask, link_dest, link_rows, link_weight):
    section = lax.axis_index("sec")
    owners = lax.axis_size("gx") * lax.axis_size("gy")
    fine_rows = REFINE * CX
    current = state[0, :, 0, 0].reshape(3, ROWS, CY)
    earlier = previous[0, :, 0, 0].reshape(3, ROWS, CY)
    factors = coeff[0, :, 0, 0].reshape(2, ROWS, CY)
    wet = wet_mask[0, 0].reshape(ROWS, CY)
    targets = link_dest.reshape(-1)
    pairs = link_rows.reshape(-1, 2)
    source_rows = pairs[:, 0]
    landing = pairs[:, 1]
    weights = link_weight.reshape(-1)
    one_hot = (targets[:, None] == jnp.arange(owners, dtype=jnp.int32)[None, :]).astype(jnp.int32)
    before = jnp.cumsum(one_hot, axis=0) - one_hot
    slot_index = jnp.sum(before * one_hot, axis=1)
    position = targets * CAP + slot_index
    send_rows = jnp.zeros((owners * CAP,), jnp.int32).at[position].set(landing).reshape(owners, CAP)
    slot_rows = jnp.full((owners * CAP,), -1, jnp.int32).at[position].set(source_rows)
    slot_weights = jnp.zeros((owners * CAP,), jnp.float32).at[position].set(weights)
    pick = jnp.where(slot_rows[:, None] == jnp.arange(fine_rows, dtype=jnp.int32)[None, :], slot_weights[:, None], 0.0)
    outgoing, edges = lax.cond(
        section == 0,
        lambda: prepare(elastic_tiles, current, pick),
        lambda: prepare(shallow_tiles, current, pick),
    )
    row_lanes = jnp.broadcast_to(send_rows.reshape(-1, 1).astype(jnp.float32), (owners * CAP, CY))
    outgoing = jnp.concatenate([outgoing, row_lanes], axis=1)
    for step_index in range(STEPS):
        arrived, low_x, high_x, low_y, high_y = exchange(
            current, edges, outgoing, owners, lax.axis_size("gx"), lax.axis_size("gy")
        )
        if step_index == 0:
            arrived_rows = arrived[:, CY].astype(jnp.int32).reshape(1, -1)
            arrived = arrived[:, :CY]

        def elastic_branch():
            scratch = [
                pltpu.VMEM((3, PAD_ROWS, CY), jnp.float32),
                pltpu.VMEM((3, ROWS + 2 * EDGE, 1), jnp.float32),
                pltpu.VMEM((3, ROWS + 2 * EDGE, 1), jnp.float32),
            ]
            return run_step(elastic_kernel, scratch, current, earlier, factors, low_x, high_x, low_y, high_y,
                            arrived_rows, arrived, pick)

        def shallow_branch():
            scratch = [
                pltpu.VMEM((3, PAD_ROWS, CY), jnp.float32),
                pltpu.VMEM((ROWS, CY), jnp.float32),
                pltpu.VMEM((3, ROWS + 2 * EDGE, 1), jnp.float32),
                pltpu.VMEM((3, ROWS + 2 * EDGE, 1), jnp.float32),
            ]
            return run_step(shallow_kernel, scratch, current, earlier, factors, wet, low_x, high_x, low_y, high_y,
                            arrived_rows, arrived, pick)

        updated, outgoing, edges = lax.cond(section == 0, elastic_branch, shallow_branch)
        earlier, current = (current, updated)
    return current.reshape(1, 3, 1, 1, -1)


def solution(mesh):
    placed = (
        P("sec", None, "gx", "gy", None),
        P("sec", None, "gx", "gy", None),
        P("sec", None, "gx", "gy", None),
        P("gx", "gy", None),
        P("sec", "gx", "gy", None, None),
        P("sec", "gx", "gy", None, None),
        P("sec", "gx", "gy", None),
    )
    return jax.shard_map(
        on_device,
        mesh=mesh,
        in_specs=placed,
        out_specs=P("sec", None, "gx", "gy", None),
        check_vma=False,
    )
```

```python
import functools

import jax
import jax.numpy as jnp
from jax import lax
from jax.experimental import pallas as pl
from jax.experimental.pallas import tpu as pltpu
from jax.sharding import PartitionSpec as P

CX = 8
CY = 128
REFINE = 10
NL = 100
STEPS = 4
CAP = 4

ROWS = CX * NL
BASE = 104
PAD_ROWS = BASE + ROWS + BASE
CHUNK = 40
EDGE = 16
HALO_ROWS = NL + 4
EDGE_LANES = 896


def from_partner(value, axis, stride):
    return lax.ppermute(value, axis, [(i, i ^ 1 << stride) for i in range(lax.axis_size(axis))])


def shift_pairs(axis):
    count = lax.axis_size(axis)
    forward = [(i, i + 1) for i in range(count - 1)]
    backward = [(target, source) for source, target in forward]
    return forward, backward


def fill_scratch(scratch, cur_ref, low_ref, high_ref, fields):
    for f in range(fields):
        scratch[f, pl.ds(BASE - HALO_ROWS, HALO_ROWS), :] = low_ref[f]
        scratch[f, pl.ds(BASE, ROWS), :] = cur_ref[f]
        scratch[f, pl.ds(BASE + ROWS, HALO_ROWS), :] = high_ref[f]


def lane_index(rows):
    return lax.broadcasted_iota(jnp.int32, (rows, CY), 1)


def row_mask(r0, rows, period, phase):
    local = lax.broadcasted_iota(jnp.int32, (rows, CY), 0)
    mask = jnp.zeros((rows, CY), jnp.bool_)
    for r in range(rows):
        if (r0 + r) % period == phase:
            mask = mask | (local == r)
    return mask


def exact_dot(a, b):
    return jnp.dot(a, b, precision=lax.Precision.HIGHEST, preferred_element_type=jnp.float32)


def select_dot(a, b):
    return jnp.dot(a, b, precision=lax.Precision.HIGH, preferred_element_type=jnp.float32)


def landing_sum(rows_ref, arrived_ref, count):
    slots = rows_ref.shape[1]
    one_hot = (lax.broadcasted_iota(jnp.int32, (count, slots), 0) == rows_ref[...]).astype(jnp.float32)
    return exact_dot(one_hot, arrived_ref[...])


def edge_rows(out_ref, edges_ref):
    rows = lax.broadcasted_iota(jnp.int32, (8, CY), 0)
    lanes = lax.broadcasted_iota(jnp.int32, (8, CY), 1)
    select = (((rows == 0) & (lanes == CY - 1)) | ((rows == 1) & (lanes == 0))).astype(jnp.float32)
    for f in range(3):
        picked = lax.dot_general(select, out_ref[f], (((1,), (1,)), ((), ())), precision=lax.Precision.HIGH,
                                 preferred_element_type=jnp.float32)
        edges_ref[f] = jnp.zeros(edges_ref.shape[1:], jnp.float32)
        edges_ref[f, :, pl.ds(0, ROWS)] = picked


def fill_sides(low_rows_ref, high_rows_ref, left_pad, right_pad):
    for f in range(3):
        left_pad[f, pl.ds(EDGE, ROWS), :] = jnp.transpose(low_rows_ref[f])[:ROWS, 0:1]
        right_pad[f, pl.ds(EDGE, ROWS), :] = jnp.transpose(high_rows_ref[f])[:ROWS, 1:2]


def spread(cb):
    coarse = lax.broadcasted_iota(jnp.int32, (CY, CY), 0)
    fine = lax.broadcasted_iota(jnp.int32, (CY, CY), 1) + cb * CY
    return ((fine >= coarse * REFINE) & (fine < coarse * REFINE + REFINE)).astype(jnp.float32)


def elastic_kernel(cur_ref, prev_ref, coef_ref, low_ref, high_ref, low_rows_ref, high_rows_ref, rows_ref, arrived_ref,
                   pick_ref, out_ref, tiles_ref, edges_ref, scratch, left_pad, right_pad):
    fill_scratch(scratch, cur_ref, low_ref, high_ref, 3)
    fill_sides(low_rows_ref, high_rows_ref, left_pad, right_pad)
    force = landing_sum(rows_ref, arrived_ref, CX)
    lanes = lane_index(CHUNK)
    first_lane = lanes == 0
    last_lane = lanes == CY - 1
    own_axis = (0, 2, 1)
    for r0 in range(0, ROWS, CHUNK):
        top_layer = row_mask(r0, CHUNK, NL, 0)
        bottom_layer = row_mask(r0, CHUNK, NL, NL - 1)
        shear = coef_ref[0, pl.ds(r0, CHUNK), :]
        lame = coef_ref[1, pl.ds(r0, CHUNK), :]
        stiffness = lame + 2.0 * shear
        for c in range(3):
            at = BASE + r0
            v = scratch[c, pl.ds(at, CHUNK), :]
            along_first = scratch[c, pl.ds(at + NL, CHUNK), :] - 2.0 * v + scratch[c, pl.ds(at - NL, CHUNK), :]
            deeper = jnp.where(bottom_layer, 0.0, scratch[c, pl.ds(at + 1, CHUNK), :])
            shallower = jnp.where(top_layer, 0.0, scratch[c, pl.ds(at - 1, CHUNK), :])
            along_depth = deeper - 2.0 * v + shallower
            after = jnp.where(last_lane, right_pad[c, pl.ds(EDGE + r0, CHUNK), :], pltpu.roll(v, CY - 1, 1))
            before = jnp.where(first_lane, left_pad[c, pl.ds(EDGE + r0, CHUNK), :], pltpu.roll(v, 1, 1))
            along_second = after - 2.0 * v + before
            factors = [stiffness if own_axis[c] == axis_index else shear for axis_index in range(3)]
            acceleration = factors[0] * along_first + factors[1] * along_depth + factors[2] * along_second
            out_ref[c, pl.ds(r0, CHUNK), :] = 2.0 * v - prev_ref[c, pl.ds(r0, CHUNK), :] + acceleration
    for x in range(CX):
        out_ref[2, pl.ds(x * NL, 1), :] = out_ref[2, pl.ds(x * NL, 1), :] + force[x : x + 1]
    elastic_tiles(out_ref, pick_ref, tiles_ref)
    edge_rows(out_ref, edges_ref)


def shallow_kernel(cur_ref, prev_ref, coef_ref, wet_ref, low_ref, high_ref, low_rows_ref, high_rows_ref, rows_ref,
                   arrived_ref, pick_ref, out_ref, tiles_ref, edges_ref, scratch, source_ref, left_pad, right_pad):
    fill_scratch(scratch, cur_ref, low_ref, high_ref, 3)
    fill_sides(low_rows_ref, high_rows_ref, left_pad, right_pad)
    coarse_source = landing_sum(rows_ref, arrived_ref, REFINE * CX)
    for cb in range(REFINE):
        source_ref[pl.ds(cb, REFINE * CX, stride=REFINE), :] = select_dot(coarse_source, spread(cb))
    lanes = lane_index(CHUNK)
    first_lane = lanes == 0
    last_lane = lanes == CY - 1
    first_block = row_mask(0, CHUNK, REFINE, 0)
    last_block = row_mask(0, CHUNK, REFINE, REFINE - 1)
    for r0 in range(0, ROWS, CHUNK):
        at = BASE + r0

        def rows_diff(f):
            return scratch[f, pl.ds(at + REFINE, CHUNK), :] - scratch[f, pl.ds(at - REFINE, CHUNK), :]

        def columns_diff(f):
            v = scratch[f, pl.ds(at, CHUNK), :]
            wrap_after = jnp.where(last_block, right_pad[f, pl.ds(EDGE + r0 - (REFINE - 1), CHUNK), :],
                                   pltpu.roll(scratch[f, pl.ds(at + 1, CHUNK), :], CY - 1, 1))
            wrap_before = jnp.where(first_block, left_pad[f, pl.ds(EDGE + r0 + REFINE - 1, CHUNK), :],
                                    pltpu.roll(scratch[f, pl.ds(at - 1, CHUNK), :], 1, 1))
            after = jnp.where(last_lane, wrap_after, pltpu.roll(v, CY - 1, 1))
            before = jnp.where(first_lane, wrap_before, pltpu.roll(v, 1, 1))
            return after - before

        wave = coef_ref[0, pl.ds(r0, CHUNK), :]
        area = coef_ref[1, pl.ds(r0, CHUNK), :]
        wet = wet_ref[pl.ds(r0, CHUNK), :].astype(jnp.float32)
        eta_r = rows_diff(0)
        eta_c = columns_diff(0)
        out_ref[1, pl.ds(r0, CHUNK), :] = wet * (prev_ref[1, pl.ds(r0, CHUNK), :] - wave * eta_r)
        out_ref[2, pl.ds(r0, CHUNK), :] = wet * (prev_ref[2, pl.ds(r0, CHUNK), :] - wave * eta_c)
        divergence = rows_diff(1) + columns_diff(2)
        out_ref[0, pl.ds(r0, CHUNK), :] = wet * (
            prev_ref[0, pl.ds(r0, CHUNK), :] - area * divergence + source_ref[pl.ds(r0, CHUNK), :]
        )
    shallow_tiles(out_ref, pick_ref, tiles_ref)
    edge_rows(out_ref, edges_ref)


def shallow_tiles(field_ref, pick_ref, tiles_ref):
    total = jnp.zeros((REFINE * CX, CY), jnp.float32)
    for cb in range(REFINE):
        total = total + select_dot(field_ref[0, pl.ds(cb, REFINE * CX, stride=REFINE), :], spread(cb).T)
    tiles_ref[...] = exact_dot(pick_ref[...], total / REFINE)


def elastic_tiles(field_ref, pick_ref, tiles_ref):
    uplift = field_ref[2, pl.ds(0, CX, stride=NL), :]
    tiles_ref[...] = exact_dot(pick_ref[:, :CX], uplift)


def prepare_kernel(tiles_of, cur_ref, pick_ref, tiles_ref, edges_ref):
    tiles_of(cur_ref, pick_ref, tiles_ref)
    edge_rows(cur_ref, edges_ref)


def prepare(tiles_of, current, pick):
    return pl.pallas_call(
        functools.partial(prepare_kernel, tiles_of),
        out_shape=(
            jax.ShapeDtypeStruct((pick.shape[0], CY), jnp.float32),
            jax.ShapeDtypeStruct((3, 8, EDGE_LANES), jnp.float32),
        ),
        in_specs=vmem_specs(2),
        out_specs=tuple(vmem_specs(2)),
    )(current, pick)


def vmem_specs(count):
    return [pl.BlockSpec(memory_space=pltpu.VMEM)] * count


def run_step(kernel, scratch_shapes, *operands):
    slots = operands[-1].shape[0]
    return pl.pallas_call(
        kernel,
        out_shape=(
            jax.ShapeDtypeStruct((3, ROWS, CY), jnp.float32),
            jax.ShapeDtypeStruct((slots, CY), jnp.float32),
            jax.ShapeDtypeStruct((3, 8, EDGE_LANES), jnp.float32),
        ),
        in_specs=vmem_specs(len(operands)),
        out_specs=tuple(vmem_specs(3)),
        scratch_shapes=scratch_shapes,
    )(*operands)


def exchange_kernel(sizes, cur_ref, edges_ref, out_ref, in_ref, low_ref, high_ref, low_rows_ref, high_rows_ref,
                    land, halo, sides, send_sem, recv_sem, halo_send, halo_recv, side_send, side_recv):
    owners, rows_of, columns = sizes
    other = 1 - lax.axis_index("sec")
    section = lax.axis_index("sec")
    gx = lax.axis_index("gx")
    gy = lax.axis_index("gy")
    me = gx * columns + gy
    has_low = gx > 0
    has_high = gx < rows_of - 1
    has_left = gy > 0
    has_right = gy < columns - 1
    halo[...] = jnp.zeros_like(halo)
    sides[...] = jnp.zeros_like(sides)
    barrier = pltpu.get_barrier_semaphore()
    def greet(d, carry):
        pl.semaphore_signal(barrier, inc=1, device_id=(other, d // columns, d % columns),
                            device_id_type=pl.DeviceIdType.MESH)
        return carry

    lax.fori_loop(0, owners, greet, 0, unroll=True)

    @pl.when(has_low)
    def _():
        pl.semaphore_signal(barrier, inc=1, device_id=(section, gx - 1, gy), device_id_type=pl.DeviceIdType.MESH)

    @pl.when(has_high)
    def _():
        pl.semaphore_signal(barrier, inc=1, device_id=(section, gx + 1, gy), device_id_type=pl.DeviceIdType.MESH)

    @pl.when(has_left)
    def _():
        pl.semaphore_signal(barrier, inc=1, device_id=(section, gx, gy - 1), device_id_type=pl.DeviceIdType.MESH)

    @pl.when(has_right)
    def _():
        pl.semaphore_signal(barrier, inc=1, device_id=(section, gx, gy + 1), device_id_type=pl.DeviceIdType.MESH)

    neighbours = [has_low, has_high, has_left, has_right]
    pl.semaphore_wait(barrier, owners + sum(n.astype(jnp.int32) for n in neighbours))

    def side_copy(slot, target):
        return pltpu.make_async_remote_copy(
            src_ref=edges_ref,
            dst_ref=sides.at[slot],
            send_sem=side_send.at[slot],
            recv_sem=side_recv.at[slot],
            device_id=(section, gx, target),
            device_id_type=pl.DeviceIdType.MESH,
        )

    @pl.when(has_right)
    def _():
        side_copy(0, gy + 1).start()

    @pl.when(has_left)
    def _():
        side_copy(1, gy - 1).start()

    def slab_copy(start, slot, target):
        return pltpu.make_async_remote_copy(
            src_ref=cur_ref.at[:, pl.ds(start, HALO_ROWS), :],
            dst_ref=halo.at[slot],
            send_sem=halo_send.at[slot],
            recv_sem=halo_recv.at[slot],
            device_id=(section, target, gy),
            device_id_type=pl.DeviceIdType.MESH,
        )

    @pl.when(has_high)
    def _():
        slab_copy(ROWS - HALO_ROWS, 0, gx + 1).start()

    @pl.when(has_low)
    def _():
        slab_copy(0, 1, gx - 1).start()

    def send(d, carry):
        pltpu.make_async_remote_copy(
            src_ref=out_ref.at[pl.ds(d * CAP, CAP)],
            dst_ref=land.at[pl.ds(me * CAP, CAP)],
            send_sem=send_sem,
            recv_sem=recv_sem,
            device_id=(other, d // columns, d % columns),
            device_id_type=pl.DeviceIdType.MESH,
        ).start()
        return carry

    lax.fori_loop(0, owners, send, 0, unroll=True)
    whole = pltpu.make_async_remote_copy(
        src_ref=out_ref,
        dst_ref=land,
        send_sem=send_sem,
        recv_sem=recv_sem,
        device_id=(other, gx, gy),
        device_id_type=pl.DeviceIdType.MESH,
    )

    @pl.when(has_high)
    def _():
        slab_copy(ROWS - HALO_ROWS, 0, gx + 1).wait_send()
        slab_copy(0, 1, gx + 1).wait_recv()

    @pl.when(has_low)
    def _():
        slab_copy(0, 1, gx - 1).wait_send()
        slab_copy(ROWS - HALO_ROWS, 0, gx - 1).wait_recv()

    @pl.when(has_right)
    def _():
        side_copy(0, gy + 1).wait_send()
        side_copy(1, gy + 1).wait_recv()

    @pl.when(has_left)
    def _():
        side_copy(1, gy - 1).wait_send()
        side_copy(0, gy - 1).wait_recv()

    whole.wait_send()
    whole.wait_recv()
    in_ref[...] = land[...]
    low_ref[...] = halo[0]
    high_ref[...] = halo[1]
    low_rows_ref[...] = sides[0]
    high_rows_ref[...] = sides[1]


def exchange(current, edges, outgoing, owners, rows_of, columns):
    halo_shape = jax.ShapeDtypeStruct((3, HALO_ROWS, CY), jnp.float32)
    side_shape = jax.ShapeDtypeStruct(edges.shape, jnp.float32)
    return pl.pallas_call(
        functools.partial(exchange_kernel, (owners, rows_of, columns)),
        out_shape=(jax.ShapeDtypeStruct(outgoing.shape, jnp.float32), halo_shape, halo_shape, side_shape, side_shape),
        in_specs=[pl.BlockSpec(memory_space=pl.ANY)] * 2 + [pl.BlockSpec(memory_space=pltpu.VMEM)],
        out_specs=tuple(vmem_specs(5)),
        scratch_shapes=[
            pltpu.VMEM(outgoing.shape, jnp.float32),
            pltpu.VMEM((2, 3, HALO_ROWS, CY), jnp.float32),
            pltpu.VMEM((2,) + edges.shape, jnp.float32),
            pltpu.SemaphoreType.DMA(()),
            pltpu.SemaphoreType.DMA(()),
            pltpu.SemaphoreType.DMA((2,)),
            pltpu.SemaphoreType.DMA((2,)),
            pltpu.SemaphoreType.DMA((2,)),
            pltpu.SemaphoreType.DMA((2,)),
        ],
        compiler_params=pltpu.CompilerParams(collective_id=outgoing.shape[1] // CY - 1, has_side_effects=True),
    )(current, edges, outgoing)


def route(payload):
    tile_data, tile_rows = payload
    width = tile_data.shape[-1]
    received_data, received_rows = (
        lax.all_to_all(tile_data, ("gx", "gy"), split_axis=0, concat_axis=0, tiled=True),
        lax.all_to_all(tile_rows, ("gx", "gy"), split_axis=0, concat_axis=0, tiled=True),
    )
    return (received_data.reshape(-1, width), received_rows.reshape(-1))


def deliver(outgoing, send_rows):
    routed = route((outgoing, send_rows))
    return from_partner((routed[0], routed[1]), "sec", 0)


def on_device(state, previous, coeff, wet_mask, link_dest, link_rows, link_weight):
    section = lax.axis_index("sec")
    owners = lax.axis_size("gx") * lax.axis_size("gy")
    fine_rows = REFINE * CX
    current = state[0, :, 0, 0].reshape(3, ROWS, CY)
    earlier = previous[0, :, 0, 0].reshape(3, ROWS, CY)
    factors = coeff[0, :, 0, 0].reshape(2, ROWS, CY)
    wet = wet_mask[0, 0].reshape(ROWS, CY)
    targets = link_dest.reshape(-1)
    pairs = link_rows.reshape(-1, 2)
    source_rows = pairs[:, 0]
    landing = pairs[:, 1]
    weights = link_weight.reshape(-1)
    one_hot = (targets[:, None] == jnp.arange(owners, dtype=jnp.int32)[None, :]).astype(jnp.int32)
    before = jnp.cumsum(one_hot, axis=0) - one_hot
    slot_index = jnp.sum(before * one_hot, axis=1)
    position = targets * CAP + slot_index
    send_rows = jnp.zeros((owners * CAP,), jnp.int32).at[position].set(landing).reshape(owners, CAP)
    slot_rows = jnp.full((owners * CAP,), -1, jnp.int32).at[position].set(source_rows)
    slot_weights = jnp.zeros((owners * CAP,), jnp.float32).at[position].set(weights)
    pick = jnp.where(slot_rows[:, None] == jnp.arange(fine_rows, dtype=jnp.int32)[None, :], slot_weights[:, None], 0.0)
    outgoing, edges = lax.cond(
        section == 0,
        lambda: prepare(elastic_tiles, current, pick),
        lambda: prepare(shallow_tiles, current, pick),
    )
    row_lanes = jnp.broadcast_to(send_rows.reshape(-1, 1).astype(jnp.float32), (owners * CAP, CY))
    outgoing = jnp.concatenate([outgoing, row_lanes], axis=1)
    for step_index in range(STEPS):
        arrived, low_x, high_x, low_y, high_y = exchange(
            current, edges, outgoing, owners, lax.axis_size("gx"), lax.axis_size("gy")
        )
        if step_index == 0:
            arrived_rows = arrived[:, CY].astype(jnp.int32).reshape(1, -1)
            arrived = arrived[:, :CY]

        def elastic_branch():
            scratch = [
                pltpu.VMEM((3, PAD_ROWS, CY), jnp.float32),
                pltpu.VMEM((3, ROWS + 2 * EDGE, 1), jnp.float32),
                pltpu.VMEM((3, ROWS + 2 * EDGE, 1), jnp.float32),
            ]
            return run_step(elastic_kernel, scratch, current, earlier, factors, low_x, high_x, low_y, high_y,
                            arrived_rows, arrived, pick)

        def shallow_branch():
            scratch = [
                pltpu.VMEM((3, PAD_ROWS, CY), jnp.float32),
                pltpu.VMEM((ROWS, CY), jnp.float32),
                pltpu.VMEM((3, ROWS + 2 * EDGE, 1), jnp.float32),
                pltpu.VMEM((3, ROWS + 2 * EDGE, 1), jnp.float32),
            ]
            return run_step(shallow_kernel, scratch, current, earlier, factors, wet, low_x, high_x, low_y, high_y,
                            arrived_rows, arrived, pick)

        updated, outgoing, edges = lax.cond(section == 0, elastic_branch, shallow_branch)
        earlier, current = (current, updated)
    return current.reshape(1, 3, 1, 1, -1)


def solution(mesh):
    placed = (
        P("sec", None, "gx", "gy", None),
        P("sec", None, "gx", "gy", None),
        P("sec", None, "gx", "gy", None),
        P("gx", "gy", None),
        P("sec", "gx", "gy", None, None),
        P("sec", "gx", "gy", None, None),
        P("sec", "gx", "gy", None),
    )
    return jax.shard_map(
        on_device,
        mesh=mesh,
        in_specs=placed,
        out_specs=P("sec", None, "gx", "gy", None),
        check_vma=False,
    )
```

```python
import functools

import jax
import jax.numpy as jnp
from jax import lax
from jax.experimental import pallas as pl
from jax.experimental.pallas import tpu as pltpu
from jax.sharding import PartitionSpec as P

CX = 8
CY = 128
REFINE = 10
NL = 100
STEPS = 4
CAP = 4

ROWS = CX * NL
BASE = 104
PAD_ROWS = BASE + ROWS + BASE
CHUNK = 40
EDGE = 16
HALO_ROWS = NL + 4
EDGE_LANES = 896


def from_partner(value, axis, stride):
    return lax.ppermute(value, axis, [(i, i ^ 1 << stride) for i in range(lax.axis_size(axis))])


def shift_pairs(axis):
    count = lax.axis_size(axis)
    forward = [(i, i + 1) for i in range(count - 1)]
    backward = [(target, source) for source, target in forward]
    return forward, backward


def fill_scratch(scratch, cur_ref, low_ref, high_ref, fields):
    for f in range(fields):
        scratch[f, pl.ds(BASE - HALO_ROWS, HALO_ROWS), :] = low_ref[f]
        scratch[f, pl.ds(BASE, ROWS), :] = cur_ref[f]
        scratch[f, pl.ds(BASE + ROWS, HALO_ROWS), :] = high_ref[f]


def lane_index(rows):
    return lax.broadcasted_iota(jnp.int32, (rows, CY), 1)


def row_mask(r0, rows, period, phase):
    local = lax.broadcasted_iota(jnp.int32, (rows, CY), 0)
    mask = jnp.zeros((rows, CY), jnp.bool_)
    for r in range(rows):
        if (r0 + r) % period == phase:
            mask = mask | (local == r)
    return mask


def exact_dot(a, b):
    return jnp.dot(a, b, precision=lax.Precision.HIGHEST, preferred_element_type=jnp.float32)


def select_dot(a, b):
    return jnp.dot(a, b, precision=lax.Precision.HIGH, preferred_element_type=jnp.float32)


def landing_sum(rows_ref, arrived_ref, count):
    slots = rows_ref.shape[1]
    one_hot = (lax.broadcasted_iota(jnp.int32, (count, slots), 0) == rows_ref[...]).astype(jnp.float32)
    return exact_dot(one_hot, arrived_ref[...])


def edge_rows(out_ref, edges_ref):
    rows = lax.broadcasted_iota(jnp.int32, (8, CY), 0)
    lanes = lax.broadcasted_iota(jnp.int32, (8, CY), 1)
    select = (((rows == 0) & (lanes == CY - 1)) | ((rows == 1) & (lanes == 0))).astype(jnp.float32)
    for f in range(3):
        picked = lax.dot_general(select, out_ref[f], (((1,), (1,)), ((), ())), precision=lax.Precision.HIGH,
                                 preferred_element_type=jnp.float32)
        edges_ref[f] = jnp.zeros(edges_ref.shape[1:], jnp.float32)
        edges_ref[f, :, pl.ds(0, ROWS)] = picked


def fill_sides(low_rows_ref, high_rows_ref, left_pad, right_pad):
    for f in range(3):
        left_pad[f, pl.ds(EDGE, ROWS), :] = jnp.transpose(low_rows_ref[f])[:ROWS, 0:1]
        right_pad[f, pl.ds(EDGE, ROWS), :] = jnp.transpose(high_rows_ref[f])[:ROWS, 1:2]


def spread(cb):
    coarse = lax.broadcasted_iota(jnp.int32, (CY, CY), 0)
    fine = lax.broadcasted_iota(jnp.int32, (CY, CY), 1) + cb * CY
    return ((fine >= coarse * REFINE) & (fine < coarse * REFINE + REFINE)).astype(jnp.float32)


def elastic_kernel(cur_ref, prev_ref, coef_ref, low_ref, high_ref, low_rows_ref, high_rows_ref, rows_ref, arrived_ref,
                   pick_ref, out_ref, tiles_ref, edges_ref, scratch, left_pad, right_pad):
    fill_scratch(scratch, cur_ref, low_ref, high_ref, 3)
    fill_sides(low_rows_ref, high_rows_ref, left_pad, right_pad)
    force = landing_sum(rows_ref, arrived_ref, CX)
    lanes = lane_index(CHUNK)
    first_lane = lanes == 0
    last_lane = lanes == CY - 1
    own_axis = (0, 2, 1)
    for r0 in range(0, ROWS, CHUNK):
        top_layer = row_mask(r0, CHUNK, NL, 0)
        bottom_layer = row_mask(r0, CHUNK, NL, NL - 1)
        shear = coef_ref[0, pl.ds(r0, CHUNK), :]
        lame = coef_ref[1, pl.ds(r0, CHUNK), :]
        stiffness = lame + 2.0 * shear
        for c in range(3):
            at = BASE + r0
            v = scratch[c, pl.ds(at, CHUNK), :]
            along_first = scratch[c, pl.ds(at + NL, CHUNK), :] - 2.0 * v + scratch[c, pl.ds(at - NL, CHUNK), :]
            deeper = jnp.where(bottom_layer, 0.0, scratch[c, pl.ds(at + 1, CHUNK), :])
            shallower = jnp.where(top_layer, 0.0, scratch[c, pl.ds(at - 1, CHUNK), :])
            along_depth = deeper - 2.0 * v + shallower
            after = jnp.where(last_lane, right_pad[c, pl.ds(EDGE + r0, CHUNK), :], pltpu.roll(v, CY - 1, 1))
            before = jnp.where(first_lane, left_pad[c, pl.ds(EDGE + r0, CHUNK), :], pltpu.roll(v, 1, 1))
            along_second = after - 2.0 * v + before
            factors = [stiffness if own_axis[c] == axis_index else shear for axis_index in range(3)]
            acceleration = factors[0] * along_first + factors[1] * along_depth + factors[2] * along_second
            out_ref[c, pl.ds(r0, CHUNK), :] = 2.0 * v - prev_ref[c, pl.ds(r0, CHUNK), :] + acceleration
    for x in range(CX):
        out_ref[2, pl.ds(x * NL, 1), :] = out_ref[2, pl.ds(x * NL, 1), :] + force[x : x + 1]
    elastic_tiles(out_ref, pick_ref, tiles_ref)
    edge_rows(out_ref, edges_ref)


def shallow_kernel(cur_ref, prev_ref, coef_ref, wet_ref, low_ref, high_ref, low_rows_ref, high_rows_ref, rows_ref,
                   arrived_ref, pick_ref, out_ref, tiles_ref, edges_ref, scratch, source_ref, left_pad, right_pad):
    fill_scratch(scratch, cur_ref, low_ref, high_ref, 3)
    fill_sides(low_rows_ref, high_rows_ref, left_pad, right_pad)
    coarse_source = landing_sum(rows_ref, arrived_ref, REFINE * CX)
    for cb in range(REFINE):
        source_ref[pl.ds(cb, REFINE * CX, stride=REFINE), :] = select_dot(coarse_source, spread(cb))
    lanes = lane_index(CHUNK)
    first_lane = lanes == 0
    last_lane = lanes == CY - 1
    first_block = row_mask(0, CHUNK, REFINE, 0)
    last_block = row_mask(0, CHUNK, REFINE, REFINE - 1)
    for r0 in range(0, ROWS, CHUNK):
        at = BASE + r0

        def rows_diff(f):
            return scratch[f, pl.ds(at + REFINE, CHUNK), :] - scratch[f, pl.ds(at - REFINE, CHUNK), :]

        def columns_diff(f):
            v = scratch[f, pl.ds(at, CHUNK), :]
            wrap_after = jnp.where(last_block, right_pad[f, pl.ds(EDGE + r0 - (REFINE - 1), CHUNK), :],
                                   pltpu.roll(scratch[f, pl.ds(at + 1, CHUNK), :], CY - 1, 1))
            wrap_before = jnp.where(first_block, left_pad[f, pl.ds(EDGE + r0 + REFINE - 1, CHUNK), :],
                                    pltpu.roll(scratch[f, pl.ds(at - 1, CHUNK), :], 1, 1))
            after = jnp.where(last_lane, wrap_after, pltpu.roll(v, CY - 1, 1))
            before = jnp.where(first_lane, wrap_before, pltpu.roll(v, 1, 1))
            return after - before

        wave = coef_ref[0, pl.ds(r0, CHUNK), :]
        area = coef_ref[1, pl.ds(r0, CHUNK), :]
        wet = wet_ref[pl.ds(r0, CHUNK), :].astype(jnp.float32)
        eta_r = rows_diff(0)
        eta_c = columns_diff(0)
        out_ref[1, pl.ds(r0, CHUNK), :] = wet * (prev_ref[1, pl.ds(r0, CHUNK), :] - wave * eta_r)
        out_ref[2, pl.ds(r0, CHUNK), :] = wet * (prev_ref[2, pl.ds(r0, CHUNK), :] - wave * eta_c)
        divergence = rows_diff(1) + columns_diff(2)
        out_ref[0, pl.ds(r0, CHUNK), :] = wet * (
            prev_ref[0, pl.ds(r0, CHUNK), :] - area * divergence + source_ref[pl.ds(r0, CHUNK), :]
        )
    shallow_tiles(out_ref, pick_ref, tiles_ref)
    edge_rows(out_ref, edges_ref)


def shallow_tiles(field_ref, pick_ref, tiles_ref):
    total = jnp.zeros((REFINE * CX, CY), jnp.float32)
    for cb in range(REFINE):
        total = total + select_dot(field_ref[0, pl.ds(cb, REFINE * CX, stride=REFINE), :], spread(cb).T)
    tiles_ref[...] = select_dot(pick_ref[...], total / REFINE)


def elastic_tiles(field_ref, pick_ref, tiles_ref):
    uplift = field_ref[2, pl.ds(0, CX, stride=NL), :]
    tiles_ref[...] = select_dot(pick_ref[:, :CX], uplift)


def prepare_kernel(tiles_of, cur_ref, pick_ref, tiles_ref, edges_ref):
    tiles_of(cur_ref, pick_ref, tiles_ref)
    edge_rows(cur_ref, edges_ref)


def prepare(tiles_of, current, pick):
    return pl.pallas_call(
        functools.partial(prepare_kernel, tiles_of),
        out_shape=(
            jax.ShapeDtypeStruct((pick.shape[0], CY), jnp.float32),
            jax.ShapeDtypeStruct((3, 8, EDGE_LANES), jnp.float32),
        ),
        in_specs=vmem_specs(2),
        out_specs=tuple(vmem_specs(2)),
    )(current, pick)


def vmem_specs(count):
    return [pl.BlockSpec(memory_space=pltpu.VMEM)] * count


def run_step(kernel, scratch_shapes, *operands):
    slots = operands[-1].shape[0]
    return pl.pallas_call(
        kernel,
        out_shape=(
            jax.ShapeDtypeStruct((3, ROWS, CY), jnp.float32),
            jax.ShapeDtypeStruct((slots, CY), jnp.float32),
            jax.ShapeDtypeStruct((3, 8, EDGE_LANES), jnp.float32),
        ),
        in_specs=vmem_specs(len(operands)),
        out_specs=tuple(vmem_specs(3)),
        scratch_shapes=scratch_shapes,
    )(*operands)


def exchange_kernel(sizes, cur_ref, edges_ref, out_ref, in_ref, low_ref, high_ref, low_rows_ref, high_rows_ref,
                    land, halo, sides, send_sem, recv_sem, halo_send, halo_recv, side_send, side_recv):
    owners, rows_of, columns = sizes
    other = 1 - lax.axis_index("sec")
    section = lax.axis_index("sec")
    gx = lax.axis_index("gx")
    gy = lax.axis_index("gy")
    me = gx * columns + gy
    has_low = gx > 0
    has_high = gx < rows_of - 1
    has_left = gy > 0
    has_right = gy < columns - 1
    halo[...] = jnp.zeros_like(halo)
    sides[...] = jnp.zeros_like(sides)
    barrier = pltpu.get_barrier_semaphore()
    def greet(d, carry):
        pl.semaphore_signal(barrier, inc=1, device_id=(other, d // columns, d % columns),
                            device_id_type=pl.DeviceIdType.MESH)
        return carry

    lax.fori_loop(0, owners, greet, 0, unroll=True)

    @pl.when(has_low)
    def _():
        pl.semaphore_signal(barrier, inc=1, device_id=(section, gx - 1, gy), device_id_type=pl.DeviceIdType.MESH)

    @pl.when(has_high)
    def _():
        pl.semaphore_signal(barrier, inc=1, device_id=(section, gx + 1, gy), device_id_type=pl.DeviceIdType.MESH)

    @pl.when(has_left)
    def _():
        pl.semaphore_signal(barrier, inc=1, device_id=(section, gx, gy - 1), device_id_type=pl.DeviceIdType.MESH)

    @pl.when(has_right)
    def _():
        pl.semaphore_signal(barrier, inc=1, device_id=(section, gx, gy + 1), device_id_type=pl.DeviceIdType.MESH)

    neighbours = [has_low, has_high, has_left, has_right]
    pl.semaphore_wait(barrier, owners + sum(n.astype(jnp.int32) for n in neighbours))

    def side_copy(slot, target):
        return pltpu.make_async_remote_copy(
            src_ref=edges_ref,
            dst_ref=sides.at[slot],
            send_sem=side_send.at[slot],
            recv_sem=side_recv.at[slot],
            device_id=(section, gx, target),
            device_id_type=pl.DeviceIdType.MESH,
        )

    @pl.when(has_right)
    def _():
        side_copy(0, gy + 1).start()

    @pl.when(has_left)
    def _():
        side_copy(1, gy - 1).start()

    def slab_copy(start, slot, target):
        return pltpu.make_async_remote_copy(
            src_ref=cur_ref.at[:, pl.ds(start, HALO_ROWS), :],
            dst_ref=halo.at[slot],
            send_sem=halo_send.at[slot],
            recv_sem=halo_recv.at[slot],
            device_id=(section, target, gy),
            device_id_type=pl.DeviceIdType.MESH,
        )

    @pl.when(has_high)
    def _():
        slab_copy(ROWS - HALO_ROWS, 0, gx + 1).start()

    @pl.when(has_low)
    def _():
        slab_copy(0, 1, gx - 1).start()

    def send(d, carry):
        pltpu.make_async_remote_copy(
            src_ref=out_ref.at[pl.ds(d * CAP, CAP)],
            dst_ref=land.at[pl.ds(me * CAP, CAP)],
            send_sem=send_sem,
            recv_sem=recv_sem,
            device_id=(other, d // columns, d % columns),
            device_id_type=pl.DeviceIdType.MESH,
        ).start()
        return carry

    lax.fori_loop(0, owners, send, 0, unroll=True)
    whole = pltpu.make_async_remote_copy(
        src_ref=out_ref,
        dst_ref=land,
        send_sem=send_sem,
        recv_sem=recv_sem,
        device_id=(other, gx, gy),
        device_id_type=pl.DeviceIdType.MESH,
    )

    @pl.when(has_high)
    def _():
        slab_copy(ROWS - HALO_ROWS, 0, gx + 1).wait_send()
        slab_copy(0, 1, gx + 1).wait_recv()

    @pl.when(has_low)
    def _():
        slab_copy(0, 1, gx - 1).wait_send()
        slab_copy(ROWS - HALO_ROWS, 0, gx - 1).wait_recv()

    @pl.when(has_right)
    def _():
        side_copy(0, gy + 1).wait_send()
        side_copy(1, gy + 1).wait_recv()

    @pl.when(has_left)
    def _():
        side_copy(1, gy - 1).wait_send()
        side_copy(0, gy - 1).wait_recv()

    whole.wait_send()
    whole.wait_recv()
    in_ref[...] = land[...]
    low_ref[...] = halo[0]
    high_ref[...] = halo[1]
    low_rows_ref[...] = sides[0]
    high_rows_ref[...] = sides[1]


def exchange(current, edges, outgoing, owners, rows_of, columns):
    halo_shape = jax.ShapeDtypeStruct((3, HALO_ROWS, CY), jnp.float32)
    side_shape = jax.ShapeDtypeStruct(edges.shape, jnp.float32)
    return pl.pallas_call(
        functools.partial(exchange_kernel, (owners, rows_of, columns)),
        out_shape=(jax.ShapeDtypeStruct(outgoing.shape, jnp.float32), halo_shape, halo_shape, side_shape, side_shape),
        in_specs=[pl.BlockSpec(memory_space=pl.ANY)] * 2 + [pl.BlockSpec(memory_space=pltpu.VMEM)],
        out_specs=tuple(vmem_specs(5)),
        scratch_shapes=[
            pltpu.VMEM(outgoing.shape, jnp.float32),
            pltpu.VMEM((2, 3, HALO_ROWS, CY), jnp.float32),
            pltpu.VMEM((2,) + edges.shape, jnp.float32),
            pltpu.SemaphoreType.DMA(()),
            pltpu.SemaphoreType.DMA(()),
            pltpu.SemaphoreType.DMA((2,)),
            pltpu.SemaphoreType.DMA((2,)),
            pltpu.SemaphoreType.DMA((2,)),
            pltpu.SemaphoreType.DMA((2,)),
        ],
        compiler_params=pltpu.CompilerParams(collective_id=outgoing.shape[1] // CY - 1, has_side_effects=True),
    )(current, edges, outgoing)


def route(payload):
    tile_data, tile_rows = payload
    width = tile_data.shape[-1]
    received_data, received_rows = (
        lax.all_to_all(tile_data, ("gx", "gy"), split_axis=0, concat_axis=0, tiled=True),
        lax.all_to_all(tile_rows, ("gx", "gy"), split_axis=0, concat_axis=0, tiled=True),
    )
    return (received_data.reshape(-1, width), received_rows.reshape(-1))


def deliver(outgoing, send_rows):
    routed = route((outgoing, send_rows))
    return from_partner((routed[0], routed[1]), "sec", 0)


def on_device(state, previous, coeff, wet_mask, link_dest, link_rows, link_weight):
    section = lax.axis_index("sec")
    owners = lax.axis_size("gx") * lax.axis_size("gy")
    fine_rows = REFINE * CX
    current = state[0, :, 0, 0].reshape(3, ROWS, CY)
    earlier = previous[0, :, 0, 0].reshape(3, ROWS, CY)
    factors = coeff[0, :, 0, 0].reshape(2, ROWS, CY)
    wet = wet_mask[0, 0].reshape(ROWS, CY)
    targets = link_dest.reshape(-1)
    pairs = link_rows.reshape(-1, 2)
    source_rows = pairs[:, 0]
    landing = pairs[:, 1]
    weights = link_weight.reshape(-1)
    one_hot = (targets[:, None] == jnp.arange(owners, dtype=jnp.int32)[None, :]).astype(jnp.int32)
    before = jnp.cumsum(one_hot, axis=0) - one_hot
    slot_index = jnp.sum(before * one_hot, axis=1)
    position = targets * CAP + slot_index
    send_rows = jnp.zeros((owners * CAP,), jnp.int32).at[position].set(landing).reshape(owners, CAP)
    slot_rows = jnp.full((owners * CAP,), -1, jnp.int32).at[position].set(source_rows)
    slot_weights = jnp.zeros((owners * CAP,), jnp.float32).at[position].set(weights)
    pick = jnp.where(slot_rows[:, None] == jnp.arange(fine_rows, dtype=jnp.int32)[None, :], slot_weights[:, None], 0.0)
    outgoing, edges = lax.cond(
        section == 0,
        lambda: prepare(elastic_tiles, current, pick),
        lambda: prepare(shallow_tiles, current, pick),
    )
    row_lanes = jnp.broadcast_to(send_rows.reshape(-1, 1).astype(jnp.float32), (owners * CAP, CY))
    outgoing = jnp.concatenate([outgoing, row_lanes], axis=1)
    for step_index in range(STEPS):
        arrived, low_x, high_x, low_y, high_y = exchange(
            current, edges, outgoing, owners, lax.axis_size("gx"), lax.axis_size("gy")
        )
        if step_index == 0:
            arrived_rows = arrived[:, CY].astype(jnp.int32).reshape(1, -1)
            arrived = arrived[:, :CY]

        def elastic_branch():
            scratch = [
                pltpu.VMEM((3, PAD_ROWS, CY), jnp.float32),
                pltpu.VMEM((3, ROWS + 2 * EDGE, 1), jnp.float32),
                pltpu.VMEM((3, ROWS + 2 * EDGE, 1), jnp.float32),
            ]
            return run_step(elastic_kernel, scratch, current, earlier, factors, low_x, high_x, low_y, high_y,
                            arrived_rows, arrived, pick)

        def shallow_branch():
            scratch = [
                pltpu.VMEM((3, PAD_ROWS, CY), jnp.float32),
                pltpu.VMEM((ROWS, CY), jnp.float32),
                pltpu.VMEM((3, ROWS + 2 * EDGE, 1), jnp.float32),
                pltpu.VMEM((3, ROWS + 2 * EDGE, 1), jnp.float32),
            ]
            return run_step(shallow_kernel, scratch, current, earlier, factors, wet, low_x, high_x, low_y, high_y,
                            arrived_rows, arrived, pick)

        updated, outgoing, edges = lax.cond(section == 0, elastic_branch, shallow_branch)
        earlier, current = (current, updated)
    return current.reshape(1, 3, 1, 1, -1)


def solution(mesh):
    placed = (
        P("sec", None, "gx", "gy", None),
        P("sec", None, "gx", "gy", None),
        P("sec", None, "gx", "gy", None),
        P("gx", "gy", None),
        P("sec", "gx", "gy", None, None),
        P("sec", "gx", "gy", None, None),
        P("sec", "gx", "gy", None),
    )
    return jax.shard_map(
        on_device,
        mesh=mesh,
        in_specs=placed,
        out_specs=P("sec", None, "gx", "gy", None),
        check_vma=False,
    )
```

```python
import functools

import jax
import jax.numpy as jnp
from jax import lax
from jax.experimental import pallas as pl
from jax.experimental.pallas import tpu as pltpu
from jax.sharding import PartitionSpec as P

CX = 8
CY = 128
REFINE = 10
NL = 100
STEPS = 4
CAP = 4

ROWS = CX * NL
BASE = 104
PAD_ROWS = BASE + ROWS + BASE
CHUNK = 40
EDGE = 16
HALO_ROWS = NL + 4
EDGE_LANES = 896


def from_partner(value, axis, stride):
    return lax.ppermute(value, axis, [(i, i ^ 1 << stride) for i in range(lax.axis_size(axis))])


def shift_pairs(axis):
    count = lax.axis_size(axis)
    forward = [(i, i + 1) for i in range(count - 1)]
    backward = [(target, source) for source, target in forward]
    return forward, backward


def fill_scratch(scratch, cur_ref, low_ref, high_ref, fields):
    for f in range(fields):
        scratch[f, pl.ds(BASE - HALO_ROWS, HALO_ROWS), :] = low_ref[f]
        scratch[f, pl.ds(BASE, ROWS), :] = cur_ref[f]
        scratch[f, pl.ds(BASE + ROWS, HALO_ROWS), :] = high_ref[f]


def lane_index(rows):
    return lax.broadcasted_iota(jnp.int32, (rows, CY), 1)


def row_mask(r0, rows, period, phase):
    local = lax.broadcasted_iota(jnp.int32, (rows, CY), 0)
    mask = jnp.zeros((rows, CY), jnp.bool_)
    for r in range(rows):
        if (r0 + r) % period == phase:
            mask = mask | (local == r)
    return mask


def exact_dot(a, b):
    return jnp.dot(a, b, precision=lax.Precision.HIGHEST, preferred_element_type=jnp.float32)


def select_dot(a, b):
    return jnp.dot(a, b, precision=lax.Precision.HIGH, preferred_element_type=jnp.float32)


def landing_sum(rows_ref, arrived_ref, count):
    slots = rows_ref.shape[1]
    one_hot = (lax.broadcasted_iota(jnp.int32, (count, slots), 0) == rows_ref[...]).astype(jnp.float32)
    return exact_dot(one_hot, arrived_ref[...])


def edge_rows(out_ref, edges_ref):
    rows = lax.broadcasted_iota(jnp.int32, (8, CY), 0)
    lanes = lax.broadcasted_iota(jnp.int32, (8, CY), 1)
    select = (((rows == 0) & (lanes == CY - 1)) | ((rows == 1) & (lanes == 0))).astype(jnp.float32)
    for f in range(3):
        picked = lax.dot_general(select, out_ref[f], (((1,), (1,)), ((), ())), precision=lax.Precision.HIGH,
                                 preferred_element_type=jnp.float32)
        edges_ref[f] = jnp.zeros(edges_ref.shape[1:], jnp.float32)
        edges_ref[f, :, pl.ds(0, ROWS)] = picked


def fill_sides(low_rows_ref, high_rows_ref, left_pad, right_pad, fields=(0, 1, 2)):
    for f in fields:
        left_pad[f, pl.ds(EDGE, ROWS), :] = jnp.transpose(low_rows_ref[f])[:ROWS, 0:1]
        right_pad[f, pl.ds(EDGE, ROWS), :] = jnp.transpose(high_rows_ref[f])[:ROWS, 1:2]


def spread(cb):
    coarse = lax.broadcasted_iota(jnp.int32, (CY, CY), 0)
    fine = lax.broadcasted_iota(jnp.int32, (CY, CY), 1) + cb * CY
    return ((fine >= coarse * REFINE) & (fine < coarse * REFINE + REFINE)).astype(jnp.float32)


def elastic_kernel(cur_ref, prev_ref, coef_ref, low_ref, high_ref, low_rows_ref, high_rows_ref, rows_ref, arrived_ref,
                   pick_ref, out_ref, tiles_ref, edges_ref, scratch, left_pad, right_pad):
    fill_scratch(scratch, cur_ref, low_ref, high_ref, 3)
    fill_sides(low_rows_ref, high_rows_ref, left_pad, right_pad)
    force = landing_sum(rows_ref, arrived_ref, CX)
    lanes = lane_index(CHUNK)
    first_lane = lanes == 0
    last_lane = lanes == CY - 1
    own_axis = (0, 2, 1)
    for r0 in range(0, ROWS, CHUNK):
        top_layer = row_mask(r0, CHUNK, NL, 0)
        bottom_layer = row_mask(r0, CHUNK, NL, NL - 1)
        shear = coef_ref[0, pl.ds(r0, CHUNK), :]
        lame = coef_ref[1, pl.ds(r0, CHUNK), :]
        stiffness = lame + 2.0 * shear
        for c in range(3):
            at = BASE + r0
            v = scratch[c, pl.ds(at, CHUNK), :]
            along_first = scratch[c, pl.ds(at + NL, CHUNK), :] - 2.0 * v + scratch[c, pl.ds(at - NL, CHUNK), :]
            deeper = jnp.where(bottom_layer, 0.0, scratch[c, pl.ds(at + 1, CHUNK), :])
            shallower = jnp.where(top_layer, 0.0, scratch[c, pl.ds(at - 1, CHUNK), :])
            along_depth = deeper - 2.0 * v + shallower
            after = jnp.where(last_lane, right_pad[c, pl.ds(EDGE + r0, CHUNK), :], pltpu.roll(v, CY - 1, 1))
            before = jnp.where(first_lane, left_pad[c, pl.ds(EDGE + r0, CHUNK), :], pltpu.roll(v, 1, 1))
            along_second = after - 2.0 * v + before
            factors = [stiffness if own_axis[c] == axis_index else shear for axis_index in range(3)]
            acceleration = factors[0] * along_first + factors[1] * along_depth + factors[2] * along_second
            out_ref[c, pl.ds(r0, CHUNK), :] = 2.0 * v - prev_ref[c, pl.ds(r0, CHUNK), :] + acceleration
    for x in range(CX):
        out_ref[2, pl.ds(x * NL, 1), :] = out_ref[2, pl.ds(x * NL, 1), :] + force[x : x + 1]
    elastic_tiles(out_ref, pick_ref, tiles_ref)
    edge_rows(out_ref, edges_ref)


def shallow_kernel(cur_ref, prev_ref, coef_ref, wet_ref, low_ref, high_ref, low_rows_ref, high_rows_ref, rows_ref,
                   arrived_ref, pick_ref, out_ref, tiles_ref, edges_ref, scratch, source_ref, left_pad, right_pad):
    fill_scratch(scratch, cur_ref, low_ref, high_ref, 3)
    fill_sides(low_rows_ref, high_rows_ref, left_pad, right_pad, (0, 2))
    coarse_source = landing_sum(rows_ref, arrived_ref, REFINE * CX)
    for cb in range(REFINE):
        source_ref[pl.ds(cb, REFINE * CX, stride=REFINE), :] = select_dot(coarse_source, spread(cb))
    lanes = lane_index(CHUNK)
    first_lane = lanes == 0
    last_lane = lanes == CY - 1
    first_block = row_mask(0, CHUNK, REFINE, 0)
    last_block = row_mask(0, CHUNK, REFINE, REFINE - 1)
    for r0 in range(0, ROWS, CHUNK):
        at = BASE + r0

        def rows_diff(f):
            return scratch[f, pl.ds(at + REFINE, CHUNK), :] - scratch[f, pl.ds(at - REFINE, CHUNK), :]

        def columns_diff(f):
            v = scratch[f, pl.ds(at, CHUNK), :]
            wrap_after = jnp.where(last_block, right_pad[f, pl.ds(EDGE + r0 - (REFINE - 1), CHUNK), :],
                                   pltpu.roll(scratch[f, pl.ds(at + 1, CHUNK), :], CY - 1, 1))
            wrap_before = jnp.where(first_block, left_pad[f, pl.ds(EDGE + r0 + REFINE - 1, CHUNK), :],
                                    pltpu.roll(scratch[f, pl.ds(at - 1, CHUNK), :], 1, 1))
            after = jnp.where(last_lane, wrap_after, pltpu.roll(v, CY - 1, 1))
            before = jnp.where(first_lane, wrap_before, pltpu.roll(v, 1, 1))
            return after - before

        wave = coef_ref[0, pl.ds(r0, CHUNK), :]
        area = coef_ref[1, pl.ds(r0, CHUNK), :]
        wet = wet_ref[pl.ds(r0, CHUNK), :].astype(jnp.float32)
        eta_r = rows_diff(0)
        eta_c = columns_diff(0)
        out_ref[1, pl.ds(r0, CHUNK), :] = wet * (prev_ref[1, pl.ds(r0, CHUNK), :] - wave * eta_r)
        out_ref[2, pl.ds(r0, CHUNK), :] = wet * (prev_ref[2, pl.ds(r0, CHUNK), :] - wave * eta_c)
        divergence = rows_diff(1) + columns_diff(2)
        out_ref[0, pl.ds(r0, CHUNK), :] = wet * (
            prev_ref[0, pl.ds(r0, CHUNK), :] - area * divergence + source_ref[pl.ds(r0, CHUNK), :]
        )
    shallow_tiles(out_ref, pick_ref, tiles_ref)
    edge_rows(out_ref, edges_ref)


def shallow_tiles(field_ref, pick_ref, tiles_ref):
    total = jnp.zeros((REFINE * CX, CY), jnp.float32)
    for cb in range(REFINE):
        total = total + select_dot(field_ref[0, pl.ds(cb, REFINE * CX, stride=REFINE), :], spread(cb).T)
    tiles_ref[...] = exact_dot(pick_ref[...], total / REFINE)


def elastic_tiles(field_ref, pick_ref, tiles_ref):
    uplift = field_ref[2, pl.ds(0, CX, stride=NL), :]
    tiles_ref[...] = exact_dot(pick_ref[:, :CX], uplift)


def prepare_kernel(tiles_of, cur_ref, pick_ref, tiles_ref, edges_ref):
    tiles_of(cur_ref, pick_ref, tiles_ref)
    edge_rows(cur_ref, edges_ref)


def prepare(tiles_of, current, pick):
    return pl.pallas_call(
        functools.partial(prepare_kernel, tiles_of),
        out_shape=(
            jax.ShapeDtypeStruct((pick.shape[0], CY), jnp.float32),
            jax.ShapeDtypeStruct((3, 8, EDGE_LANES), jnp.float32),
        ),
        in_specs=vmem_specs(2),
        out_specs=tuple(vmem_specs(2)),
    )(current, pick)


def vmem_specs(count):
    return [pl.BlockSpec(memory_space=pltpu.VMEM)] * count


def run_step(kernel, scratch_shapes, *operands):
    slots = operands[-1].shape[0]
    return pl.pallas_call(
        kernel,
        out_shape=(
            jax.ShapeDtypeStruct((3, ROWS, CY), jnp.float32),
            jax.ShapeDtypeStruct((slots, CY), jnp.float32),
            jax.ShapeDtypeStruct((3, 8, EDGE_LANES), jnp.float32),
        ),
        in_specs=vmem_specs(len(operands)),
        out_specs=tuple(vmem_specs(3)),
        scratch_shapes=scratch_shapes,
    )(*operands)


def exchange_kernel(sizes, cur_ref, edges_ref, out_ref, in_ref, low_ref, high_ref, low_rows_ref, high_rows_ref,
                    land, halo, sides, send_sem, recv_sem, halo_send, halo_recv, side_send, side_recv):
    owners, rows_of, columns = sizes
    other = 1 - lax.axis_index("sec")
    section = lax.axis_index("sec")
    gx = lax.axis_index("gx")
    gy = lax.axis_index("gy")
    me = gx * columns + gy
    has_low = gx > 0
    has_high = gx < rows_of - 1
    has_left = gy > 0
    has_right = gy < columns - 1
    halo[...] = jnp.zeros_like(halo)
    sides[...] = jnp.zeros_like(sides)
    barrier = pltpu.get_barrier_semaphore()
    def greet(d, carry):
        pl.semaphore_signal(barrier, inc=1, device_id=(other, d // columns, d % columns),
                            device_id_type=pl.DeviceIdType.MESH)
        return carry

    lax.fori_loop(0, owners, greet, 0, unroll=True)

    @pl.when(has_low)
    def _():
        pl.semaphore_signal(barrier, inc=1, device_id=(section, gx - 1, gy), device_id_type=pl.DeviceIdType.MESH)

    @pl.when(has_high)
    def _():
        pl.semaphore_signal(barrier, inc=1, device_id=(section, gx + 1, gy), device_id_type=pl.DeviceIdType.MESH)

    @pl.when(has_left)
    def _():
        pl.semaphore_signal(barrier, inc=1, device_id=(section, gx, gy - 1), device_id_type=pl.DeviceIdType.MESH)

    @pl.when(has_right)
    def _():
        pl.semaphore_signal(barrier, inc=1, device_id=(section, gx, gy + 1), device_id_type=pl.DeviceIdType.MESH)

    neighbours = [has_low, has_high, has_left, has_right]
    pl.semaphore_wait(barrier, owners + sum(n.astype(jnp.int32) for n in neighbours))

    def side_copy(slot, target):
        return pltpu.make_async_remote_copy(
            src_ref=edges_ref,
            dst_ref=sides.at[slot],
            send_sem=side_send.at[slot],
            recv_sem=side_recv.at[slot],
            device_id=(section, gx, target),
            device_id_type=pl.DeviceIdType.MESH,
        )

    @pl.when(has_right)
    def _():
        side_copy(0, gy + 1).start()

    @pl.when(has_left)
    def _():
        side_copy(1, gy - 1).start()

    def slab_copy(start, slot, target):
        return pltpu.make_async_remote_copy(
            src_ref=cur_ref.at[:, pl.ds(start, HALO_ROWS), :],
            dst_ref=halo.at[slot],
            send_sem=halo_send.at[slot],
            recv_sem=halo_recv.at[slot],
            device_id=(section, target, gy),
            device_id_type=pl.DeviceIdType.MESH,
        )

    @pl.when(has_high)
    def _():
        slab_copy(ROWS - HALO_ROWS, 0, gx + 1).start()

    @pl.when(has_low)
    def _():
        slab_copy(0, 1, gx - 1).start()

    def send(d, carry):
        pltpu.make_async_remote_copy(
            src_ref=out_ref.at[pl.ds(d * CAP, CAP)],
            dst_ref=land.at[pl.ds(me * CAP, CAP)],
            send_sem=send_sem,
            recv_sem=recv_sem,
            device_id=(other, d // columns, d % columns),
            device_id_type=pl.DeviceIdType.MESH,
        ).start()
        return carry

    lax.fori_loop(0, owners, send, 0, unroll=True)
    whole = pltpu.make_async_remote_copy(
        src_ref=out_ref,
        dst_ref=land,
        send_sem=send_sem,
        recv_sem=recv_sem,
        device_id=(other, gx, gy),
        device_id_type=pl.DeviceIdType.MESH,
    )

    @pl.when(has_high)
    def _():
        slab_copy(ROWS - HALO_ROWS, 0, gx + 1).wait_send()
        slab_copy(0, 1, gx + 1).wait_recv()

    @pl.when(has_low)
    def _():
        slab_copy(0, 1, gx - 1).wait_send()
        slab_copy(ROWS - HALO_ROWS, 0, gx - 1).wait_recv()

    @pl.when(has_right)
    def _():
        side_copy(0, gy + 1).wait_send()
        side_copy(1, gy + 1).wait_recv()

    @pl.when(has_left)
    def _():
        side_copy(1, gy - 1).wait_send()
        side_copy(0, gy - 1).wait_recv()

    whole.wait_send()
    whole.wait_recv()
    in_ref[...] = land[...]
    low_ref[...] = halo[0]
    high_ref[...] = halo[1]
    low_rows_ref[...] = sides[0]
    high_rows_ref[...] = sides[1]


def exchange(current, edges, outgoing, owners, rows_of, columns):
    halo_shape = jax.ShapeDtypeStruct((3, HALO_ROWS, CY), jnp.float32)
    side_shape = jax.ShapeDtypeStruct(edges.shape, jnp.float32)
    return pl.pallas_call(
        functools.partial(exchange_kernel, (owners, rows_of, columns)),
        out_shape=(jax.ShapeDtypeStruct(outgoing.shape, jnp.float32), halo_shape, halo_shape, side_shape, side_shape),
        in_specs=[pl.BlockSpec(memory_space=pl.ANY)] * 2 + [pl.BlockSpec(memory_space=pltpu.VMEM)],
        out_specs=tuple(vmem_specs(5)),
        scratch_shapes=[
            pltpu.VMEM(outgoing.shape, jnp.float32),
            pltpu.VMEM((2, 3, HALO_ROWS, CY), jnp.float32),
            pltpu.VMEM((2,) + edges.shape, jnp.float32),
            pltpu.SemaphoreType.DMA(()),
            pltpu.SemaphoreType.DMA(()),
            pltpu.SemaphoreType.DMA((2,)),
            pltpu.SemaphoreType.DMA((2,)),
            pltpu.SemaphoreType.DMA((2,)),
            pltpu.SemaphoreType.DMA((2,)),
        ],
        compiler_params=pltpu.CompilerParams(collective_id=outgoing.shape[1] // CY - 1, has_side_effects=True),
    )(current, edges, outgoing)


def route(payload):
    tile_data, tile_rows = payload
    width = tile_data.shape[-1]
    received_data, received_rows = (
        lax.all_to_all(tile_data, ("gx", "gy"), split_axis=0, concat_axis=0, tiled=True),
        lax.all_to_all(tile_rows, ("gx", "gy"), split_axis=0, concat_axis=0, tiled=True),
    )
    return (received_data.reshape(-1, width), received_rows.reshape(-1))


def deliver(outgoing, send_rows):
    routed = route((outgoing, send_rows))
    return from_partner((routed[0], routed[1]), "sec", 0)


def on_device(state, previous, coeff, wet_mask, link_dest, link_rows, link_weight):
    section = lax.axis_index("sec")
    owners = lax.axis_size("gx") * lax.axis_size("gy")
    fine_rows = REFINE * CX
    current = state[0, :, 0, 0].reshape(3, ROWS, CY)
    earlier = previous[0, :, 0, 0].reshape(3, ROWS, CY)
    factors = coeff[0, :, 0, 0].reshape(2, ROWS, CY)
    wet = wet_mask[0, 0].reshape(ROWS, CY)
    targets = link_dest.reshape(-1)
    pairs = link_rows.reshape(-1, 2)
    source_rows = pairs[:, 0]
    landing = pairs[:, 1]
    weights = link_weight.reshape(-1)
    one_hot = (targets[:, None] == jnp.arange(owners, dtype=jnp.int32)[None, :]).astype(jnp.int32)
    before = jnp.cumsum(one_hot, axis=0) - one_hot
    slot_index = jnp.sum(before * one_hot, axis=1)
    position = targets * CAP + slot_index
    send_rows = jnp.zeros((owners * CAP,), jnp.int32).at[position].set(landing).reshape(owners, CAP)
    slot_rows = jnp.full((owners * CAP,), -1, jnp.int32).at[position].set(source_rows)
    slot_weights = jnp.zeros((owners * CAP,), jnp.float32).at[position].set(weights)
    pick = jnp.where(slot_rows[:, None] == jnp.arange(fine_rows, dtype=jnp.int32)[None, :], slot_weights[:, None], 0.0)
    outgoing, edges = lax.cond(
        section == 0,
        lambda: prepare(elastic_tiles, current, pick),
        lambda: prepare(shallow_tiles, current, pick),
    )
    row_lanes = jnp.broadcast_to(send_rows.reshape(-1, 1).astype(jnp.float32), (owners * CAP, CY))
    outgoing = jnp.concatenate([outgoing, row_lanes], axis=1)
    for step_index in range(STEPS):
        arrived, low_x, high_x, low_y, high_y = exchange(
            current, edges, outgoing, owners, lax.axis_size("gx"), lax.axis_size("gy")
        )
        if step_index == 0:
            arrived_rows = arrived[:, CY].astype(jnp.int32).reshape(1, -1)
            arrived = arrived[:, :CY]

        def elastic_branch():
            scratch = [
                pltpu.VMEM((3, PAD_ROWS, CY), jnp.float32),
                pltpu.VMEM((3, ROWS + 2 * EDGE, 1), jnp.float32),
                pltpu.VMEM((3, ROWS + 2 * EDGE, 1), jnp.float32),
            ]
            return run_step(elastic_kernel, scratch, current, earlier, factors, low_x, high_x, low_y, high_y,
                            arrived_rows, arrived, pick)

        def shallow_branch():
            scratch = [
                pltpu.VMEM((3, PAD_ROWS, CY), jnp.float32),
                pltpu.VMEM((ROWS, CY), jnp.float32),
                pltpu.VMEM((3, ROWS + 2 * EDGE, 1), jnp.float32),
                pltpu.VMEM((3, ROWS + 2 * EDGE, 1), jnp.float32),
            ]
            return run_step(shallow_kernel, scratch, current, earlier, factors, wet, low_x, high_x, low_y, high_y,
                            arrived_rows, arrived, pick)

        updated, outgoing, edges = lax.cond(section == 0, elastic_branch, shallow_branch)
        earlier, current = (current, updated)
    return current.reshape(1, 3, 1, 1, -1)


def solution(mesh):
    placed = (
        P("sec", None, "gx", "gy", None),
        P("sec", None, "gx", "gy", None),
        P("sec", None, "gx", "gy", None),
        P("gx", "gy", None),
        P("sec", "gx", "gy", None, None),
        P("sec", "gx", "gy", None, None),
        P("sec", "gx", "gy", None),
    )
    return jax.shard_map(
        on_device,
        mesh=mesh,
        in_specs=placed,
        out_specs=P("sec", None, "gx", "gy", None),
        check_vma=False,
    )
```

```python
import functools

import jax
import jax.numpy as jnp
from jax import lax
from jax.experimental import pallas as pl
from jax.experimental.pallas import tpu as pltpu
from jax.sharding import PartitionSpec as P

CX = 8
CY = 128
REFINE = 10
NL = 100
STEPS = 4
CAP = 4

ROWS = CX * NL
BASE = 104
PAD_ROWS = BASE + ROWS + BASE
CHUNK = 40
EDGE = 16
HALO_ROWS = NL + 4
EDGE_LANES = 896


def from_partner(value, axis, stride):
    return lax.ppermute(value, axis, [(i, i ^ 1 << stride) for i in range(lax.axis_size(axis))])


def shift_pairs(axis):
    count = lax.axis_size(axis)
    forward = [(i, i + 1) for i in range(count - 1)]
    backward = [(target, source) for source, target in forward]
    return forward, backward


def fill_scratch(scratch, cur_ref, low_ref, high_ref, fields):
    for f in range(fields):
        scratch[f, pl.ds(BASE - HALO_ROWS, HALO_ROWS), :] = low_ref[f]
        scratch[f, pl.ds(BASE, ROWS), :] = cur_ref[f]
        scratch[f, pl.ds(BASE + ROWS, HALO_ROWS), :] = high_ref[f]


def lane_index(rows):
    return lax.broadcasted_iota(jnp.int32, (rows, CY), 1)


def row_mask(r0, rows, period, phase):
    local = lax.broadcasted_iota(jnp.int32, (rows, CY), 0)
    mask = jnp.zeros((rows, CY), jnp.bool_)
    for r in range(rows):
        if (r0 + r) % period == phase:
            mask = mask | (local == r)
    return mask


def exact_dot(a, b):
    return jnp.dot(a, b, precision=lax.Precision.HIGHEST, preferred_element_type=jnp.float32)


def select_dot(a, b):
    return jnp.dot(a, b, precision=lax.Precision.HIGH, preferred_element_type=jnp.float32)


def landing_sum(rows_ref, arrived_ref, count):
    slots = rows_ref.shape[1]
    one_hot = (lax.broadcasted_iota(jnp.int32, (count, slots), 0) == rows_ref[...]).astype(jnp.float32)
    return exact_dot(one_hot, arrived_ref[...])


def edge_rows(out_ref, edges_ref, fields=(0, 1, 2)):
    rows = lax.broadcasted_iota(jnp.int32, (8, CY), 0)
    lanes = lax.broadcasted_iota(jnp.int32, (8, CY), 1)
    select = (((rows == 0) & (lanes == CY - 1)) | ((rows == 1) & (lanes == 0))).astype(jnp.float32)
    for f in range(3):
        edges_ref[f] = jnp.zeros(edges_ref.shape[1:], jnp.float32)
        if f not in fields:
            continue
        picked = lax.dot_general(select, out_ref[f], (((1,), (1,)), ((), ())), precision=lax.Precision.HIGH,
                                 preferred_element_type=jnp.float32)
        edges_ref[f, :, pl.ds(0, ROWS)] = picked


def fill_sides(low_rows_ref, high_rows_ref, left_pad, right_pad, fields=(0, 1, 2)):
    for f in fields:
        left_pad[f, pl.ds(EDGE, ROWS), :] = jnp.transpose(low_rows_ref[f])[:ROWS, 0:1]
        right_pad[f, pl.ds(EDGE, ROWS), :] = jnp.transpose(high_rows_ref[f])[:ROWS, 1:2]


def spread(cb):
    coarse = lax.broadcasted_iota(jnp.int32, (CY, CY), 0)
    fine = lax.broadcasted_iota(jnp.int32, (CY, CY), 1) + cb * CY
    return ((fine >= coarse * REFINE) & (fine < coarse * REFINE + REFINE)).astype(jnp.float32)


def elastic_kernel(cur_ref, prev_ref, coef_ref, low_ref, high_ref, low_rows_ref, high_rows_ref, rows_ref, arrived_ref,
                   pick_ref, out_ref, tiles_ref, edges_ref, scratch, left_pad, right_pad):
    fill_scratch(scratch, cur_ref, low_ref, high_ref, 3)
    fill_sides(low_rows_ref, high_rows_ref, left_pad, right_pad)
    force = landing_sum(rows_ref, arrived_ref, CX)
    lanes = lane_index(CHUNK)
    first_lane = lanes == 0
    last_lane = lanes == CY - 1
    own_axis = (0, 2, 1)
    for r0 in range(0, ROWS, CHUNK):
        top_layer = row_mask(r0, CHUNK, NL, 0)
        bottom_layer = row_mask(r0, CHUNK, NL, NL - 1)
        shear = coef_ref[0, pl.ds(r0, CHUNK), :]
        lame = coef_ref[1, pl.ds(r0, CHUNK), :]
        stiffness = lame + 2.0 * shear
        for c in range(3):
            at = BASE + r0
            v = scratch[c, pl.ds(at, CHUNK), :]
            along_first = scratch[c, pl.ds(at + NL, CHUNK), :] - 2.0 * v + scratch[c, pl.ds(at - NL, CHUNK), :]
            deeper = jnp.where(bottom_layer, 0.0, scratch[c, pl.ds(at + 1, CHUNK), :])
            shallower = jnp.where(top_layer, 0.0, scratch[c, pl.ds(at - 1, CHUNK), :])
            along_depth = deeper - 2.0 * v + shallower
            after = jnp.where(last_lane, right_pad[c, pl.ds(EDGE + r0, CHUNK), :], pltpu.roll(v, CY - 1, 1))
            before = jnp.where(first_lane, left_pad[c, pl.ds(EDGE + r0, CHUNK), :], pltpu.roll(v, 1, 1))
            along_second = after - 2.0 * v + before
            factors = [stiffness if own_axis[c] == axis_index else shear for axis_index in range(3)]
            acceleration = factors[0] * along_first + factors[1] * along_depth + factors[2] * along_second
            out_ref[c, pl.ds(r0, CHUNK), :] = 2.0 * v - prev_ref[c, pl.ds(r0, CHUNK), :] + acceleration
    for x in range(CX):
        out_ref[2, pl.ds(x * NL, 1), :] = out_ref[2, pl.ds(x * NL, 1), :] + force[x : x + 1]
    elastic_tiles(out_ref, pick_ref, tiles_ref)
    edge_rows(out_ref, edges_ref)


def shallow_kernel(cur_ref, prev_ref, coef_ref, wet_ref, low_ref, high_ref, low_rows_ref, high_rows_ref, rows_ref,
                   arrived_ref, pick_ref, out_ref, tiles_ref, edges_ref, scratch, source_ref, left_pad, right_pad):
    fill_scratch(scratch, cur_ref, low_ref, high_ref, 3)
    fill_sides(low_rows_ref, high_rows_ref, left_pad, right_pad, (0, 2))
    coarse_source = landing_sum(rows_ref, arrived_ref, REFINE * CX)
    for cb in range(REFINE):
        source_ref[pl.ds(cb, REFINE * CX, stride=REFINE), :] = select_dot(coarse_source, spread(cb))
    lanes = lane_index(CHUNK)
    first_lane = lanes == 0
    last_lane = lanes == CY - 1
    first_block = row_mask(0, CHUNK, REFINE, 0)
    last_block = row_mask(0, CHUNK, REFINE, REFINE - 1)
    for r0 in range(0, ROWS, CHUNK):
        at = BASE + r0

        def rows_diff(f):
            return scratch[f, pl.ds(at + REFINE, CHUNK), :] - scratch[f, pl.ds(at - REFINE, CHUNK), :]

        def columns_diff(f):
            v = scratch[f, pl.ds(at, CHUNK), :]
            wrap_after = jnp.where(last_block, right_pad[f, pl.ds(EDGE + r0 - (REFINE - 1), CHUNK), :],
                                   pltpu.roll(scratch[f, pl.ds(at + 1, CHUNK), :], CY - 1, 1))
            wrap_before = jnp.where(first_block, left_pad[f, pl.ds(EDGE + r0 + REFINE - 1, CHUNK), :],
                                    pltpu.roll(scratch[f, pl.ds(at - 1, CHUNK), :], 1, 1))
            after = jnp.where(last_lane, wrap_after, pltpu.roll(v, CY - 1, 1))
            before = jnp.where(first_lane, wrap_before, pltpu.roll(v, 1, 1))
            return after - before

        wave = coef_ref[0, pl.ds(r0, CHUNK), :]
        area = coef_ref[1, pl.ds(r0, CHUNK), :]
        wet = wet_ref[pl.ds(r0, CHUNK), :].astype(jnp.float32)
        eta_r = rows_diff(0)
        eta_c = columns_diff(0)
        out_ref[1, pl.ds(r0, CHUNK), :] = wet * (prev_ref[1, pl.ds(r0, CHUNK), :] - wave * eta_r)
        out_ref[2, pl.ds(r0, CHUNK), :] = wet * (prev_ref[2, pl.ds(r0, CHUNK), :] - wave * eta_c)
        divergence = rows_diff(1) + columns_diff(2)
        out_ref[0, pl.ds(r0, CHUNK), :] = wet * (
            prev_ref[0, pl.ds(r0, CHUNK), :] - area * divergence + source_ref[pl.ds(r0, CHUNK), :]
        )
    shallow_tiles(out_ref, pick_ref, tiles_ref)
    edge_rows(out_ref, edges_ref, (0, 2))


def shallow_tiles(field_ref, pick_ref, tiles_ref):
    total = jnp.zeros((REFINE * CX, CY), jnp.float32)
    for cb in range(REFINE):
        total = total + select_dot(field_ref[0, pl.ds(cb, REFINE * CX, stride=REFINE), :], spread(cb).T)
    tiles_ref[...] = exact_dot(pick_ref[...], total / REFINE)


def elastic_tiles(field_ref, pick_ref, tiles_ref):
    uplift = field_ref[2, pl.ds(0, CX, stride=NL), :]
    tiles_ref[...] = exact_dot(pick_ref[:, :CX], uplift)


def prepare_kernel(tiles_of, cur_ref, pick_ref, tiles_ref, edges_ref):
    tiles_of(cur_ref, pick_ref, tiles_ref)
    edge_rows(cur_ref, edges_ref)


def prepare(tiles_of, current, pick):
    return pl.pallas_call(
        functools.partial(prepare_kernel, tiles_of),
        out_shape=(
            jax.ShapeDtypeStruct((pick.shape[0], CY), jnp.float32),
            jax.ShapeDtypeStruct((3, 8, EDGE_LANES), jnp.float32),
        ),
        in_specs=vmem_specs(2),
        out_specs=tuple(vmem_specs(2)),
    )(current, pick)


def vmem_specs(count):
    return [pl.BlockSpec(memory_space=pltpu.VMEM)] * count


def run_step(kernel, scratch_shapes, *operands):
    slots = operands[-1].shape[0]
    return pl.pallas_call(
        kernel,
        out_shape=(
            jax.ShapeDtypeStruct((3, ROWS, CY), jnp.float32),
            jax.ShapeDtypeStruct((slots, CY), jnp.float32),
            jax.ShapeDtypeStruct((3, 8, EDGE_LANES), jnp.float32),
        ),
        in_specs=vmem_specs(len(operands)),
        out_specs=tuple(vmem_specs(3)),
        scratch_shapes=scratch_shapes,
    )(*operands)


def exchange_kernel(sizes, cur_ref, edges_ref, out_ref, in_ref, low_ref, high_ref, low_rows_ref, high_rows_ref,
                    land, halo, sides, send_sem, recv_sem, halo_send, halo_recv, side_send, side_recv):
    owners, rows_of, columns = sizes
    other = 1 - lax.axis_index("sec")
    section = lax.axis_index("sec")
    gx = lax.axis_index("gx")
    gy = lax.axis_index("gy")
    me = gx * columns + gy
    has_low = gx > 0
    has_high = gx < rows_of - 1
    has_left = gy > 0
    has_right = gy < columns - 1
    halo[...] = jnp.zeros_like(halo)
    sides[...] = jnp.zeros_like(sides)
    barrier = pltpu.get_barrier_semaphore()
    def greet(d, carry):
        pl.semaphore_signal(barrier, inc=1, device_id=(other, d // columns, d % columns),
                            device_id_type=pl.DeviceIdType.MESH)
        return carry

    lax.fori_loop(0, owners, greet, 0, unroll=True)

    @pl.when(has_low)
    def _():
        pl.semaphore_signal(barrier, inc=1, device_id=(section, gx - 1, gy), device_id_type=pl.DeviceIdType.MESH)

    @pl.when(has_high)
    def _():
        pl.semaphore_signal(barrier, inc=1, device_id=(section, gx + 1, gy), device_id_type=pl.DeviceIdType.MESH)

    @pl.when(has_left)
    def _():
        pl.semaphore_signal(barrier, inc=1, device_id=(section, gx, gy - 1), device_id_type=pl.DeviceIdType.MESH)

    @pl.when(has_right)
    def _():
        pl.semaphore_signal(barrier, inc=1, device_id=(section, gx, gy + 1), device_id_type=pl.DeviceIdType.MESH)

    neighbours = [has_low, has_high, has_left, has_right]
    pl.semaphore_wait(barrier, owners + sum(n.astype(jnp.int32) for n in neighbours))

    def side_copy(slot, target):
        return pltpu.make_async_remote_copy(
            src_ref=edges_ref,
            dst_ref=sides.at[slot],
            send_sem=side_send.at[slot],
            recv_sem=side_recv.at[slot],
            device_id=(section, gx, target),
            device_id_type=pl.DeviceIdType.MESH,
        )

    @pl.when(has_right)
    def _():
        side_copy(0, gy + 1).start()

    @pl.when(has_left)
    def _():
        side_copy(1, gy - 1).start()

    def slab_copy(start, slot, target):
        return pltpu.make_async_remote_copy(
            src_ref=cur_ref.at[:, pl.ds(start, HALO_ROWS), :],
            dst_ref=halo.at[slot],
            send_sem=halo_send.at[slot],
            recv_sem=halo_recv.at[slot],
            device_id=(section, target, gy),
            device_id_type=pl.DeviceIdType.MESH,
        )

    @pl.when(has_high)
    def _():
        slab_copy(ROWS - HALO_ROWS, 0, gx + 1).start()

    @pl.when(has_low)
    def _():
        slab_copy(0, 1, gx - 1).start()

    def send(d, carry):
        pltpu.make_async_remote_copy(
            src_ref=out_ref.at[pl.ds(d * CAP, CAP)],
            dst_ref=land.at[pl.ds(me * CAP, CAP)],
            send_sem=send_sem,
            recv_sem=recv_sem,
            device_id=(other, d // columns, d % columns),
            device_id_type=pl.DeviceIdType.MESH,
        ).start()
        return carry

    lax.fori_loop(0, owners, send, 0, unroll=True)
    whole = pltpu.make_async_remote_copy(
        src_ref=out_ref,
        dst_ref=land,
        send_sem=send_sem,
        recv_sem=recv_sem,
        device_id=(other, gx, gy),
        device_id_type=pl.DeviceIdType.MESH,
    )

    @pl.when(has_high)
    def _():
        slab_copy(ROWS - HALO_ROWS, 0, gx + 1).wait_send()
        slab_copy(0, 1, gx + 1).wait_recv()

    @pl.when(has_low)
    def _():
        slab_copy(0, 1, gx - 1).wait_send()
        slab_copy(ROWS - HALO_ROWS, 0, gx - 1).wait_recv()

    @pl.when(has_right)
    def _():
        side_copy(0, gy + 1).wait_send()
        side_copy(1, gy + 1).wait_recv()

    @pl.when(has_left)
    def _():
        side_copy(1, gy - 1).wait_send()
        side_copy(0, gy - 1).wait_recv()

    whole.wait_send()
    whole.wait_recv()
    in_ref[...] = land[...]
    low_ref[...] = halo[0]
    high_ref[...] = halo[1]
    low_rows_ref[...] = sides[0]
    high_rows_ref[...] = sides[1]


def exchange(current, edges, outgoing, owners, rows_of, columns):
    halo_shape = jax.ShapeDtypeStruct((3, HALO_ROWS, CY), jnp.float32)
    side_shape = jax.ShapeDtypeStruct(edges.shape, jnp.float32)
    return pl.pallas_call(
        functools.partial(exchange_kernel, (owners, rows_of, columns)),
        out_shape=(jax.ShapeDtypeStruct(outgoing.shape, jnp.float32), halo_shape, halo_shape, side_shape, side_shape),
        in_specs=[pl.BlockSpec(memory_space=pl.ANY)] * 2 + [pl.BlockSpec(memory_space=pltpu.VMEM)],
        out_specs=tuple(vmem_specs(5)),
        scratch_shapes=[
            pltpu.VMEM(outgoing.shape, jnp.float32),
            pltpu.VMEM((2, 3, HALO_ROWS, CY), jnp.float32),
            pltpu.VMEM((2,) + edges.shape, jnp.float32),
            pltpu.SemaphoreType.DMA(()),
            pltpu.SemaphoreType.DMA(()),
            pltpu.SemaphoreType.DMA((2,)),
            pltpu.SemaphoreType.DMA((2,)),
            pltpu.SemaphoreType.DMA((2,)),
            pltpu.SemaphoreType.DMA((2,)),
        ],
        compiler_params=pltpu.CompilerParams(collective_id=outgoing.shape[1] // CY - 1, has_side_effects=True),
    )(current, edges, outgoing)


def route(payload):
    tile_data, tile_rows = payload
    width = tile_data.shape[-1]
    received_data, received_rows = (
        lax.all_to_all(tile_data, ("gx", "gy"), split_axis=0, concat_axis=0, tiled=True),
        lax.all_to_all(tile_rows, ("gx", "gy"), split_axis=0, concat_axis=0, tiled=True),
    )
    return (received_data.reshape(-1, width), received_rows.reshape(-1))


def deliver(outgoing, send_rows):
    routed = route((outgoing, send_rows))
    return from_partner((routed[0], routed[1]), "sec", 0)


def on_device(state, previous, coeff, wet_mask, link_dest, link_rows, link_weight):
    section = lax.axis_index("sec")
    owners = lax.axis_size("gx") * lax.axis_size("gy")
    fine_rows = REFINE * CX
    current = state[0, :, 0, 0].reshape(3, ROWS, CY)
    earlier = previous[0, :, 0, 0].reshape(3, ROWS, CY)
    factors = coeff[0, :, 0, 0].reshape(2, ROWS, CY)
    wet = wet_mask[0, 0].reshape(ROWS, CY)
    targets = link_dest.reshape(-1)
    pairs = link_rows.reshape(-1, 2)
    source_rows = pairs[:, 0]
    landing = pairs[:, 1]
    weights = link_weight.reshape(-1)
    one_hot = (targets[:, None] == jnp.arange(owners, dtype=jnp.int32)[None, :]).astype(jnp.int32)
    before = jnp.cumsum(one_hot, axis=0) - one_hot
    slot_index = jnp.sum(before * one_hot, axis=1)
    position = targets * CAP + slot_index
    send_rows = jnp.zeros((owners * CAP,), jnp.int32).at[position].set(landing).reshape(owners, CAP)
    slot_rows = jnp.full((owners * CAP,), -1, jnp.int32).at[position].set(source_rows)
    slot_weights = jnp.zeros((owners * CAP,), jnp.float32).at[position].set(weights)
    pick = jnp.where(slot_rows[:, None] == jnp.arange(fine_rows, dtype=jnp.int32)[None, :], slot_weights[:, None], 0.0)
    outgoing, edges = lax.cond(
        section == 0,
        lambda: prepare(elastic_tiles, current, pick),
        lambda: prepare(shallow_tiles, current, pick),
    )
    row_lanes = jnp.broadcast_to(send_rows.reshape(-1, 1).astype(jnp.float32), (owners * CAP, CY))
    outgoing = jnp.concatenate([outgoing, row_lanes], axis=1)
    for step_index in range(STEPS):
        arrived, low_x, high_x, low_y, high_y = exchange(
            current, edges, outgoing, owners, lax.axis_size("gx"), lax.axis_size("gy")
        )
        if step_index == 0:
            arrived_rows = arrived[:, CY].astype(jnp.int32).reshape(1, -1)
            arrived = arrived[:, :CY]

        def elastic_branch():
            scratch = [
                pltpu.VMEM((3, PAD_ROWS, CY), jnp.float32),
                pltpu.VMEM((3, ROWS + 2 * EDGE, 1), jnp.float32),
                pltpu.VMEM((3, ROWS + 2 * EDGE, 1), jnp.float32),
            ]
            return run_step(elastic_kernel, scratch, current, earlier, factors, low_x, high_x, low_y, high_y,
                            arrived_rows, arrived, pick)

        def shallow_branch():
            scratch = [
                pltpu.VMEM((3, PAD_ROWS, CY), jnp.float32),
                pltpu.VMEM((ROWS, CY), jnp.float32),
                pltpu.VMEM((3, ROWS + 2 * EDGE, 1), jnp.float32),
                pltpu.VMEM((3, ROWS + 2 * EDGE, 1), jnp.float32),
            ]
            return run_step(shallow_kernel, scratch, current, earlier, factors, wet, low_x, high_x, low_y, high_y,
                            arrived_rows, arrived, pick)

        updated, outgoing, edges = lax.cond(section == 0, elastic_branch, shallow_branch)
        earlier, current = (current, updated)
    return current.reshape(1, 3, 1, 1, -1)


def solution(mesh):
    placed = (
        P("sec", None, "gx", "gy", None),
        P("sec", None, "gx", "gy", None),
        P("sec", None, "gx", "gy", None),
        P("gx", "gy", None),
        P("sec", "gx", "gy", None, None),
        P("sec", "gx", "gy", None, None),
        P("sec", "gx", "gy", None),
    )
    return jax.shard_map(
        on_device,
        mesh=mesh,
        in_specs=placed,
        out_specs=P("sec", None, "gx", "gy", None),
        check_vma=False,
    )
```
